512 devices in a mesh: section: 4 (over x), row: 16 (over z, core), dp: 8 (over y).
Axes of the slice: x: 4, y: 8, z: 8, core: 2. Of those that a mesh axis runs over, the one named last changes fastest.
Arguments:
- inputs: bfloat16 [4, 8, 64, 48, 352], P(None, 'dp', 'row'), may hold values from -8 to 8
- depth_kernel: bfloat16 [4, 7, 7, 352], P('section'), may hold values from -0.875 to 0.875
- depth_bias: bfloat16 [4, 352], P('section'), may hold values from -3 to 3
- norm_gain: bfloat16 [4, 352], P('section'), may hold values from 0.099609375 to 1.8984375
- norm_bias: bfloat16 [4, 352], P('section'), may hold values from -3 to 3
- proj_in: bfloat16 [4, 352, 1408], P('section', None, 'dp'), may hold values from -0.3125 to 0.3125
- bias_in: bfloat16 [4, 1408], P('section'), may hold values from -3 to 3
- grn_gamma: bfloat16 [4, 1408], P('section'), may hold values from -3 to 3
- grn_beta: bfloat16 [4, 1408], P('section'), may hold values from -2 to 2
- proj_out: bfloat16 [4, 1408, 352], P('section', 'dp'), may hold values from -0.15625 to 0.15625
- bias_out: bfloat16 [4, 352], P('section'), may hold values from -3 to 3
Outputs:
- saved: bfloat16 [4, 4, 8, 64, 48, 352], P('section', None, 'dp', 'row')
The draws below stay inside these ranges and needn't reach their ends.
All inputs are finite; a program needn't handle non-finite values.
Results may differ from the reference program's by a relative error of at most 0.015.
Values may be sent and summed in bfloat16 or wider, within the bound.
A program may use at most 64 MiB of HBM per device.

```python
import jax
import jax.numpy as jnp
from jax import lax

C = 352
FF = 1408
COLS = 48
MICRO = 4
HEIGHT = 64
IMAGES = 8
BLOCKS = 4


def draw_inputs(key, part):
    key_noise, key_rows, key_chan, key_dir, key_amp = jax.random.split(jax.random.fold_in(key, 17), 5)
    full_shape = (MICRO, IMAGES, HEIGHT, COLS, C)
    noise = jax.random.normal(key_noise, full_shape, jnp.float32)
    row_scale = jnp.exp(jax.random.uniform(key_rows, (MICRO, IMAGES, HEIGHT, 1, 1), jnp.float32, -0.7, 0.7))
    chan_scale = jnp.exp(jax.random.uniform(key_chan, (MICRO, IMAGES, 1, 1, C), jnp.float32, 0.0, 2.3)) * 0.2
    direction = jax.random.normal(key_dir, (MICRO, IMAGES, 1, 1, C), jnp.float32)
    amplitude = jax.random.uniform(key_amp, (MICRO, IMAGES, 1, 1, 1), jnp.float32, 0.75, 2.0)
    row_ramp = (jnp.arange(HEIGHT, dtype=jnp.float32) / (HEIGHT - 1)).reshape(1, 1, HEIGHT, 1, 1)
    values = noise * chan_scale * row_scale + amplitude * row_ramp * direction
    return jnp.clip(values, -8.0, 8.0).astype(jnp.bfloat16)


def block_levels(stream_key, dims, pieces, least, high):
    gain, own = 1.0, jax.random.fold_in(stream_key, 6)
    for dim, blocks in pieces:
        draws = jnp.exp(jax.random.uniform(jax.random.fold_in(own, dim), (blocks,), jnp.float32, least / len(pieces), high / len(pieces)))
        gain = gain * jnp.repeat(draws, dims[dim] // blocks).reshape([-1 if axis == dim else 1 for axis in range(len(dims))])
    return gain


def bell_draw(rng, extent, scale, limit, cuts=(), held_as=jnp.bfloat16):
    drawn = scale * jax.random.normal(rng, extent, jnp.float32)
    if cuts:
        drawn = drawn * block_levels(rng, extent, cuts, -0.22, 0.18)
    return jnp.clip(drawn, -limit, limit).astype(held_as)


def setup_inputs(seed: int = 0) -> dict:
    splits = jax.random.split(jax.random.key(seed), 12)
    return {
        "inputs": draw_inputs(jax.random.fold_in(splits[11], 71), 0),
        "depth_kernel": bell_draw(splits[1], (BLOCKS, 7, 7, C), 49 ** -0.5, 0.875, ((0, 4),)),
        "depth_bias": bell_draw(splits[2], (BLOCKS, C), 0.5, 3.0, ((0, 4),)),
        "norm_gain": jnp.clip(1.0 + 0.18 * jax.random.normal(splits[3], (BLOCKS, C), jnp.float32), 0.099609375, 1.8984375).astype(jnp.bfloat16),
        "norm_bias": bell_draw(splits[4], (BLOCKS, C), 0.5, 3.0, ((0, 4),)),
        "proj_in": bell_draw(splits[5], (BLOCKS, C, FF), C ** -0.5, 0.3125, ((0, 4), (2, 8))),
        "bias_in": bell_draw(splits[6], (BLOCKS, FF), 0.5, 3.0, ((0, 4),)),
        "grn_gamma": bell_draw(splits[7], (BLOCKS, FF), 0.5, 3.0, ((0, 4),)),
        "grn_beta": bell_draw(splits[8], (BLOCKS, FF), 0.3, 2.0, ((0, 4),)),
        "proj_out": bell_draw(splits[9], (BLOCKS, FF, C), FF ** -0.5, 0.15625, ((0, 4), (1, 8))),
        "bias_out": bell_draw(splits[10], (BLOCKS, C), 0.5, 3.0, ((0, 4),)),
    }


EPS_NORM = 1e-06
EPS_GRN = 1e-06

def depthwise(padded, kernel, bias_term):
    channels = padded.shape[-1]
    conv_out = lax.conv_general_dilated(padded.astype(jnp.float32), kernel.astype(jnp.float32)[:, :, None, :], (1, 1), 'VALID', dimension_numbers=('NHWC', 'HWIO', 'NHWC'), feature_group_count=channels, precision=lax.Precision.HIGHEST)
    return conv_out + bias_term.astype(jnp.float32)

def one_block(current, params):
    depth_kernel, depth_bias, norm_gain, norm_bias, proj_in, bias_in, grn_gamma, grn_beta, proj_out, bias_out = params
    num_items, num_rows, num_cols, channels = current.shape
    padded = jnp.pad(current, ((0, 0), (3, 3), (3, 3), (0, 0)))
    conv_out = depthwise(padded, depth_kernel, depth_bias)
    center = conv_out - lax.optimization_barrier(jnp.mean(conv_out, axis=-1, keepdims=True))
    spread = lax.optimization_barrier(jnp.mean(center * center, axis=-1, keepdims=True))
    normed = (center * lax.rsqrt(spread + EPS_NORM) * norm_gain.astype(jnp.float32) + norm_bias.astype(jnp.float32)).astype(jnp.bfloat16)
    flat_rows = normed.reshape(num_items * num_rows * num_cols, channels)
    raised = jnp.dot(flat_rows, proj_in, preferred_element_type=jnp.float32) + bias_in.astype(jnp.float32)
    active = jax.nn.gelu(raised, approximate=False).astype(jnp.bfloat16)
    grouped = active.reshape(num_items, num_rows * num_cols, -1).astype(jnp.float32)
    total_sq = lax.optimization_barrier(jnp.sum(grouped * grouped, axis=1))
    magnitude = jnp.sqrt(total_sq)
    grn_ratio = magnitude / (lax.optimization_barrier(jnp.mean(magnitude, axis=-1, keepdims=True)) + EPS_GRN)
    hidden = (grn_gamma.astype(jnp.float32) * grouped * grn_ratio[:, None, :] + grn_beta.astype(jnp.float32) + grouped).astype(jnp.bfloat16)
    update = jnp.dot(hidden.reshape(num_items * num_rows * num_cols, -1), proj_out, preferred_element_type=jnp.float32) + bias_out.astype(jnp.float32)
    return (current.astype(jnp.float32) + update.reshape(num_items, num_rows, num_cols, channels)).astype(jnp.bfloat16)

def reference(inputs, depth_kernel, depth_bias, norm_gain, norm_bias, proj_in, bias_in, grn_gamma, grn_beta, proj_out, bias_out):
    per_layer = [[] for layer_index in range(BLOCKS)]
    for micro_index in range(MICRO):
        current = inputs[micro_index]
        for layer_index in range(BLOCKS):
            params = (depth_kernel[layer_index], depth_bias[layer_index], norm_gain[layer_index], norm_bias[layer_index], proj_in[layer_index], bias_in[layer_index], grn_gamma[layer_index], grn_beta[layer_index], proj_out[layer_index], bias_out[layer_index])
            current = one_block(current, params)
            per_layer[layer_index].append(current)
    return jnp.stack([jnp.stack(layer_list) for layer_list in per_layer])
```

```python
import functools

import jax
import jax.numpy as jnp
from jax import lax
from jax.experimental import pallas as pl
from jax.experimental.pallas import tpu as pltpu
from jax.sharding import PartitionSpec as P

MESH = pl.DeviceIdType.MESH

EPS_NORM = 1e-06
EPS_GRN = 1e-06


def extended(cells, sides, width):
    for axis, dim in sides:
        count = lax.axis_size(axis)
        ends = count - 1
        head = lax.slice_in_dim(cells, 0, width, axis=dim)
        tail = lax.slice_in_dim(cells, cells.shape[dim] - width, cells.shape[dim], axis=dim)
        cells = jnp.concatenate(
            [
                lax.ppermute(tail, axis, [(i, (i + 1) % count) for i in range(ends)]),
                cells,
                lax.ppermute(head, axis, [((i + 1) % count, i) for i in range(ends)]),
            ],
            axis=dim,
        )
    return cells


def _row_sum_kernel(n, part_ref, out_ref, slots, send_sem, recv_sem):
    me = lax.axis_index("row")
    barrier = pltpu.get_barrier_semaphore()
    for k in range(1, n):
        pl.semaphore_signal(
            barrier, inc=1, device_id={"row": lax.rem(me + k, n)}, device_id_type=MESH
        )
    pl.semaphore_wait(barrier, n - 1)
    sends = []
    for k in range(1, n):
        copy = pltpu.make_async_remote_copy(
            src_ref=part_ref,
            dst_ref=slots.at[me],
            send_sem=send_sem.at[k],
            recv_sem=recv_sem.at[me],
            device_id={"row": lax.rem(me + k, n)},
            device_id_type=MESH,
        )
        copy.start()
        sends.append(copy)
    slots[me] = part_ref[...]
    for k in range(1, n):
        src = lax.rem(me + k, n)
        pltpu.make_async_remote_copy(
            src_ref=part_ref,
            dst_ref=slots.at[src],
            send_sem=send_sem.at[k],
            recv_sem=recv_sem.at[src],
            device_id={"row": src},
            device_id_type=MESH,
        ).wait_recv()
    for copy in sends:
        copy.wait_send()
    total = slots[0]
    for j in range(1, n):
        total = total + slots[j]
    out_ref[...] = total


def row_sum(part):
    n = lax.axis_size("row")
    return pl.pallas_call(
        functools.partial(_row_sum_kernel, n),
        out_shape=jax.ShapeDtypeStruct(part.shape, part.dtype),
        in_specs=[pl.BlockSpec(memory_space=pltpu.VMEM)],
        out_specs=pl.BlockSpec(memory_space=pltpu.VMEM),
        scratch_shapes=[
            pltpu.VMEM((n,) + part.shape, part.dtype),
            pltpu.SemaphoreType.DMA((n,)),
            pltpu.SemaphoreType.DMA((n,)),
        ],
        compiler_params=pltpu.CompilerParams(collective_id=0, has_side_effects=True),
    )(part)


def passed_along(x, axis, by):
    count = lax.axis_size(axis)
    pairs = [(i, i + by) for i in range(count) if 0 <= i + by < count]
    return lax.ppermute(x, axis, pairs)


def depthwise(padded, kernel, bias_term):
    channels = padded.shape[-1]
    conv_out = lax.conv_general_dilated(
        padded.astype(jnp.float32),
        kernel.astype(jnp.float32)[:, :, None, :],
        (1, 1),
        "VALID",
        dimension_numbers=("NHWC", "HWIO", "NHWC"),
        feature_group_count=channels,
        precision=lax.Precision.HIGHEST,
    )
    return conv_out + bias_term.astype(jnp.float32)


def conv_block(current, params):
    (
        depth_kernel,
        depth_bias,
        norm_gain,
        norm_bias,
        proj_in,
        bias_in,
        grn_gamma,
        grn_beta,
        proj_out,
        bias_out,
    ) = params
    num_items, num_rows, num_cols, channels = current.shape
    padded = extended(current, (("row", 1),), 3)
    padded = jnp.pad(padded, ((0, 0), (0, 0), (3, 3), (0, 0)))
    conv_out = depthwise(padded, depth_kernel, depth_bias)
    center = conv_out - jnp.mean(conv_out, axis=-1, keepdims=True)
    spread = jnp.mean(center * center, axis=-1, keepdims=True)
    normed = (
        center * lax.rsqrt(spread + EPS_NORM) * norm_gain.astype(jnp.float32)
        + norm_bias.astype(jnp.float32)
    ).astype(jnp.bfloat16)
    flat_rows = normed.reshape(num_items * num_rows * num_cols, channels)
    raised = jnp.dot(flat_rows, proj_in, preferred_element_type=jnp.float32) + bias_in.astype(
        jnp.float32
    )
    active = jax.nn.gelu(raised, approximate=False).astype(jnp.bfloat16)
    grouped = active.reshape(num_items, num_rows * num_cols, -1).astype(jnp.float32)
    local_sq = jnp.sum(grouped * grouped, axis=1)
    total_sq = row_sum(local_sq)
    magnitude = jnp.sqrt(total_sq)
    grn_ratio = magnitude / (jnp.mean(magnitude, axis=-1, keepdims=True) + EPS_GRN)
    hidden = (
        grn_gamma.astype(jnp.float32) * grouped * grn_ratio[:, None, :]
        + grn_beta.astype(jnp.float32)
        + grouped
    ).astype(jnp.bfloat16)
    update = jnp.dot(
        hidden.reshape(num_items * num_rows * num_cols, -1),
        proj_out,
        preferred_element_type=jnp.float32,
    ) + bias_out.astype(jnp.float32)
    return (
        current.astype(jnp.float32) + update.reshape(num_items, num_rows, num_cols, channels)
    ).astype(jnp.bfloat16)


def on_device(
    inputs,
    depth_kernel,
    depth_bias,
    norm_gain,
    norm_bias,
    proj_in,
    bias_in,
    grn_gamma,
    grn_beta,
    proj_out,
    bias_out,
):
    proj_in, proj_out = (
        lax.all_gather(proj_in, "dp", axis=2, tiled=True),
        lax.all_gather(proj_out, "dp", axis=1, tiled=True),
    )
    sections = lax.axis_size("section")
    section_index = lax.axis_index("section")
    num_micro = inputs.shape[0]
    own_params = (
        depth_kernel[0],
        depth_bias[0],
        norm_gain[0],
        norm_bias[0],
        proj_in[0],
        bias_in[0],
        grn_gamma[0],
        grn_beta[0],
        proj_out[0],
        bias_out[0],
    )
    num_ticks = num_micro + sections - 1
    arriving = jnp.zeros_like(inputs[0])
    saved = jnp.zeros_like(inputs)
    for tick_index in range(num_ticks):
        fresh_input = inputs[min(tick_index, num_micro - 1)]
        current = jnp.where(section_index == 0, fresh_input, arriving)
        produced = conv_block(current, own_params)
        slot_index = tick_index - section_index
        is_valid = jnp.logical_and(slot_index >= 0, slot_index < num_micro)
        safe_slot = jnp.clip(slot_index, 0, num_micro - 1)
        previous = lax.dynamic_index_in_dim(saved, safe_slot, 0, keepdims=False)
        saved = lax.dynamic_update_index_in_dim(
            saved, jnp.where(is_valid, produced, previous), safe_slot, 0
        )
        if tick_index + 1 < num_ticks:
            arriving = passed_along(produced, "section", 1)
    return saved[None]


def solution(mesh):
    return jax.shard_map(
        on_device,
        mesh=mesh,
        in_specs=(
            P(None, "dp", "row", None, None),
            P("section", None, None, None),
            P("section", None),
            P("section", None),
            P("section", None),
            P("section", None, "dp"),
            P("section", None),
            P("section", None),
            P("section", None),
            P("section", "dp", None),
            P("section", None),
        ),
        out_specs=P("section", None, "dp", "row", None, None),
        check_vma=False,
    )
```

```python
import functools

import jax
import jax.numpy as jnp
from jax import lax
from jax.experimental import pallas as pl
from jax.experimental.pallas import tpu as pltpu
from jax.sharding import PartitionSpec as P

MESH = pl.DeviceIdType.MESH

EPS_NORM = 1e-06
EPS_GRN = 1e-06


def extended(cells, sides, width):
    for axis, dim in sides:
        count = lax.axis_size(axis)
        ends = count - 1
        head = lax.slice_in_dim(cells, 0, width, axis=dim)
        tail = lax.slice_in_dim(cells, cells.shape[dim] - width, cells.shape[dim], axis=dim)
        cells = jnp.concatenate(
            [
                lax.ppermute(tail, axis, [(i, (i + 1) % count) for i in range(ends)]),
                cells,
                lax.ppermute(head, axis, [((i + 1) % count, i) for i in range(ends)]),
            ],
            axis=dim,
        )
    return cells


def _row_sum_kernel(n, part_ref, out_ref, slots, send_sem, recv_sem):
    me = lax.axis_index("row")
    barrier = pltpu.get_barrier_semaphore()
    for k in range(1, n):
        pl.semaphore_signal(
            barrier, inc=1, device_id={"row": lax.rem(me + k, n)}, device_id_type=MESH
        )
    pl.semaphore_wait(barrier, n - 1)
    sends = []
    for k in range(1, n):
        copy = pltpu.make_async_remote_copy(
            src_ref=part_ref,
            dst_ref=slots.at[me],
            send_sem=send_sem.at[k],
            recv_sem=recv_sem.at[me],
            device_id={"row": lax.rem(me + k, n)},
            device_id_type=MESH,
        )
        copy.start()
        sends.append(copy)
    slots[me] = part_ref[...]
    for k in range(1, n):
        src = lax.rem(me + k, n)
        pltpu.make_async_remote_copy(
            src_ref=part_ref,
            dst_ref=slots.at[src],
            send_sem=send_sem.at[k],
            recv_sem=recv_sem.at[src],
            device_id={"row": src},
            device_id_type=MESH,
        ).wait_recv()
    for copy in sends:
        copy.wait_send()
    total = slots[0]
    for j in range(1, n):
        total = total + slots[j]
    out_ref[...] = total


def row_sum(part):
    n = lax.axis_size("row")
    return pl.pallas_call(
        functools.partial(_row_sum_kernel, n),
        out_shape=jax.ShapeDtypeStruct(part.shape, part.dtype),
        in_specs=[pl.BlockSpec(memory_space=pltpu.VMEM)],
        out_specs=pl.BlockSpec(memory_space=pltpu.VMEM),
        scratch_shapes=[
            pltpu.VMEM((n,) + part.shape, part.dtype),
            pltpu.SemaphoreType.DMA((n,)),
            pltpu.SemaphoreType.DMA((n,)),
        ],
        compiler_params=pltpu.CompilerParams(collective_id=0, has_side_effects=True),
    )(part)


def passed_along(x, axis, by):
    count = lax.axis_size(axis)
    pairs = [(i, i + by) for i in range(count) if 0 <= i + by < count]
    return lax.ppermute(x, axis, pairs)


def depthwise(padded, kernel, bias_term):
    channels = padded.shape[-1]
    conv_out = lax.conv_general_dilated(
        padded.astype(jnp.float32),
        kernel.astype(jnp.float32)[:, :, None, :],
        (1, 1),
        "VALID",
        dimension_numbers=("NHWC", "HWIO", "NHWC"),
        feature_group_count=channels,
        precision=lax.Precision.HIGHEST,
    )
    return conv_out + bias_term.astype(jnp.float32)


def conv_block(padded, params):
    (
        depth_kernel,
        depth_bias,
        norm_gain,
        norm_bias,
        proj_in,
        bias_in,
        grn_gamma,
        grn_beta,
        proj_out,
        bias_out,
    ) = params
    current = padded[:, 3:-3]
    num_items, num_rows, num_cols, channels = current.shape
    padded = jnp.pad(padded, ((0, 0), (0, 0), (3, 3), (0, 0)))
    conv_out = depthwise(padded, depth_kernel, depth_bias)
    center = conv_out - jnp.mean(conv_out, axis=-1, keepdims=True)
    spread = jnp.mean(center * center, axis=-1, keepdims=True)
    normed = (
        center * lax.rsqrt(spread + EPS_NORM) * norm_gain.astype(jnp.float32)
        + norm_bias.astype(jnp.float32)
    ).astype(jnp.bfloat16)
    flat_rows = normed.reshape(num_items * num_rows * num_cols, channels)
    raised = jnp.dot(flat_rows, proj_in, preferred_element_type=jnp.float32) + bias_in.astype(
        jnp.float32
    )
    active = jax.nn.gelu(raised, approximate=False).astype(jnp.bfloat16)
    grouped = active.reshape(num_items, num_rows * num_cols, -1).astype(jnp.float32)
    local_sq = jnp.sum(grouped * grouped, axis=1)
    total_sq = row_sum(local_sq)
    magnitude = jnp.sqrt(total_sq)
    grn_ratio = magnitude / (jnp.mean(magnitude, axis=-1, keepdims=True) + EPS_GRN)
    hidden = (
        grn_gamma.astype(jnp.float32) * grouped * grn_ratio[:, None, :]
        + grn_beta.astype(jnp.float32)
        + grouped
    ).astype(jnp.bfloat16)
    update = jnp.dot(
        hidden.reshape(num_items * num_rows * num_cols, -1),
        proj_out,
        preferred_element_type=jnp.float32,
    ) + bias_out.astype(jnp.float32)
    return (
        current.astype(jnp.float32) + update.reshape(num_items, num_rows, num_cols, channels)
    ).astype(jnp.bfloat16)


def handed_on(produced, sections, rows):
    axes = ("section", "row")

    def pairs(shift):
        return [
            (s * rows + r, (s + 1) * rows + r + shift)
            for s in range(sections - 1)
            for r in range(rows)
            if 0 <= r + shift < rows
        ]

    above = lax.ppermute(produced[:, -3:], axes, pairs(1))
    middle = lax.ppermute(produced, axes, pairs(0))
    below = lax.ppermute(produced[:, :3], axes, pairs(-1))
    return jnp.concatenate([above, middle, below], axis=1)


def on_device(
    inputs,
    depth_kernel,
    depth_bias,
    norm_gain,
    norm_bias,
    proj_in,
    bias_in,
    grn_gamma,
    grn_beta,
    proj_out,
    bias_out,
):
    fresh = extended(inputs[:, 0], (("row", 1),), 3)[:, None]
    proj_in, proj_out = (
        lax.all_gather(proj_in, "dp", axis=2, tiled=True),
        lax.all_gather(proj_out, "dp", axis=1, tiled=True),
    )
    sections = lax.axis_size("section")
    rows = lax.axis_size("row")
    section_index = lax.axis_index("section")
    num_micro = inputs.shape[0]
    own_params = (
        depth_kernel[0],
        depth_bias[0],
        norm_gain[0],
        norm_bias[0],
        proj_in[0],
        bias_in[0],
        grn_gamma[0],
        grn_beta[0],
        proj_out[0],
        bias_out[0],
    )
    num_ticks = num_micro + sections - 1
    arriving = jnp.zeros_like(fresh[0])
    saved = jnp.zeros_like(inputs)
    for tick_index in range(num_ticks):
        fresh_input = fresh[min(tick_index, num_micro - 1)]
        current = jnp.where(section_index == 0, fresh_input, arriving)
        produced = conv_block(current, own_params)
        slot_index = tick_index - section_index
        is_valid = jnp.logical_and(slot_index >= 0, slot_index < num_micro)
        safe_slot = jnp.clip(slot_index, 0, num_micro - 1)
        previous = lax.dynamic_index_in_dim(saved, safe_slot, 0, keepdims=False)
        saved = lax.dynamic_update_index_in_dim(
            saved, jnp.where(is_valid, produced, previous), safe_slot, 0
        )
        if tick_index + 1 < num_ticks:
            arriving = handed_on(produced, sections, rows)
    return saved[None]


def solution(mesh):
    return jax.shard_map(
        on_device,
        mesh=mesh,
        in_specs=(
            P(None, "dp", "row", None, None),
            P("section", None, None, None),
            P("section", None),
            P("section", None),
            P("section", None),
            P("section", None, "dp"),
            P("section", None),
            P("section", None),
            P("section", None),
            P("section", "dp", None),
            P("section", None),
        ),
        out_specs=P("section", None, "dp", "row", None, None),
        check_vma=False,
    )
```

```python
import functools
import math

import jax
import jax.numpy as jnp
from jax import lax
from jax.experimental import pallas as pl
from jax.experimental.pallas import tpu as pltpu
from jax.sharding import PartitionSpec as P

MESH = pl.DeviceIdType.MESH

EPS_NORM = 1e-06
EPS_GRN = 1e-06


def extended(cells, sides, width):
    for axis, dim in sides:
        count = lax.axis_size(axis)
        ends = count - 1
        head = lax.slice_in_dim(cells, 0, width, axis=dim)
        tail = lax.slice_in_dim(cells, cells.shape[dim] - width, cells.shape[dim], axis=dim)
        cells = jnp.concatenate(
            [
                lax.ppermute(tail, axis, [(i, (i + 1) % count) for i in range(ends)]),
                cells,
                lax.ppermute(head, axis, [((i + 1) % count, i) for i in range(ends)]),
            ],
            axis=dim,
        )
    return cells


def _pointwise_kernel(
    n,
    normed_ref,
    current_ref,
    proj_in_ref,
    bias_in_ref,
    gamma_ref,
    beta_ref,
    proj_out_ref,
    bias_out_ref,
    out_ref,
    act_ref,
    slots,
    send_sem,
    recv_sem,
):
    me = lax.axis_index("row")
    barrier = pltpu.get_barrier_semaphore()
    for k in range(1, n):
        pl.semaphore_signal(
            barrier, inc=1, device_id={"row": lax.rem(me + k, n)}, device_id_type=MESH
        )
    raised = jnp.dot(
        normed_ref[...], proj_in_ref[...], preferred_element_type=jnp.float32
    ) + bias_in_ref[...].astype(jnp.float32)
    active = (0.5 * raised * (1.0 + lax.erf(raised * (1.0 / math.sqrt(2.0))))).astype(
        jnp.bfloat16
    )
    act_ref[...] = active
    grouped = active.astype(jnp.float32)
    slots[me] = jnp.sum(grouped * grouped, axis=0, keepdims=True)
    pl.semaphore_wait(barrier, n - 1)
    sends = []
    for k in range(1, n):
        copy = pltpu.make_async_remote_copy(
            src_ref=slots.at[me],
            dst_ref=slots.at[me],
            send_sem=send_sem.at[k],
            recv_sem=recv_sem.at[me],
            device_id={"row": lax.rem(me + k, n)},
            device_id_type=MESH,
        )
        copy.start()
        sends.append(copy)
    for k in range(1, n):
        src = lax.rem(me + k, n)
        pltpu.make_async_remote_copy(
            src_ref=slots.at[src],
            dst_ref=slots.at[src],
            send_sem=send_sem.at[k],
            recv_sem=recv_sem.at[src],
            device_id={"row": src},
            device_id_type=MESH,
        ).wait_recv()
    for copy in sends:
        copy.wait_send()
    total_sq = slots[0]
    for j in range(1, n):
        total_sq = total_sq + slots[j]
    magnitude = jnp.sqrt(total_sq)
    grn_ratio = magnitude / (jnp.mean(magnitude, axis=-1, keepdims=True) + EPS_GRN)
    grouped = act_ref[...].astype(jnp.float32)
    hidden = (
        gamma_ref[...].astype(jnp.float32) * grouped * grn_ratio
        + beta_ref[...].astype(jnp.float32)
        + grouped
    ).astype(jnp.bfloat16)
    update = jnp.dot(
        hidden, proj_out_ref[...], preferred_element_type=jnp.float32
    ) + bias_out_ref[...].astype(jnp.float32)
    out_ref[...] = (current_ref[...].astype(jnp.float32) + update).astype(out_ref.dtype)


def pointwise(normed, current, proj_in, bias_in, grn_gamma, grn_beta, proj_out, bias_out):
    n = lax.axis_size("row")
    cells, channels = normed.shape
    hidden_units = proj_in.shape[1]
    vmem = pl.BlockSpec(memory_space=pltpu.VMEM)
    return pl.pallas_call(
        functools.partial(_pointwise_kernel, n),
        out_shape=jax.ShapeDtypeStruct(current.shape, current.dtype),
        in_specs=[vmem] * 8,
        out_specs=vmem,
        scratch_shapes=[
            pltpu.VMEM((cells, hidden_units), jnp.bfloat16),
            pltpu.VMEM((n, 1, hidden_units), jnp.float32),
            pltpu.SemaphoreType.DMA((n,)),
            pltpu.SemaphoreType.DMA((n,)),
        ],
        compiler_params=pltpu.CompilerParams(collective_id=0, has_side_effects=True),
        cost_estimate=pl.CostEstimate(
            flops=4 * cells * channels * hidden_units,
            transcendentals=cells * hidden_units,
            bytes_accessed=4 * channels * hidden_units + 4 * cells * channels,
        ),
    )(
        normed,
        current,
        proj_in,
        bias_in.reshape(1, -1),
        grn_gamma.reshape(1, -1),
        grn_beta.reshape(1, -1),
        proj_out,
        bias_out.reshape(1, -1),
    )


def passed_along(x, axis, by):
    count = lax.axis_size(axis)
    pairs = [(i, i + by) for i in range(count) if 0 <= i + by < count]
    return lax.ppermute(x, axis, pairs)


def depthwise(padded, kernel, bias_term):
    channels = padded.shape[-1]
    conv_out = lax.conv_general_dilated(
        padded.astype(jnp.float32),
        kernel.astype(jnp.float32)[:, :, None, :],
        (1, 1),
        "VALID",
        dimension_numbers=("NHWC", "HWIO", "NHWC"),
        feature_group_count=channels,
        precision=lax.Precision.HIGHEST,
    )
    return conv_out + bias_term.astype(jnp.float32)


def conv_block(current, params):
    (
        depth_kernel,
        depth_bias,
        norm_gain,
        norm_bias,
        proj_in,
        bias_in,
        grn_gamma,
        grn_beta,
        proj_out,
        bias_out,
    ) = params
    num_items, num_rows, num_cols, channels = current.shape
    padded = extended(current, (("row", 1),), 3)
    padded = jnp.pad(padded, ((0, 0), (0, 0), (3, 3), (0, 0)))
    conv_out = depthwise(padded, depth_kernel, depth_bias)
    center = conv_out - jnp.mean(conv_out, axis=-1, keepdims=True)
    spread = jnp.mean(center * center, axis=-1, keepdims=True)
    normed = (
        center * lax.rsqrt(spread + EPS_NORM) * norm_gain.astype(jnp.float32)
        + norm_bias.astype(jnp.float32)
    ).astype(jnp.bfloat16)
    flat_rows = normed.reshape(num_items * num_rows * num_cols, channels)
    update = pointwise(
        flat_rows,
        current.reshape(num_items * num_rows * num_cols, channels),
        proj_in,
        bias_in,
        grn_gamma,
        grn_beta,
        proj_out,
        bias_out,
    )
    return update.reshape(num_items, num_rows, num_cols, channels)


def on_device(
    inputs,
    depth_kernel,
    depth_bias,
    norm_gain,
    norm_bias,
    proj_in,
    bias_in,
    grn_gamma,
    grn_beta,
    proj_out,
    bias_out,
):
    proj_in, proj_out = (
        lax.all_gather(proj_in, "dp", axis=2, tiled=True),
        lax.all_gather(proj_out, "dp", axis=1, tiled=True),
    )
    sections = lax.axis_size("section")
    section_index = lax.axis_index("section")
    num_micro = inputs.shape[0]
    own_params = (
        depth_kernel[0],
        depth_bias[0],
        norm_gain[0],
        norm_bias[0],
        proj_in[0],
        bias_in[0],
        grn_gamma[0],
        grn_beta[0],
        proj_out[0],
        bias_out[0],
    )
    num_ticks = num_micro + sections - 1
    arriving = jnp.zeros_like(inputs[0])
    saved = jnp.zeros_like(inputs)
    for tick_index in range(num_ticks):
        fresh_input = inputs[min(tick_index, num_micro - 1)]
        current = jnp.where(section_index == 0, fresh_input, arriving)
        produced = conv_block(current, own_params)
        slot_index = tick_index - section_index
        is_valid = jnp.logical_and(slot_index >= 0, slot_index < num_micro)
        safe_slot = jnp.clip(slot_index, 0, num_micro - 1)
        previous = lax.dynamic_index_in_dim(saved, safe_slot, 0, keepdims=False)
        saved = lax.dynamic_update_index_in_dim(
            saved, jnp.where(is_valid, produced, previous), safe_slot, 0
        )
        if tick_index + 1 < num_ticks:
            arriving = passed_along(produced, "section", 1)
    return saved[None]


def solution(mesh):
    return jax.shard_map(
        on_device,
        mesh=mesh,
        in_specs=(
            P(None, "dp", "row", None, None),
            P("section", None, None, None),
            P("section", None),
            P("section", None),
            P("section", None),
            P("section", None, "dp"),
            P("section", None),
            P("section", None),
            P("section", None),
            P("section", "dp", None),
            P("section", None),
        ),
        out_specs=P("section", None, "dp", "row", None, None),
        check_vma=False,
    )
```

```python
import functools
import math

import jax
import jax.numpy as jnp
from jax import lax
from jax.experimental import pallas as pl
from jax.experimental.pallas import tpu as pltpu
from jax.sharding import PartitionSpec as P

MESH = pl.DeviceIdType.MESH

EPS_NORM = 1e-06
EPS_GRN = 1e-06


def extended(cells, sides, width):
    for axis, dim in sides:
        count = lax.axis_size(axis)
        ends = count - 1
        head = lax.slice_in_dim(cells, 0, width, axis=dim)
        tail = lax.slice_in_dim(cells, cells.shape[dim] - width, cells.shape[dim], axis=dim)
        cells = jnp.concatenate(
            [
                lax.ppermute(tail, axis, [(i, (i + 1) % count) for i in range(ends)]),
                cells,
                lax.ppermute(head, axis, [((i + 1) % count, i) for i in range(ends)]),
            ],
            axis=dim,
        )
    return cells


def _pointwise_kernel(
    n,
    sections,
    hand_on,
    normed_ref,
    current_ref,
    fresh_ref,
    proj_in_ref,
    bias_in_ref,
    gamma_ref,
    beta_ref,
    proj_out_ref,
    bias_out_ref,
    out_ref,
    *rest,
):
    if hand_on:
        next_ref, act_ref, slots, send_sem, recv_sem, hand_send, hand_recv = rest
    else:
        act_ref, slots, send_sem, recv_sem = rest
    me = lax.axis_index("row")
    section = lax.axis_index("section")
    barrier = pltpu.get_barrier_semaphore()
    for k in range(1, n):
        pl.semaphore_signal(
            barrier, inc=1, device_id={"row": lax.rem(me + k, n)}, device_id_type=MESH
        )
    waits = n - 1
    if hand_on:
        cells = out_ref.shape[0]
        edge = 3 * cells // 4
        has_above = me > 0
        has_below = me < n - 1
        has_prev = section > 0
        has_next = section < sections - 1
        for shift, cond in ((0, True), (-1, has_above), (1, has_below)):
            @pl.when(jnp.logical_and(has_prev, cond))
            def _():
                pl.semaphore_signal(
                    barrier,
                    inc=1,
                    device_id={"section": section - 1, "row": me + shift},
                    device_id_type=MESH,
                )
        waits = waits + jnp.where(
            has_next,
            1 + has_above.astype(jnp.int32) + has_below.astype(jnp.int32),
            0,
        )
    raised = jnp.dot(
        normed_ref[...], proj_in_ref[...], preferred_element_type=jnp.float32
    ) + bias_in_ref[...].astype(jnp.float32)
    active = (0.5 * raised * (1.0 + lax.erf(raised * (1.0 / math.sqrt(2.0))))).astype(
        jnp.bfloat16
    )
    act_ref[...] = active
    grouped = active.astype(jnp.float32)
    slots[me] = jnp.sum(grouped * grouped, axis=0, keepdims=True)
    pl.semaphore_wait(barrier, waits)
    sends = []
    for k in range(1, n):
        copy = pltpu.make_async_remote_copy(
            src_ref=slots.at[me],
            dst_ref=slots.at[me],
            send_sem=send_sem.at[k],
            recv_sem=recv_sem.at[me],
            device_id={"row": lax.rem(me + k, n)},
            device_id_type=MESH,
        )
        copy.start()
        sends.append(copy)
    if hand_on:
        @pl.when(section == 0)
        def _():
            next_ref[...] = fresh_ref[...]

        @pl.when(jnp.logical_and(has_prev, jnp.logical_not(has_above)))
        def _():
            next_ref[pl.ds(0, edge), :] = jnp.zeros((edge, next_ref.shape[1]), next_ref.dtype)

        @pl.when(jnp.logical_and(has_prev, jnp.logical_not(has_below)))
        def _():
            next_ref[pl.ds(edge + cells, edge), :] = jnp.zeros(
                (edge, next_ref.shape[1]), next_ref.dtype
            )

    for k in range(1, n):
        src = lax.rem(me + k, n)
        pltpu.make_async_remote_copy(
            src_ref=slots.at[src],
            dst_ref=slots.at[src],
            send_sem=send_sem.at[k],
            recv_sem=recv_sem.at[src],
            device_id={"row": src},
            device_id_type=MESH,
        ).wait_recv()
    for copy in sends:
        copy.wait_send()
    total_sq = slots[0]
    for j in range(1, n):
        total_sq = total_sq + slots[j]
    magnitude = jnp.sqrt(total_sq)
    grn_ratio = magnitude / (jnp.mean(magnitude, axis=-1, keepdims=True) + EPS_GRN)
    grouped = act_ref[...].astype(jnp.float32)
    hidden = (
        gamma_ref[...].astype(jnp.float32) * grouped * grn_ratio
        + beta_ref[...].astype(jnp.float32)
        + grouped
    ).astype(jnp.bfloat16)
    update = jnp.dot(
        hidden, proj_out_ref[...], preferred_element_type=jnp.float32
    ) + bias_out_ref[...].astype(jnp.float32)
    out_ref[...] = (current_ref[...].astype(jnp.float32) + update).astype(out_ref.dtype)
    if not hand_on:
        return
    pieces = (
        (1, out_ref, pl.ds(edge, cells), 0, True),
        (2, out_ref.at[pl.ds(0, edge)], pl.ds(edge + cells, edge), -1, has_above),
        (0, out_ref.at[pl.ds(cells - edge, edge)], pl.ds(0, edge), 1, has_below),
    )

    def piece_copy(slot, src, dst, shift, peer_row):
        return pltpu.make_async_remote_copy(
            src_ref=src,
            dst_ref=next_ref.at[dst],
            send_sem=hand_send.at[slot],
            recv_sem=hand_recv.at[slot],
            device_id={"section": section + 1, "row": peer_row},
            device_id_type=MESH,
        )

    for slot, src, dst, shift, cond in pieces:
        @pl.when(jnp.logical_and(has_next, cond))
        def _():
            piece_copy(slot, src, dst, shift, me + shift).start()

    arrivals = {0: has_above, 1: True, 2: has_below}
    for slot, src, dst, shift, cond in pieces:
        @pl.when(jnp.logical_and(has_prev, arrivals[slot]))
        def _():
            piece_copy(slot, src, dst, shift, me).wait_recv()

    for slot, src, dst, shift, cond in pieces:
        @pl.when(jnp.logical_and(has_next, cond))
        def _():
            piece_copy(slot, src, dst, shift, me + shift).wait_send()


def pointwise(
    normed, current, fresh, proj_in, bias_in, grn_gamma, grn_beta, proj_out, bias_out, hand_on
):
    n = lax.axis_size("row")
    sections = lax.axis_size("section")
    cells, channels = normed.shape
    hidden_units = proj_in.shape[1]
    vmem = pl.BlockSpec(memory_space=pltpu.VMEM)
    out_shape = [jax.ShapeDtypeStruct(current.shape, current.dtype)]
    scratch = [
        pltpu.VMEM((cells, hidden_units), jnp.bfloat16),
        pltpu.VMEM((n, 1, hidden_units), jnp.float32),
        pltpu.SemaphoreType.DMA((n,)),
        pltpu.SemaphoreType.DMA((n,)),
    ]
    if hand_on:
        out_shape.append(jax.ShapeDtypeStruct(fresh.shape, fresh.dtype))
        scratch += [pltpu.SemaphoreType.DMA((3,)), pltpu.SemaphoreType.DMA((3,))]
    return pl.pallas_call(
        functools.partial(_pointwise_kernel, n, sections, hand_on),
        out_shape=out_shape,
        in_specs=[vmem] * 9,
        out_specs=[vmem] * len(out_shape),
        scratch_shapes=scratch,
        compiler_params=pltpu.CompilerParams(
            collective_id=1 if hand_on else 0, has_side_effects=True
        ),
        cost_estimate=pl.CostEstimate(
            flops=4 * cells * channels * hidden_units,
            transcendentals=cells * hidden_units,
            bytes_accessed=4 * channels * hidden_units + 8 * cells * channels,
        ),
    )(
        normed,
        current,
        fresh,
        proj_in,
        bias_in.reshape(1, -1),
        grn_gamma.reshape(1, -1),
        grn_beta.reshape(1, -1),
        proj_out,
        bias_out.reshape(1, -1),
    )


def passed_along(x, axis, by):
    count = lax.axis_size(axis)
    pairs = [(i, i + by) for i in range(count) if 0 <= i + by < count]
    return lax.ppermute(x, axis, pairs)


def depthwise(padded, kernel, bias_term):
    channels = padded.shape[-1]
    conv_out = lax.conv_general_dilated(
        padded.astype(jnp.float32),
        kernel.astype(jnp.float32)[:, :, None, :],
        (1, 1),
        "VALID",
        dimension_numbers=("NHWC", "HWIO", "NHWC"),
        feature_group_count=channels,
        precision=lax.Precision.HIGHEST,
    )
    return conv_out + bias_term.astype(jnp.float32)


def conv_block(padded, fresh, params, hand_on):
    (
        depth_kernel,
        depth_bias,
        norm_gain,
        norm_bias,
        proj_in,
        bias_in,
        grn_gamma,
        grn_beta,
        proj_out,
        bias_out,
    ) = params
    current = padded[:, 3:-3]
    num_items, num_rows, num_cols, channels = current.shape
    padded = jnp.pad(padded, ((0, 0), (0, 0), (3, 3), (0, 0)))
    conv_out = depthwise(padded, depth_kernel, depth_bias)
    center = conv_out - jnp.mean(conv_out, axis=-1, keepdims=True)
    spread = jnp.mean(center * center, axis=-1, keepdims=True)
    normed = (
        center * lax.rsqrt(spread + EPS_NORM) * norm_gain.astype(jnp.float32)
        + norm_bias.astype(jnp.float32)
    ).astype(jnp.bfloat16)
    flat_rows = normed.reshape(num_items * num_rows * num_cols, channels)
    results = pointwise(
        flat_rows,
        current.reshape(num_items * num_rows * num_cols, channels),
        fresh.reshape(-1, channels),
        proj_in,
        bias_in,
        grn_gamma,
        grn_beta,
        proj_out,
        bias_out,
        hand_on,
    )
    produced = results[0].reshape(num_items, num_rows, num_cols, channels)
    arriving = results[1].reshape(fresh.shape) if hand_on else None
    return produced, arriving


def on_device(
    inputs,
    depth_kernel,
    depth_bias,
    norm_gain,
    norm_bias,
    proj_in,
    bias_in,
    grn_gamma,
    grn_beta,
    proj_out,
    bias_out,
):
    fresh = extended(inputs[:, 0], (("row", 1),), 3)[:, None]
    proj_in, proj_out = (
        lax.all_gather(proj_in, "dp", axis=2, tiled=True),
        lax.all_gather(proj_out, "dp", axis=1, tiled=True),
    )
    sections = lax.axis_size("section")
    section_index = lax.axis_index("section")
    num_micro = inputs.shape[0]
    own_params = (
        depth_kernel[0],
        depth_bias[0],
        norm_gain[0],
        norm_bias[0],
        proj_in[0],
        bias_in[0],
        grn_gamma[0],
        grn_beta[0],
        proj_out[0],
        bias_out[0],
    )
    num_ticks = num_micro + sections - 1
    current = fresh[0]
    outputs = []
    for tick_index in range(num_ticks):
        hand_on = tick_index + 1 < num_ticks
        produced, current = conv_block(
            current, fresh[min(tick_index + 1, num_micro - 1)], own_params, hand_on
        )
        outputs.append(produced)
    stacked = jnp.stack(outputs)
    saved = lax.dynamic_slice_in_dim(stacked, section_index, num_micro, axis=0)
    return saved[None]


def solution(mesh):
    return jax.shard_map(
        on_device,
        mesh=mesh,
        in_specs=(
            P(None, "dp", "row", None, None),
            P("section", None, None, None),
            P("section", None),
            P("section", None),
            P("section", None),
            P("section", None, "dp"),
            P("section", None),
            P("section", None),
            P("section", None),
            P("section", "dp", None),
            P("section", None),
        ),
        out_specs=P("section", None, "dp", "row", None, None),
        check_vma=False,
    )
```

```python
import functools
import math

import jax
import jax.numpy as jnp
from jax import lax
from jax.experimental import pallas as pl
from jax.experimental.pallas import tpu as pltpu
from jax.sharding import PartitionSpec as P

MESH = pl.DeviceIdType.MESH

EPS_NORM = 1e-06
EPS_GRN = 1e-06


def extended(cells, sides, width):
    for axis, dim in sides:
        count = lax.axis_size(axis)
        ends = count - 1
        head = lax.slice_in_dim(cells, 0, width, axis=dim)
        tail = lax.slice_in_dim(cells, cells.shape[dim] - width, cells.shape[dim], axis=dim)
        cells = jnp.concatenate(
            [
                lax.ppermute(tail, axis, [(i, (i + 1) % count) for i in range(ends)]),
                cells,
                lax.ppermute(head, axis, [((i + 1) % count, i) for i in range(ends)]),
            ],
            axis=dim,
        )
    return cells


def _pointwise_kernel(
    n,
    sections,
    hand_on,
    fresh_index,
    normed_ref,
    current_ref,
    fresh_ref,
    proj_in_ref,
    bias_in_ref,
    gamma_ref,
    beta_ref,
    proj_out_ref,
    bias_out_ref,
    out_ref,
    *rest,
):
    if hand_on:
        next_ref, act_ref, slots, send_sem, recv_sem, hand_send, hand_recv, fresh_sem = rest
    else:
        act_ref, slots, send_sem, recv_sem = rest
    me = lax.axis_index("row")
    section = lax.axis_index("section")
    barrier = pltpu.get_barrier_semaphore()
    for k in range(1, n):
        pl.semaphore_signal(
            barrier, inc=1, device_id={"row": lax.rem(me + k, n)}, device_id_type=MESH
        )
    waits = n - 1
    if hand_on:
        cells = out_ref.shape[0]
        edge = 3 * cells // 4
        has_above = me > 0
        has_below = me < n - 1
        has_prev = section > 0
        has_next = section < sections - 1
        for shift, cond in ((0, True), (-1, has_above), (1, has_below)):
            @pl.when(jnp.logical_and(has_prev, cond))
            def _():
                pl.semaphore_signal(
                    barrier,
                    inc=1,
                    device_id={"section": section - 1, "row": me + shift},
                    device_id_type=MESH,
                )
        waits = waits + jnp.where(
            has_next,
            1 + has_above.astype(jnp.int32) + has_below.astype(jnp.int32),
            0,
        )
    raised = jnp.dot(
        normed_ref[...], proj_in_ref[...], preferred_element_type=jnp.float32
    ) + bias_in_ref[...].astype(jnp.float32)
    active = (0.5 * raised * (1.0 + lax.erf(raised * (1.0 / math.sqrt(2.0))))).astype(
        jnp.bfloat16
    )
    act_ref[...] = active
    grouped = active.astype(jnp.float32)
    slots[me] = jnp.sum(grouped * grouped, axis=0, keepdims=True)
    pl.semaphore_wait(barrier, waits)
    sends = []
    for k in range(1, n):
        copy = pltpu.make_async_remote_copy(
            src_ref=slots.at[me],
            dst_ref=slots.at[me],
            send_sem=send_sem.at[k],
            recv_sem=recv_sem.at[me],
            device_id={"row": lax.rem(me + k, n)},
            device_id_type=MESH,
        )
        copy.start()
        sends.append(copy)
    if hand_on:
        @pl.when(section == 0)
        def _():
            fresh_copy = pltpu.make_async_copy(fresh_ref.at[fresh_index], next_ref, fresh_sem)
            fresh_copy.start()
            fresh_copy.wait()

        @pl.when(jnp.logical_and(has_prev, jnp.logical_not(has_above)))
        def _():
            next_ref[pl.ds(0, edge), :] = jnp.zeros((edge, next_ref.shape[1]), next_ref.dtype)

        @pl.when(jnp.logical_and(has_prev, jnp.logical_not(has_below)))
        def _():
            next_ref[pl.ds(edge + cells, edge), :] = jnp.zeros(
                (edge, next_ref.shape[1]), next_ref.dtype
            )

    for k in range(1, n):
        src = lax.rem(me + k, n)
        pltpu.make_async_remote_copy(
            src_ref=slots.at[src],
            dst_ref=slots.at[src],
            send_sem=send_sem.at[k],
            recv_sem=recv_sem.at[src],
            device_id={"row": src},
            device_id_type=MESH,
        ).wait_recv()
    for copy in sends:
        copy.wait_send()
    total_sq = slots[0]
    for j in range(1, n):
        total_sq = total_sq + slots[j]
    magnitude = jnp.sqrt(total_sq)
    grn_ratio = magnitude / (jnp.mean(magnitude, axis=-1, keepdims=True) + EPS_GRN)
    grouped = act_ref[...].astype(jnp.float32)
    hidden = (
        gamma_ref[...].astype(jnp.float32) * grouped * grn_ratio
        + beta_ref[...].astype(jnp.float32)
        + grouped
    ).astype(jnp.bfloat16)
    update = jnp.dot(
        hidden, proj_out_ref[...], preferred_element_type=jnp.float32
    ) + bias_out_ref[...].astype(jnp.float32)
    out_ref[...] = (current_ref[...].astype(jnp.float32) + update).astype(out_ref.dtype)
    if not hand_on:
        return
    pieces = (
        (1, out_ref, pl.ds(edge, cells), 0, True),
        (2, out_ref.at[pl.ds(0, edge)], pl.ds(edge + cells, edge), -1, has_above),
        (0, out_ref.at[pl.ds(cells - edge, edge)], pl.ds(0, edge), 1, has_below),
    )

    def piece_copy(slot, src, dst, shift, peer_row):
        return pltpu.make_async_remote_copy(
            src_ref=src,
            dst_ref=next_ref.at[dst],
            send_sem=hand_send.at[slot],
            recv_sem=hand_recv.at[slot],
            device_id={"section": section + 1, "row": peer_row},
            device_id_type=MESH,
        )

    for slot, src, dst, shift, cond in pieces:
        @pl.when(jnp.logical_and(has_next, cond))
        def _():
            piece_copy(slot, src, dst, shift, me + shift).start()

    arrivals = {0: has_above, 1: True, 2: has_below}
    for slot, src, dst, shift, cond in pieces:
        @pl.when(jnp.logical_and(has_prev, arrivals[slot]))
        def _():
            piece_copy(slot, src, dst, shift, me).wait_recv()

    for slot, src, dst, shift, cond in pieces:
        @pl.when(jnp.logical_and(has_next, cond))
        def _():
            piece_copy(slot, src, dst, shift, me + shift).wait_send()


def pointwise(
    normed,
    current,
    fresh,
    fresh_index,
    proj_in,
    bias_in,
    grn_gamma,
    grn_beta,
    proj_out,
    bias_out,
    hand_on,
):
    n = lax.axis_size("row")
    sections = lax.axis_size("section")
    cells, channels = normed.shape
    hidden_units = proj_in.shape[1]
    vmem = pl.BlockSpec(memory_space=pltpu.VMEM)
    out_shape = [jax.ShapeDtypeStruct(current.shape, current.dtype)]
    scratch = [
        pltpu.VMEM((cells, hidden_units), jnp.bfloat16),
        pltpu.VMEM((n, 1, hidden_units), jnp.float32),
        pltpu.SemaphoreType.DMA((n,)),
        pltpu.SemaphoreType.DMA((n,)),
    ]
    if hand_on:
        out_shape.append(jax.ShapeDtypeStruct(fresh.shape[1:], fresh.dtype))
        scratch += [
            pltpu.SemaphoreType.DMA((3,)),
            pltpu.SemaphoreType.DMA((3,)),
            pltpu.SemaphoreType.DMA(()),
        ]
    return pl.pallas_call(
        functools.partial(_pointwise_kernel, n, sections, hand_on, fresh_index),
        out_shape=out_shape,
        in_specs=[vmem, vmem, pl.BlockSpec(memory_space=pl.ANY)] + [vmem] * 6,
        out_specs=[vmem] * len(out_shape),
        scratch_shapes=scratch,
        compiler_params=pltpu.CompilerParams(
            collective_id=1 + fresh_index if hand_on else 0, has_side_effects=True
        ),
        cost_estimate=pl.CostEstimate(
            flops=4 * cells * channels * hidden_units,
            transcendentals=cells * hidden_units,
            bytes_accessed=4 * channels * hidden_units + 8 * cells * channels,
        ),
    )(
        normed,
        current,
        fresh,
        proj_in,
        bias_in.reshape(1, -1),
        grn_gamma.reshape(1, -1),
        grn_beta.reshape(1, -1),
        proj_out,
        bias_out.reshape(1, -1),
    )


def passed_along(x, axis, by):
    count = lax.axis_size(axis)
    pairs = [(i, i + by) for i in range(count) if 0 <= i + by < count]
    return lax.ppermute(x, axis, pairs)


def depthwise(padded, kernel, bias_term):
    channels = padded.shape[-1]
    conv_out = lax.conv_general_dilated(
        padded.astype(jnp.float32),
        kernel.astype(jnp.float32)[:, :, None, :],
        (1, 1),
        "VALID",
        dimension_numbers=("NHWC", "HWIO", "NHWC"),
        feature_group_count=channels,
        precision=lax.Precision.HIGHEST,
    )
    return conv_out + bias_term.astype(jnp.float32)


def conv_block(padded, fresh, fresh_index, params, hand_on):
    (
        depth_kernel,
        depth_bias,
        norm_gain,
        norm_bias,
        proj_in,
        bias_in,
        grn_gamma,
        grn_beta,
        proj_out,
        bias_out,
    ) = params
    current = padded[:, 3:-3]
    num_items, num_rows, num_cols, channels = current.shape
    padded = jnp.pad(padded, ((0, 0), (0, 0), (3, 3), (0, 0)))
    conv_out = depthwise(padded, depth_kernel, depth_bias)
    center = conv_out - jnp.mean(conv_out, axis=-1, keepdims=True)
    spread = jnp.mean(center * center, axis=-1, keepdims=True)
    normed = (
        center * lax.rsqrt(spread + EPS_NORM) * norm_gain.astype(jnp.float32)
        + norm_bias.astype(jnp.float32)
    ).astype(jnp.bfloat16)
    flat_rows = normed.reshape(num_items * num_rows * num_cols, channels)
    results = pointwise(
        flat_rows,
        current.reshape(num_items * num_rows * num_cols, channels),
        fresh.reshape(fresh.shape[0], -1, channels),
        fresh_index,
        proj_in,
        bias_in,
        grn_gamma,
        grn_beta,
        proj_out,
        bias_out,
        hand_on,
    )
    produced = results[0].reshape(num_items, num_rows, num_cols, channels)
    arriving = results[1].reshape(padded.shape[0], -1, num_cols, channels) if hand_on else None
    return produced, arriving


def gathered_weights(proj_in, proj_out):
    rows = lax.axis_size("row")
    shards = lax.axis_size("dp")
    channels, part = proj_in.shape
    first_core = lax.rem(lax.axis_index("row"), 2) == 0
    mine = jnp.where(first_core, proj_in.reshape(-1), proj_out.reshape(-1))
    held = lax.all_gather(mine, "dp")
    other = lax.ppermute(held, "row", [(r, r ^ 1) for r in range(rows)])
    gathered_in = jnp.where(first_core, held, other)
    gathered_out = jnp.where(first_core, other, held)
    full_in = gathered_in.reshape(shards, channels, part).transpose(1, 0, 2)
    return full_in.reshape(channels, shards * part), gathered_out.reshape(shards * part, channels)


def on_device(
    inputs,
    depth_kernel,
    depth_bias,
    norm_gain,
    norm_bias,
    proj_in,
    bias_in,
    grn_gamma,
    grn_beta,
    proj_out,
    bias_out,
):
    fresh = extended(inputs[:, 0], (("row", 1),), 3)
    proj_in, proj_out = gathered_weights(proj_in[0], proj_out[0])
    sections = lax.axis_size("section")
    section_index = lax.axis_index("section")
    num_micro = inputs.shape[0]
    own_params = (
        depth_kernel[0],
        depth_bias[0],
        norm_gain[0],
        norm_bias[0],
        proj_in,
        bias_in[0],
        grn_gamma[0],
        grn_beta[0],
        proj_out,
        bias_out[0],
    )
    num_ticks = num_micro + sections - 1
    current = fresh[:1]
    outputs = []
    for tick_index in range(num_ticks):
        hand_on = tick_index + 1 < num_ticks
        produced, current = conv_block(
            current, fresh, min(tick_index + 1, num_micro - 1), own_params, hand_on
        )
        outputs.append(produced)
    stacked = jnp.stack(outputs)
    saved = lax.dynamic_slice_in_dim(stacked, section_index, num_micro, axis=0)
    return saved[None]


def solution(mesh):
    return jax.shard_map(
        on_device,
        mesh=mesh,
        in_specs=(
            P(None, "dp", "row", None, None),
            P("section", None, None, None),
            P("section", None),
            P("section", None),
            P("section", None),
            P("section", None, "dp"),
            P("section", None),
            P("section", None),
            P("section", None),
            P("section", "dp", None),
            P("section", None),
        ),
        out_specs=P("section", None, "dp", "row", None, None),
        check_vma=False,
    )
```

```python
import functools
import math

import jax
import jax.numpy as jnp
from jax import lax
from jax.experimental import pallas as pl
from jax.experimental.pallas import tpu as pltpu
from jax.sharding import PartitionSpec as P

MESH = pl.DeviceIdType.MESH

EPS_NORM = 1e-06
EPS_GRN = 1e-06


def extended(cells, sides, width):
    for axis, dim in sides:
        count = lax.axis_size(axis)
        ends = count - 1
        head = lax.slice_in_dim(cells, 0, width, axis=dim)
        tail = lax.slice_in_dim(cells, cells.shape[dim] - width, cells.shape[dim], axis=dim)
        cells = jnp.concatenate(
            [
                lax.ppermute(tail, axis, [(i, (i + 1) % count) for i in range(ends)]),
                cells,
                lax.ppermute(head, axis, [((i + 1) % count, i) for i in range(ends)]),
            ],
            axis=dim,
        )
    return cells


def _pointwise_kernel(
    n,
    sections,
    hand_on,
    fresh_index,
    normed_ref,
    padded_ref,
    fresh_ref,
    held_ref,
    other_ref,
    bias_in_ref,
    gamma_ref,
    beta_ref,
    bias_out_ref,
    out_ref,
    *rest,
):
    if hand_on:
        next_ref, act_ref, slots, send_sem, recv_sem, hand_send, hand_recv, fresh_sem = rest
    else:
        act_ref, slots, send_sem, recv_sem = rest
    me = lax.axis_index("row")
    section = lax.axis_index("section")
    barrier = pltpu.get_barrier_semaphore()
    for k in range(1, n):
        pl.semaphore_signal(
            barrier, inc=1, device_id={"row": lax.rem(me + k, n)}, device_id_type=MESH
        )
    waits = n - 1
    if hand_on:
        cells = out_ref.shape[0]
        edge = 3 * cells // 4
        has_above = me > 0
        has_below = me < n - 1
        has_prev = section > 0
        has_next = section < sections - 1
        for shift, cond in ((0, True), (-1, has_above), (1, has_below)):
            @pl.when(jnp.logical_and(has_prev, cond))
            def _():
                pl.semaphore_signal(
                    barrier,
                    inc=1,
                    device_id={"section": section - 1, "row": me + shift},
                    device_id_type=MESH,
                )
        waits = waits + jnp.where(
            has_next,
            1 + has_above.astype(jnp.int32) + has_below.astype(jnp.int32),
            0,
        )
    first_core = lax.rem(me, 2) == 0

    def raise_with(proj_in_ref):
        raised = jnp.dot(
            normed_ref[...], proj_in_ref[...], preferred_element_type=jnp.float32
        ) + bias_in_ref[...].astype(jnp.float32)
        act_ref[...] = (0.5 * raised * (1.0 + lax.erf(raised * (1.0 / math.sqrt(2.0))))).astype(
            jnp.bfloat16
        )

    pl.when(first_core)(lambda: raise_with(held_ref))
    pl.when(jnp.logical_not(first_core))(lambda: raise_with(other_ref))
    grouped = act_ref[...].astype(jnp.float32)
    slots[me] = jnp.sum(grouped * grouped, axis=0, keepdims=True)
    pl.semaphore_wait(barrier, waits)
    sends = []
    for k in range(1, n):
        copy = pltpu.make_async_remote_copy(
            src_ref=slots.at[me],
            dst_ref=slots.at[me],
            send_sem=send_sem.at[k],
            recv_sem=recv_sem.at[me],
            device_id={"row": lax.rem(me + k, n)},
            device_id_type=MESH,
        )
        copy.start()
        sends.append(copy)
    if hand_on:
        @pl.when(section == 0)
        def _():
            fresh_copy = pltpu.make_async_copy(fresh_ref.at[fresh_index], next_ref, fresh_sem)
            fresh_copy.start()
            fresh_copy.wait()

        @pl.when(jnp.logical_and(has_prev, jnp.logical_not(has_above)))
        def _():
            next_ref[pl.ds(0, edge), :] = jnp.zeros((edge, next_ref.shape[1]), next_ref.dtype)

        @pl.when(jnp.logical_and(has_prev, jnp.logical_not(has_below)))
        def _():
            next_ref[pl.ds(edge + cells, edge), :] = jnp.zeros(
                (edge, next_ref.shape[1]), next_ref.dtype
            )

    for k in range(1, n):
        src = lax.rem(me + k, n)
        pltpu.make_async_remote_copy(
            src_ref=slots.at[src],
            dst_ref=slots.at[src],
            send_sem=send_sem.at[k],
            recv_sem=recv_sem.at[src],
            device_id={"row": src},
            device_id_type=MESH,
        ).wait_recv()
    for copy in sends:
        copy.wait_send()
    total_sq = slots[0]
    for j in range(1, n):
        total_sq = total_sq + slots[j]
    magnitude = jnp.sqrt(total_sq)
    grn_ratio = magnitude / (jnp.mean(magnitude, axis=-1, keepdims=True) + EPS_GRN)
    grouped = act_ref[...].astype(jnp.float32)
    hidden = (
        gamma_ref[...].astype(jnp.float32) * grouped * grn_ratio
        + beta_ref[...].astype(jnp.float32)
        + grouped
    ).astype(jnp.bfloat16)
    cells = out_ref.shape[0]
    edge = 3 * cells // 4

    def lower_with(proj_out_t_ref):
        update = lax.dot_general(
            hidden,
            proj_out_t_ref[...],
            (((1,), (1,)), ((), ())),
            preferred_element_type=jnp.float32,
        ) + bias_out_ref[...].astype(jnp.float32)
        current = padded_ref[pl.ds(edge, cells), :].astype(jnp.float32)
        out_ref[...] = (current + update).astype(out_ref.dtype)

    pl.when(first_core)(lambda: lower_with(other_ref))
    pl.when(jnp.logical_not(first_core))(lambda: lower_with(held_ref))
    if not hand_on:
        return
    pieces = (
        (1, out_ref, pl.ds(edge, cells), 0, True),
        (2, out_ref.at[pl.ds(0, edge)], pl.ds(edge + cells, edge), -1, has_above),
        (0, out_ref.at[pl.ds(cells - edge, edge)], pl.ds(0, edge), 1, has_below),
    )

    def piece_copy(slot, src, dst, shift, peer_row):
        return pltpu.make_async_remote_copy(
            src_ref=src,
            dst_ref=next_ref.at[dst],
            send_sem=hand_send.at[slot],
            recv_sem=hand_recv.at[slot],
            device_id={"section": section + 1, "row": peer_row},
            device_id_type=MESH,
        )

    for slot, src, dst, shift, cond in pieces:
        @pl.when(jnp.logical_and(has_next, cond))
        def _():
            piece_copy(slot, src, dst, shift, me + shift).start()

    arrivals = {0: has_above, 1: True, 2: has_below}
    for slot, src, dst, shift, cond in pieces:
        @pl.when(jnp.logical_and(has_prev, arrivals[slot]))
        def _():
            piece_copy(slot, src, dst, shift, me).wait_recv()

    for slot, src, dst, shift, cond in pieces:
        @pl.when(jnp.logical_and(has_next, cond))
        def _():
            piece_copy(slot, src, dst, shift, me + shift).wait_send()


def pointwise(
    normed,
    padded,
    fresh,
    fresh_index,
    held,
    other,
    bias_in,
    grn_gamma,
    grn_beta,
    bias_out,
    hand_on,
):
    n = lax.axis_size("row")
    sections = lax.axis_size("section")
    cells, channels = normed.shape
    hidden_units = held.shape[1]
    vmem = pl.BlockSpec(memory_space=pltpu.VMEM)
    out_shape = [jax.ShapeDtypeStruct((cells, channels), padded.dtype)]
    scratch = [
        pltpu.VMEM((cells, hidden_units), jnp.bfloat16),
        pltpu.VMEM((n, 1, hidden_units), jnp.float32),
        pltpu.SemaphoreType.DMA((n,)),
        pltpu.SemaphoreType.DMA((n,)),
    ]
    if hand_on:
        out_shape.append(jax.ShapeDtypeStruct(fresh.shape[1:], fresh.dtype))
        scratch += [
            pltpu.SemaphoreType.DMA((3,)),
            pltpu.SemaphoreType.DMA((3,)),
            pltpu.SemaphoreType.DMA(()),
        ]
    return pl.pallas_call(
        functools.partial(_pointwise_kernel, n, sections, hand_on, fresh_index),
        out_shape=out_shape,
        in_specs=[vmem, vmem, pl.BlockSpec(memory_space=pl.ANY)] + [vmem] * 6,
        out_specs=[vmem] * len(out_shape),
        scratch_shapes=scratch,
        compiler_params=pltpu.CompilerParams(
            collective_id=1 + fresh_index if hand_on else 0, has_side_effects=True
        ),
        cost_estimate=pl.CostEstimate(
            flops=4 * cells * channels * hidden_units,
            transcendentals=cells * hidden_units,
            bytes_accessed=4 * channels * hidden_units + 8 * cells * channels,
        ),
    )(
        normed,
        padded,
        fresh,
        held,
        other,
        bias_in.reshape(1, -1),
        grn_gamma.reshape(1, -1),
        grn_beta.reshape(1, -1),
        bias_out.reshape(1, -1),
    )


def passed_along(x, axis, by):
    count = lax.axis_size(axis)
    pairs = [(i, i + by) for i in range(count) if 0 <= i + by < count]
    return lax.ppermute(x, axis, pairs)


def depthwise(padded, kernel, bias_term):
    channels = padded.shape[-1]
    conv_out = lax.conv_general_dilated(
        padded.astype(jnp.float32),
        kernel.astype(jnp.float32)[:, :, None, :],
        (1, 1),
        "VALID",
        dimension_numbers=("NHWC", "HWIO", "NHWC"),
        feature_group_count=channels,
        precision=lax.Precision.HIGHEST,
    )
    return conv_out + bias_term.astype(jnp.float32)


def conv_block(padded, fresh, fresh_index, params, hand_on):
    (
        depth_kernel,
        depth_bias,
        norm_gain,
        norm_bias,
        proj_in,
        bias_in,
        grn_gamma,
        grn_beta,
        proj_out,
        bias_out,
    ) = params
    rows_in = padded
    num_items, num_rows, num_cols, channels = padded[:, 3:-3].shape
    padded = jnp.pad(padded, ((0, 0), (0, 0), (3, 3), (0, 0)))
    conv_out = depthwise(padded, depth_kernel, depth_bias)
    center = conv_out - jnp.mean(conv_out, axis=-1, keepdims=True)
    spread = jnp.mean(center * center, axis=-1, keepdims=True)
    normed = (
        center * lax.rsqrt(spread + EPS_NORM) * norm_gain.astype(jnp.float32)
        + norm_bias.astype(jnp.float32)
    ).astype(jnp.bfloat16)
    flat_rows = normed.reshape(num_items * num_rows * num_cols, channels)
    results = pointwise(
        flat_rows,
        rows_in.reshape(-1, channels),
        fresh.reshape(fresh.shape[0], -1, channels),
        fresh_index,
        proj_in,
        proj_out,
        bias_in,
        grn_gamma,
        grn_beta,
        bias_out,
        hand_on,
    )
    produced = results[0].reshape(num_items, num_rows, num_cols, channels)
    arriving = results[1].reshape(padded.shape[0], -1, num_cols, channels) if hand_on else None
    return produced, arriving


def gathered_weights(proj_in, proj_out):
    rows = lax.axis_size("row")
    first_core = lax.rem(lax.axis_index("row"), 2) == 0
    mine = jnp.where(first_core, proj_in, proj_out.T)
    held = lax.all_gather(mine, "dp", axis=1, tiled=True)
    other = lax.ppermute(held, "row", [(r, r ^ 1) for r in range(rows)])
    return held, other


def on_device(
    inputs,
    depth_kernel,
    depth_bias,
    norm_gain,
    norm_bias,
    proj_in,
    bias_in,
    grn_gamma,
    grn_beta,
    proj_out,
    bias_out,
):
    fresh = extended(inputs[:, 0], (("row", 1),), 3)
    proj_in, proj_out = gathered_weights(proj_in[0], proj_out[0])
    sections = lax.axis_size("section")
    section_index = lax.axis_index("section")
    num_micro = inputs.shape[0]
    own_params = (
        depth_kernel[0],
        depth_bias[0],
        norm_gain[0],
        norm_bias[0],
        proj_in,
        bias_in[0],
        grn_gamma[0],
        grn_beta[0],
        proj_out,
        bias_out[0],
    )
    num_ticks = num_micro + sections - 1
    current = fresh[:1]
    outputs = []
    for tick_index in range(num_ticks):
        hand_on = tick_index + 1 < num_ticks
        produced, current = conv_block(
            current, fresh, min(tick_index + 1, num_micro - 1), own_params, hand_on
        )
        outputs.append(produced)
    stacked = jnp.stack(outputs)
    saved = lax.dynamic_slice_in_dim(stacked, section_index, num_micro, axis=0)
    return saved[None]


def solution(mesh):
    return jax.shard_map(
        on_device,
        mesh=mesh,
        in_specs=(
            P(None, "dp", "row", None, None),
            P("section", None, None, None),
            P("section", None),
            P("section", None),
            P("section", None),
            P("section", None, "dp"),
            P("section", None),
            P("section", None),
            P("section", None),
            P("section", "dp", None),
            P("section", None),
        ),
        out_specs=P("section", None, "dp", "row", None, None),
        check_vma=False,
    )
```

```python
import functools
import math

import jax
import jax.numpy as jnp
from jax import lax
from jax.experimental import pallas as pl
from jax.experimental.pallas import tpu as pltpu
from jax.sharding import PartitionSpec as P

MESH = pl.DeviceIdType.MESH

EPS_NORM = 1e-06
EPS_GRN = 1e-06


def extended(cells, sides, width):
    for axis, dim in sides:
        count = lax.axis_size(axis)
        ends = count - 1
        head = lax.slice_in_dim(cells, 0, width, axis=dim)
        tail = lax.slice_in_dim(cells, cells.shape[dim] - width, cells.shape[dim], axis=dim)
        cells = jnp.concatenate(
            [
                lax.ppermute(tail, axis, [(i, (i + 1) % count) for i in range(ends)]),
                cells,
                lax.ppermute(head, axis, [((i + 1) % count, i) for i in range(ends)]),
            ],
            axis=dim,
        )
    return cells


def _pointwise_kernel(
    n,
    sections,
    hand_on,
    fresh_index,
    normed_ref,
    padded_ref,
    fresh_ref,
    held_ref,
    other_ref,
    bias_in_ref,
    gamma_ref,
    beta_ref,
    bias_out_ref,
    out_ref,
    *rest,
):
    if hand_on:
        next_ref, act_ref, slots, send_sem, recv_sem, hand_send, hand_recv, fresh_sem = rest
    else:
        act_ref, slots, send_sem, recv_sem = rest
    me = lax.axis_index("row")
    section = lax.axis_index("section")
    barrier = pltpu.get_barrier_semaphore()
    for k in range(1, n):
        pl.semaphore_signal(
            barrier, inc=1, device_id={"row": lax.rem(me + k, n)}, device_id_type=MESH
        )
    waits = n - 1
    if hand_on:
        cells = out_ref.shape[0]
        edge = 3 * cells // 4
        has_above = me > 0
        has_below = me < n - 1
        has_prev = section > 0
        has_next = section < sections - 1
        @pl.when(has_prev)
        def _():
            pl.semaphore_signal(
                barrier, inc=1, device_id={"section": section - 1}, device_id_type=MESH
            )

        waits = waits + has_next.astype(jnp.int32)
    first_core = lax.rem(me, 2) == 0

    def raise_with(proj_in_ref):
        raised = jnp.dot(
            normed_ref[...], proj_in_ref[...], preferred_element_type=jnp.float32
        ) + bias_in_ref[...].astype(jnp.float32)
        act_ref[...] = (0.5 * raised * (1.0 + lax.erf(raised * (1.0 / math.sqrt(2.0))))).astype(
            jnp.bfloat16
        )

    pl.when(first_core)(lambda: raise_with(held_ref))
    pl.when(jnp.logical_not(first_core))(lambda: raise_with(other_ref))
    grouped = act_ref[...].astype(jnp.float32)
    slots[me] = jnp.sum(grouped * grouped, axis=0, keepdims=True)
    pl.semaphore_wait(barrier, waits)
    sends = []
    for k in range(1, n):
        copy = pltpu.make_async_remote_copy(
            src_ref=slots.at[me],
            dst_ref=slots.at[me],
            send_sem=send_sem.at[k],
            recv_sem=recv_sem.at[me],
            device_id={"row": lax.rem(me + k, n)},
            device_id_type=MESH,
        )
        copy.start()
        sends.append(copy)
    if hand_on:
        @pl.when(section == 0)
        def _():
            fresh_copy = pltpu.make_async_copy(fresh_ref.at[fresh_index], next_ref, fresh_sem)
            fresh_copy.start()
            fresh_copy.wait()

        @pl.when(jnp.logical_and(has_prev, jnp.logical_not(has_above)))
        def _():
            next_ref[pl.ds(0, edge), :] = jnp.zeros((edge, next_ref.shape[1]), next_ref.dtype)

        @pl.when(jnp.logical_and(has_prev, jnp.logical_not(has_below)))
        def _():
            next_ref[pl.ds(edge + cells, edge), :] = jnp.zeros(
                (edge, next_ref.shape[1]), next_ref.dtype
            )

    for k in range(1, n):
        src = lax.rem(me + k, n)
        pltpu.make_async_remote_copy(
            src_ref=slots.at[src],
            dst_ref=slots.at[src],
            send_sem=send_sem.at[k],
            recv_sem=recv_sem.at[src],
            device_id={"row": src},
            device_id_type=MESH,
        ).wait_recv()
    for copy in sends:
        copy.wait_send()
    total_sq = slots[0]
    for j in range(1, n):
        total_sq = total_sq + slots[j]
    magnitude = jnp.sqrt(total_sq)
    grn_ratio = magnitude / (jnp.mean(magnitude, axis=-1, keepdims=True) + EPS_GRN)
    grouped = act_ref[...].astype(jnp.float32)
    hidden = (
        gamma_ref[...].astype(jnp.float32) * grouped * grn_ratio
        + beta_ref[...].astype(jnp.float32)
        + grouped
    ).astype(jnp.bfloat16)
    cells = out_ref.shape[0]
    edge = 3 * cells // 4

    def lower_with(proj_out_t_ref):
        update = lax.dot_general(
            hidden,
            proj_out_t_ref[...],
            (((1,), (1,)), ((), ())),
            preferred_element_type=jnp.float32,
        ) + bias_out_ref[...].astype(jnp.float32)
        current = padded_ref[pl.ds(edge, cells), :].astype(jnp.float32)
        out_ref[...] = (current + update).astype(out_ref.dtype)

    pl.when(first_core)(lambda: lower_with(other_ref))
    pl.when(jnp.logical_not(first_core))(lambda: lower_with(held_ref))
    if not hand_on:
        return
    own_rows = pl.ds(edge, cells)
    handed = pltpu.make_async_remote_copy(
        src_ref=out_ref,
        dst_ref=next_ref.at[own_rows],
        send_sem=hand_send.at[1],
        recv_sem=hand_recv.at[1],
        device_id={"section": section + 1},
        device_id_type=MESH,
    )

    @pl.when(has_next)
    def _():
        handed.start()

    halos = (
        (2, pl.ds(edge, edge), pl.ds(edge + cells, edge), -1, has_above),
        (0, pl.ds(cells, edge), pl.ds(0, edge), 1, has_below),
    )

    def halo_copy(slot, src, dst, peer_row):
        return pltpu.make_async_remote_copy(
            src_ref=next_ref.at[src],
            dst_ref=next_ref.at[dst],
            send_sem=hand_send.at[slot],
            recv_sem=hand_recv.at[slot],
            device_id={"row": peer_row},
            device_id_type=MESH,
        )

    @pl.when(has_prev)
    def _():
        handed.wait_recv()
        for slot, src, dst, shift, cond in halos:
            @pl.when(cond)
            def _():
                halo_copy(slot, src, dst, me + shift).start()

        for slot, src, dst, shift, cond in halos:
            @pl.when(halos[slot // 2][4])
            def _():
                halo_copy(slot, src, dst, me).wait_recv()

        for slot, src, dst, shift, cond in halos:
            @pl.when(cond)
            def _():
                halo_copy(slot, src, dst, me + shift).wait_send()

    @pl.when(has_next)
    def _():
        handed.wait_send()


def pointwise(
    normed,
    padded,
    fresh,
    fresh_index,
    held,
    other,
    bias_in,
    grn_gamma,
    grn_beta,
    bias_out,
    hand_on,
):
    n = lax.axis_size("row")
    sections = lax.axis_size("section")
    cells, channels = normed.shape
    hidden_units = held.shape[1]
    vmem = pl.BlockSpec(memory_space=pltpu.VMEM)
    out_shape = [jax.ShapeDtypeStruct((cells, channels), padded.dtype)]
    scratch = [
        pltpu.VMEM((cells, hidden_units), jnp.bfloat16),
        pltpu.VMEM((n, 1, hidden_units), jnp.float32),
        pltpu.SemaphoreType.DMA((n,)),
        pltpu.SemaphoreType.DMA((n,)),
    ]
    if hand_on:
        out_shape.append(jax.ShapeDtypeStruct(fresh.shape[1:], fresh.dtype))
        scratch += [
            pltpu.SemaphoreType.DMA((3,)),
            pltpu.SemaphoreType.DMA((3,)),
            pltpu.SemaphoreType.DMA(()),
        ]
    return pl.pallas_call(
        functools.partial(_pointwise_kernel, n, sections, hand_on, fresh_index),
        out_shape=out_shape,
        in_specs=[vmem, vmem, pl.BlockSpec(memory_space=pl.ANY)] + [vmem] * 6,
        out_specs=[vmem] * len(out_shape),
        scratch_shapes=scratch,
        compiler_params=pltpu.CompilerParams(
            collective_id=1 + fresh_index if hand_on else 0, has_side_effects=True
        ),
        cost_estimate=pl.CostEstimate(
            flops=4 * cells * channels * hidden_units,
            transcendentals=cells * hidden_units,
            bytes_accessed=4 * channels * hidden_units + 8 * cells * channels,
        ),
    )(
        normed,
        padded,
        fresh,
        held,
        other,
        bias_in.reshape(1, -1),
        grn_gamma.reshape(1, -1),
        grn_beta.reshape(1, -1),
        bias_out.reshape(1, -1),
    )


def passed_along(x, axis, by):
    count = lax.axis_size(axis)
    pairs = [(i, i + by) for i in range(count) if 0 <= i + by < count]
    return lax.ppermute(x, axis, pairs)


def depthwise(padded, kernel, bias_term):
    channels = padded.shape[-1]
    conv_out = lax.conv_general_dilated(
        padded.astype(jnp.float32),
        kernel.astype(jnp.float32)[:, :, None, :],
        (1, 1),
        "VALID",
        dimension_numbers=("NHWC", "HWIO", "NHWC"),
        feature_group_count=channels,
        precision=lax.Precision.HIGHEST,
    )
    return conv_out + bias_term.astype(jnp.float32)


def conv_block(padded, fresh, fresh_index, params, hand_on):
    (
        depth_kernel,
        depth_bias,
        norm_gain,
        norm_bias,
        proj_in,
        bias_in,
        grn_gamma,
        grn_beta,
        proj_out,
        bias_out,
    ) = params
    rows_in = padded
    num_items, num_rows, num_cols, channels = padded[:, 3:-3].shape
    padded = jnp.pad(padded, ((0, 0), (0, 0), (3, 3), (0, 0)))
    conv_out = depthwise(padded, depth_kernel, depth_bias)
    center = conv_out - jnp.mean(conv_out, axis=-1, keepdims=True)
    spread = jnp.mean(center * center, axis=-1, keepdims=True)
    normed = (
        center * lax.rsqrt(spread + EPS_NORM) * norm_gain.astype(jnp.float32)
        + norm_bias.astype(jnp.float32)
    ).astype(jnp.bfloat16)
    flat_rows = normed.reshape(num_items * num_rows * num_cols, channels)
    results = pointwise(
        flat_rows,
        rows_in.reshape(-1, channels),
        fresh.reshape(fresh.shape[0], -1, channels),
        fresh_index,
        proj_in,
        proj_out,
        bias_in,
        grn_gamma,
        grn_beta,
        bias_out,
        hand_on,
    )
    produced = results[0].reshape(num_items, num_rows, num_cols, channels)
    arriving = results[1].reshape(padded.shape[0], -1, num_cols, channels) if hand_on else None
    return produced, arriving


def gathered_weights(proj_in, proj_out):
    rows = lax.axis_size("row")
    first_core = lax.rem(lax.axis_index("row"), 2) == 0
    mine = jnp.where(first_core, proj_in, proj_out.T)
    held = lax.all_gather(mine, "dp", axis=1, tiled=True)
    other = lax.ppermute(held, "row", [(r, r ^ 1) for r in range(rows)])
    return held, other


def on_device(
    inputs,
    depth_kernel,
    depth_bias,
    norm_gain,
    norm_bias,
    proj_in,
    bias_in,
    grn_gamma,
    grn_beta,
    proj_out,
    bias_out,
):
    fresh = extended(inputs[:, 0], (("row", 1),), 3)
    proj_in, proj_out = gathered_weights(proj_in[0], proj_out[0])
    sections = lax.axis_size("section")
    section_index = lax.axis_index("section")
    num_micro = inputs.shape[0]
    own_params = (
        depth_kernel[0],
        depth_bias[0],
        norm_gain[0],
        norm_bias[0],
        proj_in,
        bias_in[0],
        grn_gamma[0],
        grn_beta[0],
        proj_out,
        bias_out[0],
    )
    num_ticks = num_micro + sections - 1
    current = fresh[:1]
    outputs = []
    for tick_index in range(num_ticks):
        hand_on = tick_index + 1 < num_ticks
        produced, current = conv_block(
            current, fresh, min(tick_index + 1, num_micro - 1), own_params, hand_on
        )
        outputs.append(produced)
    stacked = jnp.stack(outputs)
    saved = lax.dynamic_slice_in_dim(stacked, section_index, num_micro, axis=0)
    return saved[None]


def solution(mesh):
    return jax.shard_map(
        on_device,
        mesh=mesh,
        in_specs=(
            P(None, "dp", "row", None, None),
            P("section", None, None, None),
            P("section", None),
            P("section", None),
            P("section", None),
            P("section", None, "dp"),
            P("section", None),
            P("section", None),
            P("section", None),
            P("section", "dp", None),
            P("section", None),
        ),
        out_specs=P("section", None, "dp", "row", None, None),
        check_vma=False,
    )
```

```python
import functools
import math

import jax
import jax.numpy as jnp
from jax import lax
from jax.experimental import pallas as pl
from jax.experimental.pallas import tpu as pltpu
from jax.sharding import PartitionSpec as P

MESH = pl.DeviceIdType.MESH

EPS_NORM = 1e-06
EPS_GRN = 1e-06


def extended(cells, sides, width):
    for axis, dim in sides:
        count = lax.axis_size(axis)
        ends = count - 1
        head = lax.slice_in_dim(cells, 0, width, axis=dim)
        tail = lax.slice_in_dim(cells, cells.shape[dim] - width, cells.shape[dim], axis=dim)
        cells = jnp.concatenate(
            [
                lax.ppermute(tail, axis, [(i, (i + 1) % count) for i in range(ends)]),
                cells,
                lax.ppermute(head, axis, [((i + 1) % count, i) for i in range(ends)]),
            ],
            axis=dim,
        )
    return cells


def _pointwise_kernel(
    n,
    sections,
    hand_on,
    fresh_index,
    padded_ref,
    fresh_ref,
    held_ref,
    other_ref,
    bias_in_ref,
    gamma_ref,
    beta_ref,
    bias_out_ref,
    taps_ref,
    depth_bias_ref,
    gain_ref,
    shift_ref,
    out_ref,
    *rest,
):
    if hand_on:
        next_ref, wide_ref, normed_ref, act_ref, slots, send_sem, recv_sem = rest[:7]
        hand_send, hand_recv, fresh_sem = rest[7:]
    else:
        wide_ref, normed_ref, act_ref, slots, send_sem, recv_sem = rest
    me = lax.axis_index("row")
    section = lax.axis_index("section")
    barrier = pltpu.get_barrier_semaphore()
    for k in range(1, n):
        pl.semaphore_signal(
            barrier, inc=1, device_id={"row": lax.rem(me + k, n)}, device_id_type=MESH
        )
    waits = n - 1
    if hand_on:
        cells = out_ref.shape[0]
        edge = 3 * cells // 4
        has_above = me > 0
        has_below = me < n - 1
        has_prev = section > 0
        has_next = section < sections - 1
        @pl.when(has_prev)
        def _():
            pl.semaphore_signal(
                barrier, inc=1, device_id={"section": section - 1}, device_id_type=MESH
            )

        waits = waits + has_next.astype(jnp.int32)
    padded_rows, margin_cols, channels = wide_ref.shape
    cols = padded_ref.shape[0] // padded_rows
    out_rows = padded_rows - 6
    zeros = jnp.zeros((8, channels), jnp.float32)
    for r in range(padded_rows):
        wide_ref[r, pl.ds(0, 8), :] = zeros
        wide_ref[r, pl.ds(8, cols), :] = padded_ref[pl.ds(r * cols, cols), :].astype(jnp.float32)
        wide_ref[r, pl.ds(8 + cols, margin_cols - 8 - cols), :] = zeros[: margin_cols - 8 - cols]

    def conv_row(h, carry):
        acc = jnp.broadcast_to(depth_bias_ref[...].astype(jnp.float32), (cols, channels))
        for i in range(7):
            for j in range(7):
                tap = taps_ref[pl.ds(i * 7 + j, 1), :].astype(jnp.float32)
                acc = acc + wide_ref[h + i, pl.ds(j + 5, cols), :] * tap
        mean = jnp.mean(acc, axis=-1, keepdims=True)
        center = acc - mean
        spread = jnp.mean(center * center, axis=-1, keepdims=True)
        normed = (
            center * lax.rsqrt(spread + EPS_NORM) * gain_ref[...].astype(jnp.float32)
            + shift_ref[...].astype(jnp.float32)
        )
        normed_ref[pl.ds(pl.multiple_of(h * cols, 16), cols), :] = normed.astype(normed_ref.dtype)
        return carry

    lax.fori_loop(0, out_rows, conv_row, 0)
    first_core = lax.rem(me, 2) == 0

    def raise_with(proj_in_ref):
        raised = jnp.dot(
            normed_ref[...], proj_in_ref[...], preferred_element_type=jnp.float32
        ) + bias_in_ref[...].astype(jnp.float32)
        act_ref[...] = (0.5 * raised * (1.0 + lax.erf(raised * (1.0 / math.sqrt(2.0))))).astype(
            jnp.bfloat16
        )

    pl.when(first_core)(lambda: raise_with(held_ref))
    pl.when(jnp.logical_not(first_core))(lambda: raise_with(other_ref))
    grouped = act_ref[...].astype(jnp.float32)
    slots[me] = jnp.sum(grouped * grouped, axis=0, keepdims=True)
    pl.semaphore_wait(barrier, waits)
    sends = []
    for k in range(1, n):
        copy = pltpu.make_async_remote_copy(
            src_ref=slots.at[me],
            dst_ref=slots.at[me],
            send_sem=send_sem.at[k],
            recv_sem=recv_sem.at[me],
            device_id={"row": lax.rem(me + k, n)},
            device_id_type=MESH,
        )
        copy.start()
        sends.append(copy)
    if hand_on:
        @pl.when(section == 0)
        def _():
            fresh_copy = pltpu.make_async_copy(fresh_ref.at[fresh_index], next_ref, fresh_sem)
            fresh_copy.start()
            fresh_copy.wait()

        @pl.when(jnp.logical_and(has_prev, jnp.logical_not(has_above)))
        def _():
            next_ref[pl.ds(0, edge), :] = jnp.zeros((edge, next_ref.shape[1]), next_ref.dtype)

        @pl.when(jnp.logical_and(has_prev, jnp.logical_not(has_below)))
        def _():
            next_ref[pl.ds(edge + cells, edge), :] = jnp.zeros(
                (edge, next_ref.shape[1]), next_ref.dtype
            )

    for k in range(1, n):
        src = lax.rem(me + k, n)
        pltpu.make_async_remote_copy(
            src_ref=slots.at[src],
            dst_ref=slots.at[src],
            send_sem=send_sem.at[k],
            recv_sem=recv_sem.at[src],
            device_id={"row": src},
            device_id_type=MESH,
        ).wait_recv()
    for copy in sends:
        copy.wait_send()
    total_sq = slots[0]
    for j in range(1, n):
        total_sq = total_sq + slots[j]
    magnitude = jnp.sqrt(total_sq)
    grn_ratio = magnitude / (jnp.mean(magnitude, axis=-1, keepdims=True) + EPS_GRN)
    grouped = act_ref[...].astype(jnp.float32)
    hidden = (
        gamma_ref[...].astype(jnp.float32) * grouped * grn_ratio
        + beta_ref[...].astype(jnp.float32)
        + grouped
    ).astype(jnp.bfloat16)
    cells = out_ref.shape[0]
    edge = 3 * cells // 4

    def lower_with(proj_out_t_ref):
        update = lax.dot_general(
            hidden,
            proj_out_t_ref[...],
            (((1,), (1,)), ((), ())),
            preferred_element_type=jnp.float32,
        ) + bias_out_ref[...].astype(jnp.float32)
        current = padded_ref[pl.ds(edge, cells), :].astype(jnp.float32)
        out_ref[...] = (current + update).astype(out_ref.dtype)

    pl.when(first_core)(lambda: lower_with(other_ref))
    pl.when(jnp.logical_not(first_core))(lambda: lower_with(held_ref))
    if not hand_on:
        return
    own_rows = pl.ds(edge, cells)
    handed = pltpu.make_async_remote_copy(
        src_ref=out_ref,
        dst_ref=next_ref.at[own_rows],
        send_sem=hand_send.at[1],
        recv_sem=hand_recv.at[1],
        device_id={"section": section + 1},
        device_id_type=MESH,
    )

    @pl.when(has_next)
    def _():
        handed.start()

    halos = (
        (2, pl.ds(edge, edge), pl.ds(edge + cells, edge), -1, has_above),
        (0, pl.ds(cells, edge), pl.ds(0, edge), 1, has_below),
    )

    def halo_copy(slot, src, dst, peer_row):
        return pltpu.make_async_remote_copy(
            src_ref=next_ref.at[src],
            dst_ref=next_ref.at[dst],
            send_sem=hand_send.at[slot],
            recv_sem=hand_recv.at[slot],
            device_id={"row": peer_row},
            device_id_type=MESH,
        )

    @pl.when(has_prev)
    def _():
        handed.wait_recv()
        for slot, src, dst, shift, cond in halos:
            @pl.when(cond)
            def _():
                halo_copy(slot, src, dst, me + shift).start()

        for slot, src, dst, shift, cond in halos:
            @pl.when(halos[slot // 2][4])
            def _():
                halo_copy(slot, src, dst, me).wait_recv()

        for slot, src, dst, shift, cond in halos:
            @pl.when(cond)
            def _():
                halo_copy(slot, src, dst, me + shift).wait_send()

    @pl.when(has_next)
    def _():
        handed.wait_send()


def pointwise(
    padded,
    fresh,
    fresh_index,
    held,
    other,
    bias_in,
    grn_gamma,
    grn_beta,
    bias_out,
    depth_kernel,
    depth_bias,
    norm_gain,
    norm_bias,
    cols,
    hand_on,
):
    n = lax.axis_size("row")
    sections = lax.axis_size("section")
    channels = padded.shape[1]
    padded_rows = padded.shape[0] // cols
    cells = (padded_rows - 6) * cols
    hidden_units = held.shape[1]
    vmem = pl.BlockSpec(memory_space=pltpu.VMEM)
    out_shape = [jax.ShapeDtypeStruct((cells, channels), padded.dtype)]
    scratch = [
        pltpu.VMEM((padded_rows, -(-(cols + 11) // 8) * 8, channels), jnp.float32),
        pltpu.VMEM((cells, channels), jnp.bfloat16),
        pltpu.VMEM((cells, hidden_units), jnp.bfloat16),
        pltpu.VMEM((n, 1, hidden_units), jnp.float32),
        pltpu.SemaphoreType.DMA((n,)),
        pltpu.SemaphoreType.DMA((n,)),
    ]
    if hand_on:
        out_shape.append(jax.ShapeDtypeStruct(fresh.shape[1:], fresh.dtype))
        scratch += [
            pltpu.SemaphoreType.DMA((3,)),
            pltpu.SemaphoreType.DMA((3,)),
            pltpu.SemaphoreType.DMA(()),
        ]
    return pl.pallas_call(
        functools.partial(_pointwise_kernel, n, sections, hand_on, fresh_index),
        out_shape=out_shape,
        in_specs=[vmem, pl.BlockSpec(memory_space=pl.ANY)] + [vmem] * 10,
        out_specs=[vmem] * len(out_shape),
        scratch_shapes=scratch,
        compiler_params=pltpu.CompilerParams(
            collective_id=1 + fresh_index if hand_on else 0, has_side_effects=True
        ),
        cost_estimate=pl.CostEstimate(
            flops=4 * cells * channels * hidden_units,
            transcendentals=cells * hidden_units,
            bytes_accessed=4 * channels * hidden_units + 8 * cells * channels,
        ),
    )(
        padded,
        fresh,
        held,
        other,
        bias_in.reshape(1, -1),
        grn_gamma.reshape(1, -1),
        grn_beta.reshape(1, -1),
        bias_out.reshape(1, -1),
        depth_kernel.reshape(-1, channels),
        depth_bias.reshape(1, -1),
        norm_gain.reshape(1, -1),
        norm_bias.reshape(1, -1),
    )


def passed_along(x, axis, by):
    count = lax.axis_size(axis)
    pairs = [(i, i + by) for i in range(count) if 0 <= i + by < count]
    return lax.ppermute(x, axis, pairs)


def depthwise(padded, kernel, bias_term):
    channels = padded.shape[-1]
    conv_out = lax.conv_general_dilated(
        padded.astype(jnp.float32),
        kernel.astype(jnp.float32)[:, :, None, :],
        (1, 1),
        "VALID",
        dimension_numbers=("NHWC", "HWIO", "NHWC"),
        feature_group_count=channels,
        precision=lax.Precision.HIGHEST,
    )
    return conv_out + bias_term.astype(jnp.float32)


def conv_block(padded, fresh, fresh_index, params, hand_on):
    (
        depth_kernel,
        depth_bias,
        norm_gain,
        norm_bias,
        proj_in,
        bias_in,
        grn_gamma,
        grn_beta,
        proj_out,
        bias_out,
    ) = params
    num_items, padded_rows, num_cols, channels = padded.shape
    results = pointwise(
        padded.reshape(-1, channels),
        fresh.reshape(fresh.shape[0], -1, channels),
        fresh_index,
        proj_in,
        proj_out,
        bias_in,
        grn_gamma,
        grn_beta,
        bias_out,
        depth_kernel,
        depth_bias,
        norm_gain,
        norm_bias,
        num_cols,
        hand_on,
    )
    produced = results[0].reshape(num_items, padded_rows - 6, num_cols, channels)
    arriving = results[1].reshape(padded.shape) if hand_on else None
    return produced, arriving


def gathered_weights(proj_in, proj_out):
    rows = lax.axis_size("row")
    first_core = lax.rem(lax.axis_index("row"), 2) == 0
    mine = jnp.where(first_core, proj_in, proj_out.T)
    held = lax.all_gather(mine, "dp", axis=1, tiled=True)
    other = lax.ppermute(held, "row", [(r, r ^ 1) for r in range(rows)])
    return held, other


def on_device(
    inputs,
    depth_kernel,
    depth_bias,
    norm_gain,
    norm_bias,
    proj_in,
    bias_in,
    grn_gamma,
    grn_beta,
    proj_out,
    bias_out,
):
    fresh = extended(inputs[:, 0], (("row", 1),), 3)
    proj_in, proj_out = gathered_weights(proj_in[0], proj_out[0])
    sections = lax.axis_size("section")
    section_index = lax.axis_index("section")
    num_micro = inputs.shape[0]
    own_params = (
        depth_kernel[0],
        depth_bias[0],
        norm_gain[0],
        norm_bias[0],
        proj_in,
        bias_in[0],
        grn_gamma[0],
        grn_beta[0],
        proj_out,
        bias_out[0],
    )
    num_ticks = num_micro + sections - 1
    current = fresh[:1]
    outputs = []
    for tick_index in range(num_ticks):
        hand_on = tick_index + 1 < num_ticks
        produced, current = conv_block(
            current, fresh, min(tick_index + 1, num_micro - 1), own_params, hand_on
        )
        outputs.append(produced)
    stacked = jnp.stack(outputs)
    saved = lax.dynamic_slice_in_dim(stacked, section_index, num_micro, axis=0)
    return saved[None]


def solution(mesh):
    return jax.shard_map(
        on_device,
        mesh=mesh,
        in_specs=(
            P(None, "dp", "row", None, None),
            P("section", None, None, None),
            P("section", None),
            P("section", None),
            P("section", None),
            P("section", None, "dp"),
            P("section", None),
            P("section", None),
            P("section", None),
            P("section", "dp", None),
            P("section", None),
        ),
        out_specs=P("section", None, "dp", "row", None, None),
        check_vma=False,
    )
```

```python
import functools
import math

import jax
import jax.numpy as jnp
from jax import lax
from jax.experimental import pallas as pl
from jax.experimental.pallas import tpu as pltpu
from jax.sharding import PartitionSpec as P

MESH = pl.DeviceIdType.MESH

EPS_NORM = 1e-06
EPS_GRN = 1e-06


def extended(cells, sides, width):
    for axis, dim in sides:
        count = lax.axis_size(axis)
        ends = count - 1
        head = lax.slice_in_dim(cells, 0, width, axis=dim)
        tail = lax.slice_in_dim(cells, cells.shape[dim] - width, cells.shape[dim], axis=dim)
        cells = jnp.concatenate(
            [
                lax.ppermute(tail, axis, [(i, (i + 1) % count) for i in range(ends)]),
                cells,
                lax.ppermute(head, axis, [((i + 1) % count, i) for i in range(ends)]),
            ],
            axis=dim,
        )
    return cells


def _pointwise_kernel(
    n,
    sections,
    hand_on,
    fresh_index,
    padded_ref,
    fresh_ref,
    held_ref,
    other_ref,
    bias_in_ref,
    gamma_ref,
    beta_ref,
    bias_out_ref,
    taps_ref,
    depth_bias_ref,
    gain_ref,
    shift_ref,
    out_ref,
    *rest,
):
    if hand_on:
        next_ref, wide_ref, normed_ref, act_ref, slots, send_sem, recv_sem = rest[:7]
        hand_send, hand_recv, fresh_sem = rest[7:]
    else:
        wide_ref, normed_ref, act_ref, slots, send_sem, recv_sem = rest
    me = lax.axis_index("row")
    section = lax.axis_index("section")
    barrier = pltpu.get_barrier_semaphore()
    for k in range(1, n):
        pl.semaphore_signal(
            barrier, inc=1, device_id={"row": lax.rem(me + k, n)}, device_id_type=MESH
        )
    waits = n - 1
    if hand_on:
        cells = out_ref.shape[0]
        edge = 3 * cells // 4
        has_above = me > 0
        has_below = me < n - 1
        has_prev = section > 0
        has_next = section < sections - 1
        @pl.when(has_prev)
        def _():
            pl.semaphore_signal(
                barrier, inc=1, device_id={"section": section - 1}, device_id_type=MESH
            )

        waits = waits + has_next.astype(jnp.int32)
    padded_rows, margin_cols, channels = wide_ref.shape
    cols = padded_ref.shape[0] // padded_rows
    out_rows = padded_rows - 6
    zeros = jnp.zeros((8, channels), jnp.float32)
    for r in range(padded_rows):
        wide_ref[r, pl.ds(0, 8), :] = zeros
        wide_ref[r, pl.ds(8, cols), :] = padded_ref[pl.ds(r * cols, cols), :].astype(jnp.float32)
        wide_ref[r, pl.ds(8 + cols, margin_cols - 8 - cols), :] = zeros[: margin_cols - 8 - cols]

    def conv_row(h, carry):
        acc = jnp.broadcast_to(depth_bias_ref[...].astype(jnp.float32), (cols, channels))
        for i in range(7):
            for j in range(7):
                tap = taps_ref[pl.ds(i * 7 + j, 1), :].astype(jnp.float32)
                acc = acc + wide_ref[h + i, pl.ds(j + 5, cols), :] * tap
        mean = jnp.mean(acc, axis=-1, keepdims=True)
        center = acc - mean
        spread = jnp.mean(center * center, axis=-1, keepdims=True)
        normed = (
            center * lax.rsqrt(spread + EPS_NORM) * gain_ref[...].astype(jnp.float32)
            + shift_ref[...].astype(jnp.float32)
        )
        normed_ref[pl.ds(pl.multiple_of(h * cols, 16), cols), :] = normed.astype(normed_ref.dtype)
        return carry

    lax.fori_loop(0, out_rows, conv_row, 0)
    first_core = lax.rem(me, 2) == 0

    def raise_with(proj_in_t_ref):
        raised = lax.dot_general(
            normed_ref[...],
            proj_in_t_ref[...],
            (((1,), (1,)), ((), ())),
            preferred_element_type=jnp.float32,
        ) + bias_in_ref[...].astype(jnp.float32)
        act_ref[...] = (0.5 * raised * (1.0 + lax.erf(raised * (1.0 / math.sqrt(2.0))))).astype(
            jnp.bfloat16
        )

    pl.when(first_core)(lambda: raise_with(held_ref))
    pl.when(jnp.logical_not(first_core))(lambda: raise_with(other_ref))
    grouped = act_ref[...].astype(jnp.float32)
    slots[me] = jnp.sum(grouped * grouped, axis=0, keepdims=True)
    pl.semaphore_wait(barrier, waits)
    sends = []
    for k in range(1, n):
        copy = pltpu.make_async_remote_copy(
            src_ref=slots.at[me],
            dst_ref=slots.at[me],
            send_sem=send_sem.at[k],
            recv_sem=recv_sem.at[me],
            device_id={"row": lax.rem(me + k, n)},
            device_id_type=MESH,
        )
        copy.start()
        sends.append(copy)
    if hand_on:
        @pl.when(section == 0)
        def _():
            fresh_copy = pltpu.make_async_copy(fresh_ref.at[fresh_index], next_ref, fresh_sem)
            fresh_copy.start()
            fresh_copy.wait()

        @pl.when(jnp.logical_and(has_prev, jnp.logical_not(has_above)))
        def _():
            next_ref[pl.ds(0, edge), :] = jnp.zeros((edge, next_ref.shape[1]), next_ref.dtype)

        @pl.when(jnp.logical_and(has_prev, jnp.logical_not(has_below)))
        def _():
            next_ref[pl.ds(edge + cells, edge), :] = jnp.zeros(
                (edge, next_ref.shape[1]), next_ref.dtype
            )

    for k in range(1, n):
        src = lax.rem(me + k, n)
        pltpu.make_async_remote_copy(
            src_ref=slots.at[src],
            dst_ref=slots.at[src],
            send_sem=send_sem.at[k],
            recv_sem=recv_sem.at[src],
            device_id={"row": src},
            device_id_type=MESH,
        ).wait_recv()
    for copy in sends:
        copy.wait_send()
    total_sq = slots[0]
    for j in range(1, n):
        total_sq = total_sq + slots[j]
    magnitude = jnp.sqrt(total_sq)
    grn_ratio = magnitude / (jnp.mean(magnitude, axis=-1, keepdims=True) + EPS_GRN)
    grouped = act_ref[...].astype(jnp.float32)
    hidden = (
        gamma_ref[...].astype(jnp.float32) * grouped * grn_ratio
        + beta_ref[...].astype(jnp.float32)
        + grouped
    ).astype(jnp.bfloat16)
    cells = out_ref.shape[0]
    edge = 3 * cells // 4

    def lower_with(proj_out_ref):
        update = jnp.dot(
            hidden, proj_out_ref[...], preferred_element_type=jnp.float32
        ) + bias_out_ref[...].astype(jnp.float32)
        current = padded_ref[pl.ds(edge, cells), :].astype(jnp.float32)
        out_ref[...] = (current + update).astype(out_ref.dtype)

    pl.when(first_core)(lambda: lower_with(other_ref))
    pl.when(jnp.logical_not(first_core))(lambda: lower_with(held_ref))
    if not hand_on:
        return
    own_rows = pl.ds(edge, cells)
    handed = pltpu.make_async_remote_copy(
        src_ref=out_ref,
        dst_ref=next_ref.at[own_rows],
        send_sem=hand_send.at[1],
        recv_sem=hand_recv.at[1],
        device_id={"section": section + 1},
        device_id_type=MESH,
    )

    @pl.when(has_next)
    def _():
        handed.start()

    halos = (
        (2, pl.ds(edge, edge), pl.ds(edge + cells, edge), -1, has_above),
        (0, pl.ds(cells, edge), pl.ds(0, edge), 1, has_below),
    )

    def halo_copy(slot, src, dst, peer_row):
        return pltpu.make_async_remote_copy(
            src_ref=next_ref.at[src],
            dst_ref=next_ref.at[dst],
            send_sem=hand_send.at[slot],
            recv_sem=hand_recv.at[slot],
            device_id={"row": peer_row},
            device_id_type=MESH,
        )

    @pl.when(has_prev)
    def _():
        handed.wait_recv()
        for slot, src, dst, shift, cond in halos:
            @pl.when(cond)
            def _():
                halo_copy(slot, src, dst, me + shift).start()

        for slot, src, dst, shift, cond in halos:
            @pl.when(halos[slot // 2][4])
            def _():
                halo_copy(slot, src, dst, me).wait_recv()

        for slot, src, dst, shift, cond in halos:
            @pl.when(cond)
            def _():
                halo_copy(slot, src, dst, me + shift).wait_send()

    @pl.when(has_next)
    def _():
        handed.wait_send()


def pointwise(
    padded,
    fresh,
    fresh_index,
    held,
    other,
    bias_in,
    grn_gamma,
    grn_beta,
    bias_out,
    depth_kernel,
    depth_bias,
    norm_gain,
    norm_bias,
    cols,
    hand_on,
):
    n = lax.axis_size("row")
    sections = lax.axis_size("section")
    channels = padded.shape[1]
    padded_rows = padded.shape[0] // cols
    cells = (padded_rows - 6) * cols
    hidden_units = held.shape[0]
    vmem = pl.BlockSpec(memory_space=pltpu.VMEM)
    out_shape = [jax.ShapeDtypeStruct((cells, channels), padded.dtype)]
    scratch = [
        pltpu.VMEM((padded_rows, -(-(cols + 11) // 8) * 8, channels), jnp.float32),
        pltpu.VMEM((cells, channels), jnp.bfloat16),
        pltpu.VMEM((cells, hidden_units), jnp.bfloat16),
        pltpu.VMEM((n, 1, hidden_units), jnp.float32),
        pltpu.SemaphoreType.DMA((n,)),
        pltpu.SemaphoreType.DMA((n,)),
    ]
    if hand_on:
        out_shape.append(jax.ShapeDtypeStruct(fresh.shape[1:], fresh.dtype))
        scratch += [
            pltpu.SemaphoreType.DMA((3,)),
            pltpu.SemaphoreType.DMA((3,)),
            pltpu.SemaphoreType.DMA(()),
        ]
    return pl.pallas_call(
        functools.partial(_pointwise_kernel, n, sections, hand_on, fresh_index),
        out_shape=out_shape,
        in_specs=[vmem, pl.BlockSpec(memory_space=pl.ANY)] + [vmem] * 10,
        out_specs=[vmem] * len(out_shape),
        scratch_shapes=scratch,
        compiler_params=pltpu.CompilerParams(
            collective_id=1 + fresh_index if hand_on else 0, has_side_effects=True
        ),
        cost_estimate=pl.CostEstimate(
            flops=4 * cells * channels * hidden_units,
            transcendentals=cells * hidden_units,
            bytes_accessed=4 * channels * hidden_units + 8 * cells * channels,
        ),
    )(
        padded,
        fresh,
        held,
        other,
        bias_in.reshape(1, -1),
        grn_gamma.reshape(1, -1),
        grn_beta.reshape(1, -1),
        bias_out.reshape(1, -1),
        depth_kernel.reshape(-1, channels),
        depth_bias.reshape(1, -1),
        norm_gain.reshape(1, -1),
        norm_bias.reshape(1, -1),
    )


def passed_along(x, axis, by):
    count = lax.axis_size(axis)
    pairs = [(i, i + by) for i in range(count) if 0 <= i + by < count]
    return lax.ppermute(x, axis, pairs)


def depthwise(padded, kernel, bias_term):
    channels = padded.shape[-1]
    conv_out = lax.conv_general_dilated(
        padded.astype(jnp.float32),
        kernel.astype(jnp.float32)[:, :, None, :],
        (1, 1),
        "VALID",
        dimension_numbers=("NHWC", "HWIO", "NHWC"),
        feature_group_count=channels,
        precision=lax.Precision.HIGHEST,
    )
    return conv_out + bias_term.astype(jnp.float32)


def conv_block(padded, fresh, fresh_index, params, hand_on):
    (
        depth_kernel,
        depth_bias,
        norm_gain,
        norm_bias,
        proj_in,
        bias_in,
        grn_gamma,
        grn_beta,
        proj_out,
        bias_out,
    ) = params
    num_items, padded_rows, num_cols, channels = padded.shape
    results = pointwise(
        padded.reshape(-1, channels),
        fresh.reshape(fresh.shape[0], -1, channels),
        fresh_index,
        proj_in,
        proj_out,
        bias_in,
        grn_gamma,
        grn_beta,
        bias_out,
        depth_kernel,
        depth_bias,
        norm_gain,
        norm_bias,
        num_cols,
        hand_on,
    )
    produced = results[0].reshape(num_items, padded_rows - 6, num_cols, channels)
    arriving = results[1].reshape(padded.shape) if hand_on else None
    return produced, arriving


def _gather_kernel(n, mine_ref, held_ref, other_ref, send_sem, recv_sem, pass_send, pass_recv):
    me = lax.axis_index("dp")
    row = lax.axis_index("row")
    partner = {"row": row + 1 - 2 * lax.rem(row, 2)}
    right = {"dp": lax.rem(me + 1, n)}
    left = {"dp": lax.rem(me + n - 1, n)}
    barrier = pltpu.get_barrier_semaphore()
    for peer in (right, left, partner):
        pl.semaphore_signal(barrier, inc=1, device_id=peer, device_id_type=MESH)
    pl.semaphore_wait(barrier, 3)
    sends = []

    def send(src, dst, send_sems, recv_sems, slot, peer):
        copy = pltpu.make_async_remote_copy(
            src_ref=src,
            dst_ref=dst.at[slot],
            send_sem=send_sems.at[len(sends)],
            recv_sem=recv_sems.at[slot],
            device_id=peer,
            device_id_type=MESH,
        )
        copy.start()
        sends.append(copy)

    def arrived(slot):
        pltpu.make_async_remote_copy(
            src_ref=mine_ref,
            dst_ref=held_ref.at[slot],
            send_sem=send_sem.at[0],
            recv_sem=recv_sem.at[slot],
            device_id=right,
            device_id_type=MESH,
        ).wait_recv()

    to_right = n // 2
    to_left = n - 1 - to_right
    send(mine_ref, held_ref, send_sem, recv_sem, me, right)
    send(mine_ref, held_ref, send_sem, recv_sem, me, left)
    send(mine_ref, other_ref, pass_send, pass_recv, me, partner)
    held_ref[me] = mine_ref[...]
    for k in range(1, max(to_right, to_left) + 1):
        if k <= to_right:
            origin = lax.rem(me + n - k, n)
            arrived(origin)
            if k < to_right:
                send(held_ref.at[origin], held_ref, send_sem, recv_sem, origin, right)
            send(held_ref.at[origin], other_ref, pass_send, pass_recv, origin, partner)
        if k <= to_left:
            origin = lax.rem(me + k, n)
            arrived(origin)
            if k < to_left:
                send(held_ref.at[origin], held_ref, send_sem, recv_sem, origin, left)
            send(held_ref.at[origin], other_ref, pass_send, pass_recv, origin, partner)
    for slot in range(n):
        pltpu.make_async_remote_copy(
            src_ref=mine_ref,
            dst_ref=other_ref.at[slot],
            send_sem=pass_send.at[0],
            recv_sem=pass_recv.at[slot],
            device_id=partner,
            device_id_type=MESH,
        ).wait_recv()
    for copy in sends:
        copy.wait_send()


def gathered_weights(proj_in, proj_out):
    n = lax.axis_size("dp")
    first_core = lax.rem(lax.axis_index("row"), 2) == 0
    mine = jnp.where(first_core, proj_in.T, proj_out)
    part, channels = mine.shape
    vmem = pl.BlockSpec(memory_space=pltpu.VMEM)
    gathered = jax.ShapeDtypeStruct((n, part, channels), mine.dtype)
    held, other = pl.pallas_call(
        functools.partial(_gather_kernel, n),
        out_shape=[gathered, gathered],
        in_specs=[vmem],
        out_specs=[vmem, vmem],
        scratch_shapes=[
            pltpu.SemaphoreType.DMA((2 * n,)),
            pltpu.SemaphoreType.DMA((n,)),
            pltpu.SemaphoreType.DMA((2 * n,)),
            pltpu.SemaphoreType.DMA((n,)),
        ],
        compiler_params=pltpu.CompilerParams(collective_id=7, has_side_effects=True),
    )(mine)
    return held.reshape(n * part, channels), other.reshape(n * part, channels)


def on_device(
    inputs,
    depth_kernel,
    depth_bias,
    norm_gain,
    norm_bias,
    proj_in,
    bias_in,
    grn_gamma,
    grn_beta,
    proj_out,
    bias_out,
):
    fresh = extended(inputs[:, 0], (("row", 1),), 3)
    proj_in, proj_out = gathered_weights(proj_in[0], proj_out[0])
    sections = lax.axis_size("section")
    section_index = lax.axis_index("section")
    num_micro = inputs.shape[0]
    own_params = (
        depth_kernel[0],
        depth_bias[0],
        norm_gain[0],
        norm_bias[0],
        proj_in,
        bias_in[0],
        grn_gamma[0],
        grn_beta[0],
        proj_out,
        bias_out[0],
    )
    num_ticks = num_micro + sections - 1
    current = fresh[:1]
    outputs = []
    for tick_index in range(num_ticks):
        hand_on = tick_index + 1 < num_ticks
        produced, current = conv_block(
            current, fresh, min(tick_index + 1, num_micro - 1), own_params, hand_on
        )
        outputs.append(produced)
    stacked = jnp.stack(outputs)
    saved = lax.dynamic_slice_in_dim(stacked, section_index, num_micro, axis=0)
    return saved[None]


def solution(mesh):
    return jax.shard_map(
        on_device,
        mesh=mesh,
        in_specs=(
            P(None, "dp", "row", None, None),
            P("section", None, None, None),
            P("section", None),
            P("section", None),
            P("section", None),
            P("section", None, "dp"),
            P("section", None),
            P("section", None),
            P("section", None),
            P("section", "dp", None),
            P("section", None),
        ),
        out_specs=P("section", None, "dp", "row", None, None),
        check_vma=False,
    )
```

```python
import functools
import math

import jax
import jax.numpy as jnp
from jax import lax
from jax.experimental import pallas as pl
from jax.experimental.pallas import tpu as pltpu
from jax.sharding import PartitionSpec as P

MESH = pl.DeviceIdType.MESH

EPS_NORM = 1e-06
EPS_GRN = 1e-06


def extended(cells, sides, width):
    for axis, dim in sides:
        count = lax.axis_size(axis)
        ends = count - 1
        head = lax.slice_in_dim(cells, 0, width, axis=dim)
        tail = lax.slice_in_dim(cells, cells.shape[dim] - width, cells.shape[dim], axis=dim)
        cells = jnp.concatenate(
            [
                lax.ppermute(tail, axis, [(i, (i + 1) % count) for i in range(ends)]),
                cells,
                lax.ppermute(head, axis, [((i + 1) % count, i) for i in range(ends)]),
            ],
            axis=dim,
        )
    return cells


def _pointwise_kernel(
    n,
    sections,
    hand_on,
    fresh_index,
    padded_ref,
    fresh_ref,
    held_ref,
    other_ref,
    bias_in_ref,
    gamma_ref,
    beta_ref,
    bias_out_ref,
    taps_ref,
    depth_bias_ref,
    gain_ref,
    shift_ref,
    out_ref,
    *rest,
):
    if hand_on:
        next_ref, wide_ref, normed_ref, act_ref, slots, send_sem, recv_sem = rest[:7]
        hand_send, hand_recv, fresh_sem = rest[7:]
    else:
        wide_ref, normed_ref, act_ref, slots, send_sem, recv_sem = rest
    me = lax.axis_index("row")
    section = lax.axis_index("section")
    barrier = pltpu.get_barrier_semaphore()
    for k in range(1, n):
        pl.semaphore_signal(
            barrier, inc=1, device_id={"row": lax.rem(me + k, n)}, device_id_type=MESH
        )
    waits = n - 1
    if hand_on:
        cells = out_ref.shape[0]
        edge = 3 * cells // 4
        has_above = me > 0
        has_below = me < n - 1
        has_prev = section > 0
        has_next = section < sections - 1
        @pl.when(has_prev)
        def _():
            pl.semaphore_signal(
                barrier, inc=1, device_id={"section": section - 1}, device_id_type=MESH
            )

        waits = waits + has_next.astype(jnp.int32)
    padded_rows, margin_cols, channels = wide_ref.shape
    cols = padded_ref.shape[0] // padded_rows
    out_rows = padded_rows - 6
    zeros = jnp.zeros((8, channels), jnp.float32)
    for r in range(padded_rows):
        wide_ref[r, pl.ds(0, 8), :] = zeros
        wide_ref[r, pl.ds(8, cols), :] = padded_ref[pl.ds(r * cols, cols), :].astype(jnp.float32)
        wide_ref[r, pl.ds(8 + cols, margin_cols - 8 - cols), :] = zeros[: margin_cols - 8 - cols]

    def conv_row(h, carry):
        acc = jnp.broadcast_to(depth_bias_ref[...].astype(jnp.float32), (cols, channels))
        for i in range(7):
            for j in range(7):
                tap = taps_ref[pl.ds(i * 7 + j, 1), :].astype(jnp.float32)
                acc = acc + wide_ref[h + i, pl.ds(j + 5, cols), :] * tap
        mean = jnp.mean(acc, axis=-1, keepdims=True)
        center = acc - mean
        spread = jnp.mean(center * center, axis=-1, keepdims=True)
        normed = (
            center * lax.rsqrt(spread + EPS_NORM) * gain_ref[...].astype(jnp.float32)
            + shift_ref[...].astype(jnp.float32)
        )
        normed_ref[pl.ds(pl.multiple_of(h * cols, 16), cols), :] = normed.astype(normed_ref.dtype)
        return carry

    lax.fori_loop(0, out_rows, conv_row, 0)
    first_core = lax.rem(me, 2) == 0

    def raise_with(proj_in_t_ref):
        raised = lax.dot_general(
            normed_ref[...],
            proj_in_t_ref[...],
            (((1,), (1,)), ((), ())),
            preferred_element_type=jnp.float32,
        ) + bias_in_ref[...].astype(jnp.float32)
        act_ref[...] = (0.5 * raised * (1.0 + lax.erf(raised * (1.0 / math.sqrt(2.0))))).astype(
            jnp.bfloat16
        )

    pl.when(first_core)(lambda: raise_with(held_ref))
    pl.when(jnp.logical_not(first_core))(lambda: raise_with(other_ref))
    grouped = act_ref[...].astype(jnp.float32)
    slots[me] = jnp.sum(grouped * grouped, axis=0, keepdims=True)
    pl.semaphore_wait(barrier, waits)
    sends = []
    for k in range(1, n):
        copy = pltpu.make_async_remote_copy(
            src_ref=slots.at[me],
            dst_ref=slots.at[me],
            send_sem=send_sem.at[k],
            recv_sem=recv_sem.at[me],
            device_id={"row": lax.rem(me + k, n)},
            device_id_type=MESH,
        )
        copy.start()
        sends.append(copy)
    if hand_on:
        @pl.when(section == 0)
        def _():
            fresh_copy = pltpu.make_async_copy(fresh_ref.at[fresh_index], next_ref, fresh_sem)
            fresh_copy.start()
            fresh_copy.wait()

        @pl.when(jnp.logical_and(has_prev, jnp.logical_not(has_above)))
        def _():
            next_ref[pl.ds(0, edge), :] = jnp.zeros((edge, next_ref.shape[1]), next_ref.dtype)

        @pl.when(jnp.logical_and(has_prev, jnp.logical_not(has_below)))
        def _():
            next_ref[pl.ds(edge + cells, edge), :] = jnp.zeros(
                (edge, next_ref.shape[1]), next_ref.dtype
            )

    for k in range(1, n):
        src = lax.rem(me + k, n)
        pltpu.make_async_remote_copy(
            src_ref=slots.at[src],
            dst_ref=slots.at[src],
            send_sem=send_sem.at[k],
            recv_sem=recv_sem.at[src],
            device_id={"row": src},
            device_id_type=MESH,
        ).wait_recv()
    for copy in sends:
        copy.wait_send()
    total_sq = slots[0]
    for j in range(1, n):
        total_sq = total_sq + slots[j]
    magnitude = jnp.sqrt(total_sq)
    grn_ratio = magnitude / (jnp.mean(magnitude, axis=-1, keepdims=True) + EPS_GRN)
    grouped = act_ref[...].astype(jnp.float32)
    hidden = (
        gamma_ref[...].astype(jnp.float32) * grouped * grn_ratio
        + beta_ref[...].astype(jnp.float32)
        + grouped
    ).astype(jnp.bfloat16)
    cells = out_ref.shape[0]
    edge = 3 * cells // 4

    def lower_with(proj_out_ref):
        update = jnp.dot(
            hidden, proj_out_ref[...], preferred_element_type=jnp.float32
        ) + bias_out_ref[...].astype(jnp.float32)
        current = padded_ref[pl.ds(edge, cells), :].astype(jnp.float32)
        out_ref[...] = (current + update).astype(out_ref.dtype)

    pl.when(first_core)(lambda: lower_with(other_ref))
    pl.when(jnp.logical_not(first_core))(lambda: lower_with(held_ref))
    if not hand_on:
        return
    own_rows = pl.ds(edge, cells)
    handed = pltpu.make_async_remote_copy(
        src_ref=out_ref,
        dst_ref=next_ref.at[own_rows],
        send_sem=hand_send.at[1],
        recv_sem=hand_recv.at[1],
        device_id={"section": section + 1},
        device_id_type=MESH,
    )

    @pl.when(has_next)
    def _():
        handed.start()

    halos = (
        (2, pl.ds(edge, edge), pl.ds(edge + cells, edge), -1, has_above),
        (0, pl.ds(cells, edge), pl.ds(0, edge), 1, has_below),
    )

    def halo_copy(slot, src, dst, peer_row):
        return pltpu.make_async_remote_copy(
            src_ref=next_ref.at[src],
            dst_ref=next_ref.at[dst],
            send_sem=hand_send.at[slot],
            recv_sem=hand_recv.at[slot],
            device_id={"row": peer_row},
            device_id_type=MESH,
        )

    @pl.when(has_prev)
    def _():
        handed.wait_recv()
        for slot, src, dst, shift, cond in halos:
            @pl.when(cond)
            def _():
                halo_copy(slot, src, dst, me + shift).start()

        for slot, src, dst, shift, cond in halos:
            @pl.when(halos[slot // 2][4])
            def _():
                halo_copy(slot, src, dst, me).wait_recv()

        for slot, src, dst, shift, cond in halos:
            @pl.when(cond)
            def _():
                halo_copy(slot, src, dst, me + shift).wait_send()

    @pl.when(has_next)
    def _():
        handed.wait_send()


def pointwise(
    padded,
    fresh,
    fresh_index,
    held,
    other,
    bias_in,
    grn_gamma,
    grn_beta,
    bias_out,
    depth_kernel,
    depth_bias,
    norm_gain,
    norm_bias,
    cols,
    hand_on,
):
    n = lax.axis_size("row")
    sections = lax.axis_size("section")
    channels = padded.shape[1]
    padded_rows = padded.shape[0] // cols
    cells = (padded_rows - 6) * cols
    hidden_units = held.shape[0]
    vmem = pl.BlockSpec(memory_space=pltpu.VMEM)
    out_shape = [jax.ShapeDtypeStruct((cells, channels), padded.dtype)]
    scratch = [
        pltpu.VMEM((padded_rows, -(-(cols + 11) // 8) * 8, channels), jnp.float32),
        pltpu.VMEM((cells, channels), jnp.bfloat16),
        pltpu.VMEM((cells, hidden_units), jnp.bfloat16),
        pltpu.VMEM((n, 1, hidden_units), jnp.float32),
        pltpu.SemaphoreType.DMA((n,)),
        pltpu.SemaphoreType.DMA((n,)),
    ]
    if hand_on:
        out_shape.append(jax.ShapeDtypeStruct(fresh.shape[1:], fresh.dtype))
        scratch += [
            pltpu.SemaphoreType.DMA((3,)),
            pltpu.SemaphoreType.DMA((3,)),
            pltpu.SemaphoreType.DMA(()),
        ]
    return pl.pallas_call(
        functools.partial(_pointwise_kernel, n, sections, hand_on, fresh_index),
        out_shape=out_shape,
        in_specs=[vmem, pl.BlockSpec(memory_space=pl.ANY)] + [vmem] * 10,
        out_specs=[vmem] * len(out_shape),
        scratch_shapes=scratch,
        compiler_params=pltpu.CompilerParams(
            collective_id=1 + fresh_index if hand_on else 0, has_side_effects=True
        ),
        cost_estimate=pl.CostEstimate(
            flops=4 * cells * channels * hidden_units,
            transcendentals=cells * hidden_units,
            bytes_accessed=4 * channels * hidden_units + 8 * cells * channels,
        ),
    )(
        padded,
        fresh,
        held,
        other,
        bias_in.reshape(1, -1),
        grn_gamma.reshape(1, -1),
        grn_beta.reshape(1, -1),
        bias_out.reshape(1, -1),
        depth_kernel.reshape(-1, channels),
        depth_bias.reshape(1, -1),
        norm_gain.reshape(1, -1),
        norm_bias.reshape(1, -1),
    )


def passed_along(x, axis, by):
    count = lax.axis_size(axis)
    pairs = [(i, i + by) for i in range(count) if 0 <= i + by < count]
    return lax.ppermute(x, axis, pairs)


def depthwise(padded, kernel, bias_term):
    channels = padded.shape[-1]
    conv_out = lax.conv_general_dilated(
        padded.astype(jnp.float32),
        kernel.astype(jnp.float32)[:, :, None, :],
        (1, 1),
        "VALID",
        dimension_numbers=("NHWC", "HWIO", "NHWC"),
        feature_group_count=channels,
        precision=lax.Precision.HIGHEST,
    )
    return conv_out + bias_term.astype(jnp.float32)


def conv_block(padded, fresh, fresh_index, params, hand_on):
    (
        depth_kernel,
        depth_bias,
        norm_gain,
        norm_bias,
        proj_in,
        bias_in,
        grn_gamma,
        grn_beta,
        proj_out,
        bias_out,
    ) = params
    num_items, padded_rows, num_cols, channels = padded.shape
    results = pointwise(
        padded.reshape(-1, channels),
        fresh.reshape(fresh.shape[0], -1, channels),
        fresh_index,
        proj_in,
        proj_out,
        bias_in,
        grn_gamma,
        grn_beta,
        bias_out,
        depth_kernel,
        depth_bias,
        norm_gain,
        norm_bias,
        num_cols,
        hand_on,
    )
    produced = results[0].reshape(num_items, padded_rows - 6, num_cols, channels)
    arriving = results[1].reshape(padded.shape) if hand_on else None
    return produced, arriving


def _gather_kernel(n, mine_ref, held_ref, other_ref, send_sem, recv_sem, pass_send, pass_recv):
    me = lax.axis_index("dp")
    row = lax.axis_index("row")
    partner = {"row": row + 1 - 2 * lax.rem(row, 2)}
    right = {"dp": lax.rem(me + 1, n)}
    left = {"dp": lax.rem(me + n - 1, n)}
    barrier = pltpu.get_barrier_semaphore()
    for peer in (right, left, partner):
        pl.semaphore_signal(barrier, inc=1, device_id=peer, device_id_type=MESH)
    pl.semaphore_wait(barrier, 3)
    sends = []

    def send(src, dst, send_sems, recv_sems, slot, peer):
        copy = pltpu.make_async_remote_copy(
            src_ref=src,
            dst_ref=dst.at[slot],
            send_sem=send_sems.at[len(sends)],
            recv_sem=recv_sems.at[slot],
            device_id=peer,
            device_id_type=MESH,
        )
        copy.start()
        sends.append(copy)

    def arrived(slot):
        pltpu.make_async_remote_copy(
            src_ref=mine_ref,
            dst_ref=held_ref.at[slot],
            send_sem=send_sem.at[0],
            recv_sem=recv_sem.at[slot],
            device_id=right,
            device_id_type=MESH,
        ).wait_recv()

    to_right = n // 2
    to_left = n - 1 - to_right
    send(mine_ref, held_ref, send_sem, recv_sem, me, right)
    send(mine_ref, held_ref, send_sem, recv_sem, me, left)
    held_ref[me] = mine_ref[...]
    landed = []
    for k in range(1, max(to_right, to_left) + 1):
        if k <= to_right:
            origin = lax.rem(me + n - k, n)
            arrived(origin)
            if k < to_right:
                send(held_ref.at[origin], held_ref, send_sem, recv_sem, origin, right)
            landed.append(origin)
        if k <= to_left:
            origin = lax.rem(me + k, n)
            arrived(origin)
            if k < to_left:
                send(held_ref.at[origin], held_ref, send_sem, recv_sem, origin, left)
            landed.append(origin)
    send(mine_ref, other_ref, pass_send, pass_recv, me, partner)
    for origin in landed:
        send(held_ref.at[origin], other_ref, pass_send, pass_recv, origin, partner)
    for slot in range(n):
        pltpu.make_async_remote_copy(
            src_ref=mine_ref,
            dst_ref=other_ref.at[slot],
            send_sem=pass_send.at[0],
            recv_sem=pass_recv.at[slot],
            device_id=partner,
            device_id_type=MESH,
        ).wait_recv()
    for copy in sends:
        copy.wait_send()


def gathered_weights(proj_in, proj_out):
    n = lax.axis_size("dp")
    first_core = lax.rem(lax.axis_index("row"), 2) == 0
    mine = jnp.where(first_core, proj_in.T, proj_out)
    part, channels = mine.shape
    vmem = pl.BlockSpec(memory_space=pltpu.VMEM)
    gathered = jax.ShapeDtypeStruct((n, part, channels), mine.dtype)
    held, other = pl.pallas_call(
        functools.partial(_gather_kernel, n),
        out_shape=[gathered, gathered],
        in_specs=[vmem],
        out_specs=[vmem, vmem],
        scratch_shapes=[
            pltpu.SemaphoreType.DMA((2 * n,)),
            pltpu.SemaphoreType.DMA((n,)),
            pltpu.SemaphoreType.DMA((2 * n,)),
            pltpu.SemaphoreType.DMA((n,)),
        ],
        compiler_params=pltpu.CompilerParams(collective_id=7, has_side_effects=True),
    )(mine)
    return held.reshape(n * part, channels), other.reshape(n * part, channels)


def on_device(
    inputs,
    depth_kernel,
    depth_bias,
    norm_gain,
    norm_bias,
    proj_in,
    bias_in,
    grn_gamma,
    grn_beta,
    proj_out,
    bias_out,
):
    fresh = extended(inputs[:, 0], (("row", 1),), 3)
    proj_in, proj_out = gathered_weights(proj_in[0], proj_out[0])
    sections = lax.axis_size("section")
    section_index = lax.axis_index("section")
    num_micro = inputs.shape[0]
    own_params = (
        depth_kernel[0],
        depth_bias[0],
        norm_gain[0],
        norm_bias[0],
        proj_in,
        bias_in[0],
        grn_gamma[0],
        grn_beta[0],
        proj_out,
        bias_out[0],
    )
    num_ticks = num_micro + sections - 1
    current = fresh[:1]
    outputs = []
    for tick_index in range(num_ticks):
        hand_on = tick_index + 1 < num_ticks
        produced, current = conv_block(
            current, fresh, min(tick_index + 1, num_micro - 1), own_params, hand_on
        )
        outputs.append(produced)
    stacked = jnp.stack(outputs)
    saved = lax.dynamic_slice_in_dim(stacked, section_index, num_micro, axis=0)
    return saved[None]


def solution(mesh):
    return jax.shard_map(
        on_device,
        mesh=mesh,
        in_specs=(
            P(None, "dp", "row", None, None),
            P("section", None, None, None),
            P("section", None),
            P("section", None),
            P("section", None),
            P("section", None, "dp"),
            P("section", None),
            P("section", None),
            P("section", None),
            P("section", "dp", None),
            P("section", None),
        ),
        out_specs=P("section", None, "dp", "row", None, None),
        check_vma=False,
    )
```

```python
import functools
import math

import jax
import jax.numpy as jnp
from jax import lax
from jax.experimental import pallas as pl
from jax.experimental.pallas import tpu as pltpu
from jax.sharding import PartitionSpec as P

MESH = pl.DeviceIdType.MESH

EPS_NORM = 1e-06
EPS_GRN = 1e-06


def extended(cells, sides, width):
    for axis, dim in sides:
        count = lax.axis_size(axis)
        ends = count - 1
        head = lax.slice_in_dim(cells, 0, width, axis=dim)
        tail = lax.slice_in_dim(cells, cells.shape[dim] - width, cells.shape[dim], axis=dim)
        cells = jnp.concatenate(
            [
                lax.ppermute(tail, axis, [(i, (i + 1) % count) for i in range(ends)]),
                cells,
                lax.ppermute(head, axis, [((i + 1) % count, i) for i in range(ends)]),
            ],
            axis=dim,
        )
    return cells


def _pointwise_kernel(
    n,
    sections,
    hand_on,
    fresh_index,
    padded_ref,
    fresh_ref,
    held_ref,
    other_ref,
    bias_in_ref,
    gamma_ref,
    beta_ref,
    bias_out_ref,
    taps_ref,
    depth_bias_ref,
    gain_ref,
    shift_ref,
    out_ref,
    *rest,
):
    if hand_on:
        next_ref, wide_ref, normed_ref, act_ref, slots, send_sem, recv_sem = rest[:7]
        hand_send, hand_recv, fresh_sem = rest[7:]
    else:
        wide_ref, normed_ref, act_ref, slots, send_sem, recv_sem = rest
    me = lax.axis_index("row")
    section = lax.axis_index("section")
    barrier = pltpu.get_barrier_semaphore()
    for k in range(1, n):
        pl.semaphore_signal(
            barrier, inc=1, device_id={"row": lax.rem(me + k, n)}, device_id_type=MESH
        )
    waits = n - 1
    if hand_on:
        cells = out_ref.shape[0]
        edge = 3 * cells // 4
        has_above = me > 0
        has_below = me < n - 1
        has_prev = section > 0
        has_next = section < sections - 1
        @pl.when(has_prev)
        def _():
            pl.semaphore_signal(
                barrier, inc=1, device_id={"section": section - 1}, device_id_type=MESH
            )

        waits = waits + has_next.astype(jnp.int32)
    padded_rows, margin_cols, channels = wide_ref.shape
    cols = padded_ref.shape[0] // padded_rows
    out_rows = padded_rows - 6
    zeros = jnp.zeros((8, channels), jnp.float32)
    for r in range(padded_rows):
        wide_ref[r, pl.ds(0, 8), :] = zeros
        wide_ref[r, pl.ds(8, cols), :] = padded_ref[pl.ds(r * cols, cols), :].astype(jnp.float32)
        wide_ref[r, pl.ds(8 + cols, margin_cols - 8 - cols), :] = zeros[: margin_cols - 8 - cols]

    def conv_row(h, carry):
        acc = jnp.broadcast_to(depth_bias_ref[...].astype(jnp.float32), (cols, channels))
        for i in range(7):
            for j in range(7):
                tap = taps_ref[pl.ds(i * 7 + j, 1), :].astype(jnp.float32)
                acc = acc + wide_ref[h + i, pl.ds(j + 5, cols), :] * tap
        mean = jnp.mean(acc, axis=-1, keepdims=True)
        center = acc - mean
        spread = jnp.mean(center * center, axis=-1, keepdims=True)
        normed = (
            center * lax.rsqrt(spread + EPS_NORM) * gain_ref[...].astype(jnp.float32)
            + shift_ref[...].astype(jnp.float32)
        )
        normed_ref[pl.ds(pl.multiple_of(h * cols, 16), cols), :] = normed.astype(normed_ref.dtype)
        return carry

    lax.fori_loop(0, out_rows, conv_row, 0)
    first_core = lax.rem(me, 2) == 0

    def raise_with(proj_in_t_ref):
        raised = lax.dot_general(
            normed_ref[...],
            proj_in_t_ref[...],
            (((1,), (1,)), ((), ())),
            preferred_element_type=jnp.float32,
        ) + bias_in_ref[...].astype(jnp.float32)
        act_ref[...] = (0.5 * raised * (1.0 + lax.erf(raised * (1.0 / math.sqrt(2.0))))).astype(
            jnp.bfloat16
        )

    pl.when(first_core)(lambda: raise_with(held_ref))
    pl.when(jnp.logical_not(first_core))(lambda: raise_with(other_ref))
    grouped = act_ref[...].astype(jnp.float32)
    slots[me] = jnp.sum(grouped * grouped, axis=0, keepdims=True)
    pl.semaphore_wait(barrier, waits)
    sends = []
    for k in range(1, n):
        copy = pltpu.make_async_remote_copy(
            src_ref=slots.at[me],
            dst_ref=slots.at[me],
            send_sem=send_sem.at[k],
            recv_sem=recv_sem.at[me],
            device_id={"row": lax.rem(me + k, n)},
            device_id_type=MESH,
        )
        copy.start()
        sends.append(copy)
    if hand_on:
        @pl.when(section == 0)
        def _():
            fresh_copy = pltpu.make_async_copy(fresh_ref.at[fresh_index], next_ref, fresh_sem)
            fresh_copy.start()
            fresh_copy.wait()

        @pl.when(jnp.logical_and(has_prev, jnp.logical_not(has_above)))
        def _():
            next_ref[pl.ds(0, edge), :] = jnp.zeros((edge, next_ref.shape[1]), next_ref.dtype)

        @pl.when(jnp.logical_and(has_prev, jnp.logical_not(has_below)))
        def _():
            next_ref[pl.ds(edge + cells, edge), :] = jnp.zeros(
                (edge, next_ref.shape[1]), next_ref.dtype
            )

    for k in range(1, n):
        src = lax.rem(me + k, n)
        pltpu.make_async_remote_copy(
            src_ref=slots.at[src],
            dst_ref=slots.at[src],
            send_sem=send_sem.at[k],
            recv_sem=recv_sem.at[src],
            device_id={"row": src},
            device_id_type=MESH,
        ).wait_recv()
    for copy in sends:
        copy.wait_send()
    total_sq = slots[0]
    for j in range(1, n):
        total_sq = total_sq + slots[j]
    magnitude = jnp.sqrt(total_sq)
    grn_ratio = magnitude / (jnp.mean(magnitude, axis=-1, keepdims=True) + EPS_GRN)
    grouped = act_ref[...].astype(jnp.float32)
    hidden = (
        gamma_ref[...].astype(jnp.float32) * grouped * grn_ratio
        + beta_ref[...].astype(jnp.float32)
        + grouped
    ).astype(jnp.bfloat16)
    cells = out_ref.shape[0]
    edge = 3 * cells // 4

    def lower_with(proj_out_ref):
        update = jnp.dot(
            hidden, proj_out_ref[...], preferred_element_type=jnp.float32
        ) + bias_out_ref[...].astype(jnp.float32)
        current = padded_ref[pl.ds(edge, cells), :].astype(jnp.float32)
        out_ref[...] = (current + update).astype(out_ref.dtype)

    pl.when(first_core)(lambda: lower_with(other_ref))
    pl.when(jnp.logical_not(first_core))(lambda: lower_with(held_ref))
    if not hand_on:
        return
    own_rows = pl.ds(edge, cells)
    handed = pltpu.make_async_remote_copy(
        src_ref=out_ref,
        dst_ref=next_ref.at[own_rows],
        send_sem=hand_send.at[1],
        recv_sem=hand_recv.at[1],
        device_id={"section": section + 1},
        device_id_type=MESH,
    )

    @pl.when(has_next)
    def _():
        handed.start()

    halos = (
        (2, pl.ds(edge, edge), pl.ds(edge + cells, edge), -1, has_above),
        (0, pl.ds(cells, edge), pl.ds(0, edge), 1, has_below),
    )

    def halo_copy(slot, src, dst, peer_row):
        return pltpu.make_async_remote_copy(
            src_ref=next_ref.at[src],
            dst_ref=next_ref.at[dst],
            send_sem=hand_send.at[slot],
            recv_sem=hand_recv.at[slot],
            device_id={"row": peer_row},
            device_id_type=MESH,
        )

    @pl.when(has_prev)
    def _():
        handed.wait_recv()
        for slot, src, dst, shift, cond in halos:
            @pl.when(cond)
            def _():
                halo_copy(slot, src, dst, me + shift).start()

        for slot, src, dst, shift, cond in halos:
            @pl.when(halos[slot // 2][4])
            def _():
                halo_copy(slot, src, dst, me).wait_recv()

        for slot, src, dst, shift, cond in halos:
            @pl.when(cond)
            def _():
                halo_copy(slot, src, dst, me + shift).wait_send()

    @pl.when(has_next)
    def _():
        handed.wait_send()


def pointwise(
    padded,
    fresh,
    fresh_index,
    held,
    other,
    bias_in,
    grn_gamma,
    grn_beta,
    bias_out,
    depth_kernel,
    depth_bias,
    norm_gain,
    norm_bias,
    cols,
    hand_on,
):
    n = lax.axis_size("row")
    sections = lax.axis_size("section")
    channels = padded.shape[1]
    padded_rows = padded.shape[0] // cols
    cells = (padded_rows - 6) * cols
    hidden_units = held.shape[0]
    vmem = pl.BlockSpec(memory_space=pltpu.VMEM)
    out_shape = [jax.ShapeDtypeStruct((cells, channels), padded.dtype)]
    scratch = [
        pltpu.VMEM((padded_rows, -(-(cols + 11) // 8) * 8, channels), jnp.float32),
        pltpu.VMEM((cells, channels), jnp.bfloat16),
        pltpu.VMEM((cells, hidden_units), jnp.bfloat16),
        pltpu.VMEM((n, 1, hidden_units), jnp.float32),
        pltpu.SemaphoreType.DMA((n,)),
        pltpu.SemaphoreType.DMA((n,)),
    ]
    if hand_on:
        out_shape.append(jax.ShapeDtypeStruct(fresh.shape[1:], fresh.dtype))
        scratch += [
            pltpu.SemaphoreType.DMA((3,)),
            pltpu.SemaphoreType.DMA((3,)),
            pltpu.SemaphoreType.DMA(()),
        ]
    return pl.pallas_call(
        functools.partial(_pointwise_kernel, n, sections, hand_on, fresh_index),
        out_shape=out_shape,
        in_specs=[vmem, pl.BlockSpec(memory_space=pl.ANY)] + [vmem] * 10,
        out_specs=[vmem] * len(out_shape),
        scratch_shapes=scratch,
        compiler_params=pltpu.CompilerParams(
            collective_id=1 + fresh_index if hand_on else 0, has_side_effects=True
        ),
        cost_estimate=pl.CostEstimate(
            flops=4 * cells * channels * hidden_units,
            transcendentals=cells * hidden_units,
            bytes_accessed=4 * channels * hidden_units + 8 * cells * channels,
        ),
    )(
        padded,
        fresh,
        held,
        other,
        bias_in.reshape(1, -1),
        grn_gamma.reshape(1, -1),
        grn_beta.reshape(1, -1),
        bias_out.reshape(1, -1),
        depth_kernel.reshape(-1, channels),
        depth_bias.reshape(1, -1),
        norm_gain.reshape(1, -1),
        norm_bias.reshape(1, -1),
    )


def passed_along(x, axis, by):
    count = lax.axis_size(axis)
    pairs = [(i, i + by) for i in range(count) if 0 <= i + by < count]
    return lax.ppermute(x, axis, pairs)


def depthwise(padded, kernel, bias_term):
    channels = padded.shape[-1]
    conv_out = lax.conv_general_dilated(
        padded.astype(jnp.float32),
        kernel.astype(jnp.float32)[:, :, None, :],
        (1, 1),
        "VALID",
        dimension_numbers=("NHWC", "HWIO", "NHWC"),
        feature_group_count=channels,
        precision=lax.Precision.HIGHEST,
    )
    return conv_out + bias_term.astype(jnp.float32)


def conv_block(padded, fresh, fresh_index, params, hand_on):
    (
        depth_kernel,
        depth_bias,
        norm_gain,
        norm_bias,
        proj_in,
        bias_in,
        grn_gamma,
        grn_beta,
        proj_out,
        bias_out,
    ) = params
    num_items, padded_rows, num_cols, channels = padded.shape
    results = pointwise(
        padded.reshape(-1, channels),
        fresh.reshape(fresh.shape[0], -1, channels),
        fresh_index,
        proj_in,
        proj_out,
        bias_in,
        grn_gamma,
        grn_beta,
        bias_out,
        depth_kernel,
        depth_bias,
        norm_gain,
        norm_bias,
        num_cols,
        hand_on,
    )
    produced = results[0].reshape(num_items, padded_rows - 6, num_cols, channels)
    arriving = results[1].reshape(padded.shape) if hand_on else None
    return produced, arriving


def _gather_kernel(n, chunks, mine_ref, held_ref, other_ref, send_sem, recv_sem, pass_send, pass_recv):
    me = lax.axis_index("dp")
    row = lax.axis_index("row")
    partner = {"row": row + 1 - 2 * lax.rem(row, 2)}
    right = {"dp": lax.rem(me + 1, n)}
    left = {"dp": lax.rem(me + n - 1, n)}
    barrier = pltpu.get_barrier_semaphore()
    for peer in (right, left, partner):
        pl.semaphore_signal(barrier, inc=1, device_id=peer, device_id_type=MESH)
    pl.semaphore_wait(barrier, 3)
    sends = []
    parts = len(chunks)

    def send(src, dst, send_sems, recv_sems, slot, c, peer):
        copy = pltpu.make_async_remote_copy(
            src_ref=src.at[chunks[c]],
            dst_ref=dst.at[slot, chunks[c]],
            send_sem=send_sems.at[len(sends)],
            recv_sem=recv_sems.at[slot * parts + c],
            device_id=peer,
            device_id_type=MESH,
        )
        copy.start()
        sends.append(copy)

    def arrived(dst, recv_sems, slot, c):
        pltpu.make_async_remote_copy(
            src_ref=mine_ref.at[chunks[c]],
            dst_ref=dst.at[slot, chunks[c]],
            send_sem=send_sem.at[0],
            recv_sem=recv_sems.at[slot * parts + c],
            device_id=right,
            device_id_type=MESH,
        ).wait_recv()

    to_right = n // 2
    to_left = n - 1 - to_right
    for c in range(parts):
        send(mine_ref, held_ref, send_sem, recv_sem, me, c, right)
        send(mine_ref, held_ref, send_sem, recv_sem, me, c, left)
    for c in range(parts):
        send(mine_ref, other_ref, pass_send, pass_recv, me, c, partner)
    held_ref[me] = mine_ref[...]
    for k in range(1, max(to_right, to_left) + 1):
        for c in range(parts):
            for steps, way, peer in ((to_right, -1, right), (to_left, 1, left)):
                if k > steps:
                    continue
                origin = lax.rem(me + n + way * k, n)
                arrived(held_ref, recv_sem, origin, c)
                if k < steps:
                    send(held_ref.at[origin], held_ref, send_sem, recv_sem, origin, c, peer)
                send(held_ref.at[origin], other_ref, pass_send, pass_recv, origin, c, partner)
    for slot in range(n):
        for c in range(parts):
            arrived(other_ref, pass_recv, slot, c)
    for copy in sends:
        copy.wait_send()


def gathered_weights(proj_in, proj_out):
    n = lax.axis_size("dp")
    first_core = lax.rem(lax.axis_index("row"), 2) == 0
    mine = jnp.where(first_core, proj_in.T, proj_out)
    part, channels = mine.shape
    vmem = pl.BlockSpec(memory_space=pltpu.VMEM)
    gathered = jax.ShapeDtypeStruct((n, part, channels), mine.dtype)
    held, other = pl.pallas_call(
        functools.partial(_gather_kernel, n, (pl.ds(0, 96), pl.ds(96, part - 96))),
        out_shape=[gathered, gathered],
        in_specs=[vmem],
        out_specs=[vmem, vmem],
        scratch_shapes=[
            pltpu.SemaphoreType.DMA((4 * n,)),
            pltpu.SemaphoreType.DMA((2 * n,)),
            pltpu.SemaphoreType.DMA((4 * n,)),
            pltpu.SemaphoreType.DMA((2 * n,)),
        ],
        compiler_params=pltpu.CompilerParams(collective_id=7, has_side_effects=True),
    )(mine)
    return held.reshape(n * part, channels), other.reshape(n * part, channels)


def on_device(
    inputs,
    depth_kernel,
    depth_bias,
    norm_gain,
    norm_bias,
    proj_in,
    bias_in,
    grn_gamma,
    grn_beta,
    proj_out,
    bias_out,
):
    fresh = extended(inputs[:, 0], (("row", 1),), 3)
    proj_in, proj_out = gathered_weights(proj_in[0], proj_out[0])
    sections = lax.axis_size("section")
    section_index = lax.axis_index("section")
    num_micro = inputs.shape[0]
    own_params = (
        depth_kernel[0],
        depth_bias[0],
        norm_gain[0],
        norm_bias[0],
        proj_in,
        bias_in[0],
        grn_gamma[0],
        grn_beta[0],
        proj_out,
        bias_out[0],
    )
    num_ticks = num_micro + sections - 1
    current = fresh[:1]
    outputs = []
    for tick_index in range(num_ticks):
        hand_on = tick_index + 1 < num_ticks
        produced, current = conv_block(
            current, fresh, min(tick_index + 1, num_micro - 1), own_params, hand_on
        )
        outputs.append(produced)
    stacked = jnp.stack(outputs)
    saved = lax.dynamic_slice_in_dim(stacked, section_index, num_micro, axis=0)
    return saved[None]


def solution(mesh):
    return jax.shard_map(
        on_device,
        mesh=mesh,
        in_specs=(
            P(None, "dp", "row", None, None),
            P("section", None, None, None),
            P("section", None),
            P("section", None),
            P("section", None),
            P("section", None, "dp"),
            P("section", None),
            P("section", None),
            P("section", None),
            P("section", "dp", None),
            P("section", None),
        ),
        out_specs=P("section", None, "dp", "row", None, None),
        check_vma=False,
    )
```

```python
import functools
import math

import jax
import jax.numpy as jnp
from jax import lax
from jax.experimental import pallas as pl
from jax.experimental.pallas import tpu as pltpu
from jax.sharding import PartitionSpec as P

MESH = pl.DeviceIdType.MESH

EPS_NORM = 1e-06
EPS_GRN = 1e-06


def extended(cells, sides, width):
    for axis, dim in sides:
        count = lax.axis_size(axis)
        ends = count - 1
        head = lax.slice_in_dim(cells, 0, width, axis=dim)
        tail = lax.slice_in_dim(cells, cells.shape[dim] - width, cells.shape[dim], axis=dim)
        cells = jnp.concatenate(
            [
                lax.ppermute(tail, axis, [(i, (i + 1) % count) for i in range(ends)]),
                cells,
                lax.ppermute(head, axis, [((i + 1) % count, i) for i in range(ends)]),
            ],
            axis=dim,
        )
    return cells


def _pointwise_kernel(
    n,
    sections,
    hand_on,
    fresh_index,
    padded_ref,
    fresh_ref,
    held_ref,
    other_ref,
    bias_in_ref,
    gamma_ref,
    beta_ref,
    bias_out_ref,
    taps_ref,
    depth_bias_ref,
    gain_ref,
    shift_ref,
    out_ref,
    *rest,
):
    if hand_on:
        next_ref, wide_ref, conv_ref, normed_ref, act_ref, slots, send_sem, recv_sem = rest[:8]
        hand_send, hand_recv, fresh_sem = rest[8:]
    else:
        wide_ref, conv_ref, normed_ref, act_ref, slots, send_sem, recv_sem = rest
    me = lax.axis_index("row")
    section = lax.axis_index("section")
    barrier = pltpu.get_barrier_semaphore()
    for k in range(1, n):
        pl.semaphore_signal(
            barrier, inc=1, device_id={"row": lax.rem(me + k, n)}, device_id_type=MESH
        )
    waits = n - 1
    if hand_on:
        cells = out_ref.shape[0]
        edge = 3 * cells // 4
        has_above = me > 0
        has_below = me < n - 1
        has_prev = section > 0
        has_next = section < sections - 1
        @pl.when(has_prev)
        def _():
            pl.semaphore_signal(
                barrier, inc=1, device_id={"section": section - 1}, device_id_type=MESH
            )

        waits = waits + has_next.astype(jnp.int32)
    padded_rows, margin_cols, channels = wide_ref.shape
    cols = padded_ref.shape[0] // padded_rows
    out_rows = padded_rows - 6
    zeros = jnp.zeros((8, channels), jnp.float32)
    for r in range(padded_rows):
        wide_ref[r, pl.ds(0, 8), :] = zeros
        wide_ref[r, pl.ds(8, cols), :] = padded_ref[pl.ds(r * cols, cols), :].astype(jnp.float32)
        wide_ref[r, pl.ds(8 + cols, margin_cols - 8 - cols), :] = zeros[: margin_cols - 8 - cols]

    for start in range(0, channels, 128):
        lanes = pl.ds(start, min(128, channels - start))
        acc = [
            jnp.broadcast_to(
                depth_bias_ref[:, lanes].astype(jnp.float32), (cols, min(128, channels - start))
            )
            for h in range(out_rows)
        ]
        for r in range(padded_rows):
            for j in range(7):
                slab = wide_ref[r, pl.ds(j + 5, cols), lanes]
                for h in range(out_rows):
                    i = r - h
                    if 0 <= i < 7:
                        tap = taps_ref[pl.ds(i * 7 + j, 1), lanes].astype(jnp.float32)
                        acc[h] = acc[h] + slab * tap
        for h in range(out_rows):
            conv_ref[h, :, lanes] = acc[h]

    def norm_row(h, carry):
        acc = conv_ref[h]
        mean = jnp.mean(acc, axis=-1, keepdims=True)
        center = acc - mean
        spread = jnp.mean(center * center, axis=-1, keepdims=True)
        normed = (
            center * lax.rsqrt(spread + EPS_NORM) * gain_ref[...].astype(jnp.float32)
            + shift_ref[...].astype(jnp.float32)
        )
        normed_ref[pl.ds(pl.multiple_of(h * cols, 16), cols), :] = normed.astype(normed_ref.dtype)
        return carry

    lax.fori_loop(0, out_rows, norm_row, 0)
    first_core = lax.rem(me, 2) == 0

    def raise_with(proj_in_t_ref):
        raised = lax.dot_general(
            normed_ref[...],
            proj_in_t_ref[...],
            (((1,), (1,)), ((), ())),
            preferred_element_type=jnp.float32,
        ) + bias_in_ref[...].astype(jnp.float32)
        act_ref[...] = (0.5 * raised * (1.0 + lax.erf(raised * (1.0 / math.sqrt(2.0))))).astype(
            jnp.bfloat16
        )

    pl.when(first_core)(lambda: raise_with(held_ref))
    pl.when(jnp.logical_not(first_core))(lambda: raise_with(other_ref))
    grouped = act_ref[...].astype(jnp.float32)
    slots[me] = jnp.sum(grouped * grouped, axis=0, keepdims=True)
    pl.semaphore_wait(barrier, waits)
    sends = []
    for k in range(1, n):
        copy = pltpu.make_async_remote_copy(
            src_ref=slots.at[me],
            dst_ref=slots.at[me],
            send_sem=send_sem.at[k],
            recv_sem=recv_sem.at[me],
            device_id={"row": lax.rem(me + k, n)},
            device_id_type=MESH,
        )
        copy.start()
        sends.append(copy)
    if hand_on:
        @pl.when(section == 0)
        def _():
            fresh_copy = pltpu.make_async_copy(fresh_ref.at[fresh_index], next_ref, fresh_sem)
            fresh_copy.start()
            fresh_copy.wait()

        @pl.when(jnp.logical_and(has_prev, jnp.logical_not(has_above)))
        def _():
            next_ref[pl.ds(0, edge), :] = jnp.zeros((edge, next_ref.shape[1]), next_ref.dtype)

        @pl.when(jnp.logical_and(has_prev, jnp.logical_not(has_below)))
        def _():
            next_ref[pl.ds(edge + cells, edge), :] = jnp.zeros(
                (edge, next_ref.shape[1]), next_ref.dtype
            )

    for k in range(1, n):
        src = lax.rem(me + k, n)
        pltpu.make_async_remote_copy(
            src_ref=slots.at[src],
            dst_ref=slots.at[src],
            send_sem=send_sem.at[k],
            recv_sem=recv_sem.at[src],
            device_id={"row": src},
            device_id_type=MESH,
        ).wait_recv()
    for copy in sends:
        copy.wait_send()
    total_sq = slots[0]
    for j in range(1, n):
        total_sq = total_sq + slots[j]
    magnitude = jnp.sqrt(total_sq)
    grn_ratio = magnitude / (jnp.mean(magnitude, axis=-1, keepdims=True) + EPS_GRN)
    grouped = act_ref[...].astype(jnp.float32)
    hidden = (
        gamma_ref[...].astype(jnp.float32) * grouped * grn_ratio
        + beta_ref[...].astype(jnp.float32)
        + grouped
    ).astype(jnp.bfloat16)
    cells = out_ref.shape[0]
    edge = 3 * cells // 4

    def lower_with(proj_out_ref):
        update = jnp.dot(
            hidden, proj_out_ref[...], preferred_element_type=jnp.float32
        ) + bias_out_ref[...].astype(jnp.float32)
        current = padded_ref[pl.ds(edge, cells), :].astype(jnp.float32)
        out_ref[...] = (current + update).astype(out_ref.dtype)

    pl.when(first_core)(lambda: lower_with(other_ref))
    pl.when(jnp.logical_not(first_core))(lambda: lower_with(held_ref))
    if not hand_on:
        return
    own_rows = pl.ds(edge, cells)
    handed = pltpu.make_async_remote_copy(
        src_ref=out_ref,
        dst_ref=next_ref.at[own_rows],
        send_sem=hand_send.at[1],
        recv_sem=hand_recv.at[1],
        device_id={"section": section + 1},
        device_id_type=MESH,
    )

    @pl.when(has_next)
    def _():
        handed.start()

    halos = (
        (2, pl.ds(edge, edge), pl.ds(edge + cells, edge), -1, has_above),
        (0, pl.ds(cells, edge), pl.ds(0, edge), 1, has_below),
    )

    def halo_copy(slot, src, dst, peer_row):
        return pltpu.make_async_remote_copy(
            src_ref=next_ref.at[src],
            dst_ref=next_ref.at[dst],
            send_sem=hand_send.at[slot],
            recv_sem=hand_recv.at[slot],
            device_id={"row": peer_row},
            device_id_type=MESH,
        )

    @pl.when(has_prev)
    def _():
        handed.wait_recv()
        for slot, src, dst, shift, cond in halos:
            @pl.when(cond)
            def _():
                halo_copy(slot, src, dst, me + shift).start()

        for slot, src, dst, shift, cond in halos:
            @pl.when(halos[slot // 2][4])
            def _():
                halo_copy(slot, src, dst, me).wait_recv()

        for slot, src, dst, shift, cond in halos:
            @pl.when(cond)
            def _():
                halo_copy(slot, src, dst, me + shift).wait_send()

    @pl.when(has_next)
    def _():
        handed.wait_send()


def pointwise(
    padded,
    fresh,
    fresh_index,
    held,
    other,
    bias_in,
    grn_gamma,
    grn_beta,
    bias_out,
    depth_kernel,
    depth_bias,
    norm_gain,
    norm_bias,
    cols,
    hand_on,
):
    n = lax.axis_size("row")
    sections = lax.axis_size("section")
    channels = padded.shape[1]
    padded_rows = padded.shape[0] // cols
    cells = (padded_rows - 6) * cols
    hidden_units = held.shape[0]
    vmem = pl.BlockSpec(memory_space=pltpu.VMEM)
    out_shape = [jax.ShapeDtypeStruct((cells, channels), padded.dtype)]
    scratch = [
        pltpu.VMEM((padded_rows, -(-(cols + 11) // 8) * 8, channels), jnp.float32),
        pltpu.VMEM((padded_rows - 6, cols, channels), jnp.float32),
        pltpu.VMEM((cells, channels), jnp.bfloat16),
        pltpu.VMEM((cells, hidden_units), jnp.bfloat16),
        pltpu.VMEM((n, 1, hidden_units), jnp.float32),
        pltpu.SemaphoreType.DMA((n,)),
        pltpu.SemaphoreType.DMA((n,)),
    ]
    if hand_on:
        out_shape.append(jax.ShapeDtypeStruct(fresh.shape[1:], fresh.dtype))
        scratch += [
            pltpu.SemaphoreType.DMA((3,)),
            pltpu.SemaphoreType.DMA((3,)),
            pltpu.SemaphoreType.DMA(()),
        ]
    return pl.pallas_call(
        functools.partial(_pointwise_kernel, n, sections, hand_on, fresh_index),
        out_shape=out_shape,
        in_specs=[vmem, pl.BlockSpec(memory_space=pl.ANY)] + [vmem] * 10,
        out_specs=[vmem] * len(out_shape),
        scratch_shapes=scratch,
        compiler_params=pltpu.CompilerParams(
            collective_id=1 + fresh_index if hand_on else 0, has_side_effects=True
        ),
        cost_estimate=pl.CostEstimate(
            flops=4 * cells * channels * hidden_units,
            transcendentals=cells * hidden_units,
            bytes_accessed=4 * channels * hidden_units + 8 * cells * channels,
        ),
    )(
        padded,
        fresh,
        held,
        other,
        bias_in.reshape(1, -1),
        grn_gamma.reshape(1, -1),
        grn_beta.reshape(1, -1),
        bias_out.reshape(1, -1),
        depth_kernel.reshape(-1, channels),
        depth_bias.reshape(1, -1),
        norm_gain.reshape(1, -1),
        norm_bias.reshape(1, -1),
    )


def passed_along(x, axis, by):
    count = lax.axis_size(axis)
    pairs = [(i, i + by) for i in range(count) if 0 <= i + by < count]
    return lax.ppermute(x, axis, pairs)


def depthwise(padded, kernel, bias_term):
    channels = padded.shape[-1]
    conv_out = lax.conv_general_dilated(
        padded.astype(jnp.float32),
        kernel.astype(jnp.float32)[:, :, None, :],
        (1, 1),
        "VALID",
        dimension_numbers=("NHWC", "HWIO", "NHWC"),
        feature_group_count=channels,
        precision=lax.Precision.HIGHEST,
    )
    return conv_out + bias_term.astype(jnp.float32)


def conv_block(padded, fresh, fresh_index, params, hand_on):
    (
        depth_kernel,
        depth_bias,
        norm_gain,
        norm_bias,
        proj_in,
        bias_in,
        grn_gamma,
        grn_beta,
        proj_out,
        bias_out,
    ) = params
    num_items, padded_rows, num_cols, channels = padded.shape
    results = pointwise(
        padded.reshape(-1, channels),
        fresh.reshape(fresh.shape[0], -1, channels),
        fresh_index,
        proj_in,
        proj_out,
        bias_in,
        grn_gamma,
        grn_beta,
        bias_out,
        depth_kernel,
        depth_bias,
        norm_gain,
        norm_bias,
        num_cols,
        hand_on,
    )
    produced = results[0].reshape(num_items, padded_rows - 6, num_cols, channels)
    arriving = results[1].reshape(padded.shape) if hand_on else None
    return produced, arriving


def _gather_kernel(n, chunks, mine_ref, held_ref, other_ref, send_sem, recv_sem, pass_send, pass_recv):
    me = lax.axis_index("dp")
    row = lax.axis_index("row")
    partner = {"row": row + 1 - 2 * lax.rem(row, 2)}
    right = {"dp": lax.rem(me + 1, n)}
    left = {"dp": lax.rem(me + n - 1, n)}
    barrier = pltpu.get_barrier_semaphore()
    for peer in (right, left, partner):
        pl.semaphore_signal(barrier, inc=1, device_id=peer, device_id_type=MESH)
    pl.semaphore_wait(barrier, 3)
    sends = []
    parts = len(chunks)

    def send(src, dst, send_sems, recv_sems, slot, c, peer):
        copy = pltpu.make_async_remote_copy(
            src_ref=src.at[chunks[c]],
            dst_ref=dst.at[slot, chunks[c]],
            send_sem=send_sems.at[len(sends)],
            recv_sem=recv_sems.at[slot * parts + c],
            device_id=peer,
            device_id_type=MESH,
        )
        copy.start()
        sends.append(copy)

    def arrived(dst, recv_sems, slot, c):
        pltpu.make_async_remote_copy(
            src_ref=mine_ref.at[chunks[c]],
            dst_ref=dst.at[slot, chunks[c]],
            send_sem=send_sem.at[0],
            recv_sem=recv_sems.at[slot * parts + c],
            device_id=right,
            device_id_type=MESH,
        ).wait_recv()

    to_right = n // 2
    to_left = n - 1 - to_right
    for c in range(parts):
        send(mine_ref, held_ref, send_sem, recv_sem, me, c, right)
        send(mine_ref, held_ref, send_sem, recv_sem, me, c, left)
    for c in range(parts):
        send(mine_ref, other_ref, pass_send, pass_recv, me, c, partner)
    held_ref[me] = mine_ref[...]
    for k in range(1, max(to_right, to_left) + 1):
        for c in range(parts):
            for steps, way, peer in ((to_right, -1, right), (to_left, 1, left)):
                if k > steps:
                    continue
                origin = lax.rem(me + n + way * k, n)
                arrived(held_ref, recv_sem, origin, c)
                if k < steps:
                    send(held_ref.at[origin], held_ref, send_sem, recv_sem, origin, c, peer)
                send(held_ref.at[origin], other_ref, pass_send, pass_recv, origin, c, partner)
    for slot in range(n):
        for c in range(parts):
            arrived(other_ref, pass_recv, slot, c)
    for copy in sends:
        copy.wait_send()


def gathered_weights(proj_in, proj_out):
    n = lax.axis_size("dp")
    first_core = lax.rem(lax.axis_index("row"), 2) == 0
    mine = jnp.where(first_core, proj_in.T, proj_out)
    part, channels = mine.shape
    vmem = pl.BlockSpec(memory_space=pltpu.VMEM)
    gathered = jax.ShapeDtypeStruct((n, part, channels), mine.dtype)
    held, other = pl.pallas_call(
        functools.partial(_gather_kernel, n, (pl.ds(0, 96), pl.ds(96, part - 96))),
        out_shape=[gathered, gathered],
        in_specs=[vmem],
        out_specs=[vmem, vmem],
        scratch_shapes=[
            pltpu.SemaphoreType.DMA((4 * n,)),
            pltpu.SemaphoreType.DMA((2 * n,)),
            pltpu.SemaphoreType.DMA((4 * n,)),
            pltpu.SemaphoreType.DMA((2 * n,)),
        ],
        compiler_params=pltpu.CompilerParams(collective_id=7, has_side_effects=True),
    )(mine)
    return held.reshape(n * part, channels), other.reshape(n * part, channels)


def on_device(
    inputs,
    depth_kernel,
    depth_bias,
    norm_gain,
    norm_bias,
    proj_in,
    bias_in,
    grn_gamma,
    grn_beta,
    proj_out,
    bias_out,
):
    fresh = extended(inputs[:, 0], (("row", 1),), 3)
    proj_in, proj_out = gathered_weights(proj_in[0], proj_out[0])
    sections = lax.axis_size("section")
    section_index = lax.axis_index("section")
    num_micro = inputs.shape[0]
    own_params = (
        depth_kernel[0],
        depth_bias[0],
        norm_gain[0],
        norm_bias[0],
        proj_in,
        bias_in[0],
        grn_gamma[0],
        grn_beta[0],
        proj_out,
        bias_out[0],
    )
    num_ticks = num_micro + sections - 1
    current = fresh[:1]
    outputs = []
    for tick_index in range(num_ticks):
        hand_on = tick_index + 1 < num_ticks
        produced, current = conv_block(
            current, fresh, min(tick_index + 1, num_micro - 1), own_params, hand_on
        )
        outputs.append(produced)
    stacked = jnp.stack(outputs)
    saved = lax.dynamic_slice_in_dim(stacked, section_index, num_micro, axis=0)
    return saved[None]


def solution(mesh):
    return jax.shard_map(
        on_device,
        mesh=mesh,
        in_specs=(
            P(None, "dp", "row", None, None),
            P("section", None, None, None),
            P("section", None),
            P("section", None),
            P("section", None),
            P("section", None, "dp"),
            P("section", None),
            P("section", None),
            P("section", None),
            P("section", "dp", None),
            P("section", None),
        ),
        out_specs=P("section", None, "dp", "row", None, None),
        check_vma=False,
    )
```

```python
import functools
import math

import jax
import jax.numpy as jnp
from jax import lax
from jax.experimental import pallas as pl
from jax.experimental.pallas import tpu as pltpu
from jax.sharding import PartitionSpec as P

MESH = pl.DeviceIdType.MESH

EPS_NORM = 1e-06
EPS_GRN = 1e-06


def extended(cells, sides, width):
    for axis, dim in sides:
        count = lax.axis_size(axis)
        ends = count - 1
        head = lax.slice_in_dim(cells, 0, width, axis=dim)
        tail = lax.slice_in_dim(cells, cells.shape[dim] - width, cells.shape[dim], axis=dim)
        cells = jnp.concatenate(
            [
                lax.ppermute(tail, axis, [(i, (i + 1) % count) for i in range(ends)]),
                cells,
                lax.ppermute(head, axis, [((i + 1) % count, i) for i in range(ends)]),
            ],
            axis=dim,
        )
    return cells


def _pointwise_kernel(
    n,
    sections,
    hand_on,
    fresh_index,
    padded_ref,
    fresh_ref,
    held_ref,
    other_ref,
    bias_in_ref,
    gamma_ref,
    beta_ref,
    bias_out_ref,
    taps_ref,
    depth_bias_ref,
    gain_ref,
    shift_ref,
    out_ref,
    *rest,
):
    if hand_on:
        next_ref, wide_ref, conv_ref, normed_ref, act_ref, slots, send_sem, recv_sem = rest[:8]
        hand_send, hand_recv, fresh_sem = rest[8:]
    else:
        wide_ref, conv_ref, normed_ref, act_ref, slots, send_sem, recv_sem = rest
    me = lax.axis_index("row")
    section = lax.axis_index("section")
    barrier = pltpu.get_barrier_semaphore()
    for k in range(1, n):
        pl.semaphore_signal(
            barrier, inc=1, device_id={"row": lax.rem(me + k, n)}, device_id_type=MESH
        )
    waits = n - 1
    if hand_on:
        cells = out_ref.shape[0]
        edge = 3 * cells // 4
        has_above = me > 0
        has_below = me < n - 1
        has_prev = section > 0
        has_next = section < sections - 1
        @pl.when(has_prev)
        def _():
            pl.semaphore_signal(
                barrier, inc=1, device_id={"section": section - 1}, device_id_type=MESH
            )

        waits = waits + has_next.astype(jnp.int32)
    padded_rows, margin_cols, channels = wide_ref.shape
    cols = padded_ref.shape[0] // padded_rows
    out_rows = padded_rows - 6
    zeros = jnp.zeros((8, channels), jnp.float32)
    for r in range(padded_rows):
        wide_ref[r, pl.ds(0, 8), :] = zeros
        wide_ref[r, pl.ds(8, cols), :] = padded_ref[pl.ds(r * cols, cols), :].astype(jnp.float32)
        wide_ref[r, pl.ds(8 + cols, margin_cols - 8 - cols), :] = zeros[: margin_cols - 8 - cols]

    for start in range(0, channels, 128):
        lanes = pl.ds(start, min(128, channels - start))
        acc = [
            jnp.broadcast_to(
                depth_bias_ref[:, lanes].astype(jnp.float32), (cols, min(128, channels - start))
            )
            for h in range(out_rows)
        ]
        for r in range(padded_rows):
            for j in range(7):
                slab = wide_ref[r, pl.ds(j + 5, cols), lanes]
                for h in range(out_rows):
                    i = r - h
                    if 0 <= i < 7:
                        tap = taps_ref[pl.ds(i * 7 + j, 1), lanes].astype(jnp.float32)
                        acc[h] = acc[h] + slab * tap
        for h in range(out_rows):
            conv_ref[h, :, lanes] = acc[h]

    def norm_row(h, carry):
        acc = conv_ref[h]
        mean = jnp.mean(acc, axis=-1, keepdims=True)
        center = acc - mean
        spread = jnp.mean(center * center, axis=-1, keepdims=True)
        normed = (
            center * lax.rsqrt(spread + EPS_NORM) * gain_ref[...].astype(jnp.float32)
            + shift_ref[...].astype(jnp.float32)
        )
        normed_ref[pl.ds(pl.multiple_of(h * cols, 16), cols), :] = normed.astype(normed_ref.dtype)
        return carry

    lax.fori_loop(0, out_rows, norm_row, 0)
    first_core = lax.rem(me, 2) == 0

    def raise_with(proj_in_t_ref):
        raised = lax.dot_general(
            normed_ref[...],
            proj_in_t_ref[...],
            (((1,), (1,)), ((), ())),
            preferred_element_type=jnp.float32,
        ) + bias_in_ref[...].astype(jnp.float32)
        act_ref[...] = (0.5 * raised * (1.0 + lax.erf(raised * (1.0 / math.sqrt(2.0))))).astype(
            jnp.bfloat16
        )

    pl.when(first_core)(lambda: raise_with(held_ref))
    pl.when(jnp.logical_not(first_core))(lambda: raise_with(other_ref))
    grouped = act_ref[...].astype(jnp.float32)
    slots[me] = jnp.sum(grouped * grouped, axis=0, keepdims=True)
    pl.semaphore_wait(barrier, waits)
    sends = []
    for k in sorted(range(1, n), key=lambda k: -min(k, n - k)):
        copy = pltpu.make_async_remote_copy(
            src_ref=slots.at[me],
            dst_ref=slots.at[me],
            send_sem=send_sem.at[k],
            recv_sem=recv_sem.at[me],
            device_id={"row": lax.rem(me + k, n)},
            device_id_type=MESH,
        )
        copy.start()
        sends.append(copy)
    if hand_on:
        @pl.when(section == 0)
        def _():
            fresh_copy = pltpu.make_async_copy(fresh_ref.at[fresh_index], next_ref, fresh_sem)
            fresh_copy.start()
            fresh_copy.wait()

        @pl.when(jnp.logical_and(has_prev, jnp.logical_not(has_above)))
        def _():
            next_ref[pl.ds(0, edge), :] = jnp.zeros((edge, next_ref.shape[1]), next_ref.dtype)

        @pl.when(jnp.logical_and(has_prev, jnp.logical_not(has_below)))
        def _():
            next_ref[pl.ds(edge + cells, edge), :] = jnp.zeros(
                (edge, next_ref.shape[1]), next_ref.dtype
            )

    for k in range(1, n):
        src = lax.rem(me + k, n)
        pltpu.make_async_remote_copy(
            src_ref=slots.at[src],
            dst_ref=slots.at[src],
            send_sem=send_sem.at[k],
            recv_sem=recv_sem.at[src],
            device_id={"row": src},
            device_id_type=MESH,
        ).wait_recv()
    total_sq = slots[0]
    for j in range(1, n):
        total_sq = total_sq + slots[j]
    magnitude = jnp.sqrt(total_sq)
    grn_ratio = magnitude / (jnp.mean(magnitude, axis=-1, keepdims=True) + EPS_GRN)
    grouped = act_ref[...].astype(jnp.float32)
    hidden = (
        gamma_ref[...].astype(jnp.float32) * grouped * grn_ratio
        + beta_ref[...].astype(jnp.float32)
        + grouped
    ).astype(jnp.bfloat16)
    cells = out_ref.shape[0]
    edge = 3 * cells // 4

    def lower_with(proj_out_ref):
        update = jnp.dot(
            hidden, proj_out_ref[...], preferred_element_type=jnp.float32
        ) + bias_out_ref[...].astype(jnp.float32)
        current = padded_ref[pl.ds(edge, cells), :].astype(jnp.float32)
        out_ref[...] = (current + update).astype(out_ref.dtype)

    pl.when(first_core)(lambda: lower_with(other_ref))
    pl.when(jnp.logical_not(first_core))(lambda: lower_with(held_ref))
    if not hand_on:
        for copy in sends:
            copy.wait_send()
        return
    own_rows = pl.ds(edge, cells)
    handed = pltpu.make_async_remote_copy(
        src_ref=out_ref,
        dst_ref=next_ref.at[own_rows],
        send_sem=hand_send.at[1],
        recv_sem=hand_recv.at[1],
        device_id={"section": section + 1},
        device_id_type=MESH,
    )

    @pl.when(has_next)
    def _():
        handed.start()

    halos = (
        (2, pl.ds(edge, edge), pl.ds(edge + cells, edge), -1, has_above),
        (0, pl.ds(cells, edge), pl.ds(0, edge), 1, has_below),
    )

    def halo_copy(slot, src, dst, peer_row):
        return pltpu.make_async_remote_copy(
            src_ref=next_ref.at[src],
            dst_ref=next_ref.at[dst],
            send_sem=hand_send.at[slot],
            recv_sem=hand_recv.at[slot],
            device_id={"row": peer_row},
            device_id_type=MESH,
        )

    @pl.when(has_prev)
    def _():
        handed.wait_recv()
        for slot, src, dst, shift, cond in halos:
            @pl.when(cond)
            def _():
                halo_copy(slot, src, dst, me + shift).start()

        for slot, src, dst, shift, cond in halos:
            @pl.when(halos[slot // 2][4])
            def _():
                halo_copy(slot, src, dst, me).wait_recv()

        for slot, src, dst, shift, cond in halos:
            @pl.when(cond)
            def _():
                halo_copy(slot, src, dst, me + shift).wait_send()

    @pl.when(has_next)
    def _():
        handed.wait_send()

    for copy in sends:
        copy.wait_send()


def pointwise(
    padded,
    fresh,
    fresh_index,
    held,
    other,
    bias_in,
    grn_gamma,
    grn_beta,
    bias_out,
    depth_kernel,
    depth_bias,
    norm_gain,
    norm_bias,
    cols,
    hand_on,
):
    n = lax.axis_size("row")
    sections = lax.axis_size("section")
    channels = padded.shape[1]
    padded_rows = padded.shape[0] // cols
    cells = (padded_rows - 6) * cols
    hidden_units = held.shape[0]
    vmem = pl.BlockSpec(memory_space=pltpu.VMEM)
    out_shape = [jax.ShapeDtypeStruct((cells, channels), padded.dtype)]
    scratch = [
        pltpu.VMEM((padded_rows, -(-(cols + 11) // 8) * 8, channels), jnp.float32),
        pltpu.VMEM((padded_rows - 6, cols, channels), jnp.float32),
        pltpu.VMEM((cells, channels), jnp.bfloat16),
        pltpu.VMEM((cells, hidden_units), jnp.bfloat16),
        pltpu.VMEM((n, 1, hidden_units), jnp.float32),
        pltpu.SemaphoreType.DMA((n,)),
        pltpu.SemaphoreType.DMA((n,)),
    ]
    if hand_on:
        out_shape.append(jax.ShapeDtypeStruct(fresh.shape[1:], fresh.dtype))
        scratch += [
            pltpu.SemaphoreType.DMA((3,)),
            pltpu.SemaphoreType.DMA((3,)),
            pltpu.SemaphoreType.DMA(()),
        ]
    return pl.pallas_call(
        functools.partial(_pointwise_kernel, n, sections, hand_on, fresh_index),
        out_shape=out_shape,
        in_specs=[vmem, pl.BlockSpec(memory_space=pl.ANY)] + [vmem] * 10,
        out_specs=[vmem] * len(out_shape),
        scratch_shapes=scratch,
        compiler_params=pltpu.CompilerParams(
            collective_id=1 + fresh_index if hand_on else 0, has_side_effects=True
        ),
        cost_estimate=pl.CostEstimate(
            flops=4 * cells * channels * hidden_units,
            transcendentals=cells * hidden_units,
            bytes_accessed=4 * channels * hidden_units + 8 * cells * channels,
        ),
    )(
        padded,
        fresh,
        held,
        other,
        bias_in.reshape(1, -1),
        grn_gamma.reshape(1, -1),
        grn_beta.reshape(1, -1),
        bias_out.reshape(1, -1),
        depth_kernel.reshape(-1, channels),
        depth_bias.reshape(1, -1),
        norm_gain.reshape(1, -1),
        norm_bias.reshape(1, -1),
    )


def passed_along(x, axis, by):
    count = lax.axis_size(axis)
    pairs = [(i, i + by) for i in range(count) if 0 <= i + by < count]
    return lax.ppermute(x, axis, pairs)


def depthwise(padded, kernel, bias_term):
    channels = padded.shape[-1]
    conv_out = lax.conv_general_dilated(
        padded.astype(jnp.float32),
        kernel.astype(jnp.float32)[:, :, None, :],
        (1, 1),
        "VALID",
        dimension_numbers=("NHWC", "HWIO", "NHWC"),
        feature_group_count=channels,
        precision=lax.Precision.HIGHEST,
    )
    return conv_out + bias_term.astype(jnp.float32)


def conv_block(padded, fresh, fresh_index, params, hand_on):
    (
        depth_kernel,
        depth_bias,
        norm_gain,
        norm_bias,
        proj_in,
        bias_in,
        grn_gamma,
        grn_beta,
        proj_out,
        bias_out,
    ) = params
    num_items, padded_rows, num_cols, channels = padded.shape
    results = pointwise(
        padded.reshape(-1, channels),
        fresh.reshape(fresh.shape[0], -1, channels),
        fresh_index,
        proj_in,
        proj_out,
        bias_in,
        grn_gamma,
        grn_beta,
        bias_out,
        depth_kernel,
        depth_bias,
        norm_gain,
        norm_bias,
        num_cols,
        hand_on,
    )
    produced = results[0].reshape(num_items, padded_rows - 6, num_cols, channels)
    arriving = results[1].reshape(padded.shape) if hand_on else None
    return produced, arriving


def _gather_kernel(n, chunks, mine_ref, held_ref, other_ref, send_sem, recv_sem, pass_send, pass_recv):
    me = lax.axis_index("dp")
    row = lax.axis_index("row")
    partner = {"row": row + 1 - 2 * lax.rem(row, 2)}
    right = {"dp": lax.rem(me + 1, n)}
    left = {"dp": lax.rem(me + n - 1, n)}
    barrier = pltpu.get_barrier_semaphore()
    for peer in (right, left, partner):
        pl.semaphore_signal(barrier, inc=1, device_id=peer, device_id_type=MESH)
    pl.semaphore_wait(barrier, 3)
    sends = []
    parts = len(chunks)

    def send(src, dst, send_sems, recv_sems, slot, c, peer):
        copy = pltpu.make_async_remote_copy(
            src_ref=src.at[chunks[c]],
            dst_ref=dst.at[slot, chunks[c]],
            send_sem=send_sems.at[len(sends)],
            recv_sem=recv_sems.at[slot * parts + c],
            device_id=peer,
            device_id_type=MESH,
        )
        copy.start()
        sends.append(copy)

    def arrived(dst, recv_sems, slot, c):
        pltpu.make_async_remote_copy(
            src_ref=mine_ref.at[chunks[c]],
            dst_ref=dst.at[slot, chunks[c]],
            send_sem=send_sem.at[0],
            recv_sem=recv_sems.at[slot * parts + c],
            device_id=right,
            device_id_type=MESH,
        ).wait_recv()

    to_right = n // 2
    to_left = n - 1 - to_right
    for c in range(parts):
        send(mine_ref, held_ref, send_sem, recv_sem, me, c, right)
        send(mine_ref, held_ref, send_sem, recv_sem, me, c, left)
    for c in range(parts):
        send(mine_ref, other_ref, pass_send, pass_recv, me, c, partner)
    held_ref[me] = mine_ref[...]
    for k in range(1, max(to_right, to_left) + 1):
        for c in range(parts):
            for steps, way, peer in ((to_right, -1, right), (to_left, 1, left)):
                if k > steps:
                    continue
                origin = lax.rem(me + n + way * k, n)
                arrived(held_ref, recv_sem, origin, c)
                if k < steps:
                    send(held_ref.at[origin], held_ref, send_sem, recv_sem, origin, c, peer)
                send(held_ref.at[origin], other_ref, pass_send, pass_recv, origin, c, partner)
    for slot in range(n):
        for c in range(parts):
            arrived(other_ref, pass_recv, slot, c)
    for copy in sends:
        copy.wait_send()


def gathered_weights(proj_in, proj_out):
    n = lax.axis_size("dp")
    first_core = lax.rem(lax.axis_index("row"), 2) == 0
    mine = jnp.where(first_core, proj_in.T, proj_out)
    part, channels = mine.shape
    vmem = pl.BlockSpec(memory_space=pltpu.VMEM)
    gathered = jax.ShapeDtypeStruct((n, part, channels), mine.dtype)
    held, other = pl.pallas_call(
        functools.partial(_gather_kernel, n, (pl.ds(0, 96), pl.ds(96, part - 96))),
        out_shape=[gathered, gathered],
        in_specs=[vmem],
        out_specs=[vmem, vmem],
        scratch_shapes=[
            pltpu.SemaphoreType.DMA((4 * n,)),
            pltpu.SemaphoreType.DMA((2 * n,)),
            pltpu.SemaphoreType.DMA((4 * n,)),
            pltpu.SemaphoreType.DMA((2 * n,)),
        ],
        compiler_params=pltpu.CompilerParams(collective_id=7, has_side_effects=True),
    )(mine)
    return held.reshape(n * part, channels), other.reshape(n * part, channels)


def on_device(
    inputs,
    depth_kernel,
    depth_bias,
    norm_gain,
    norm_bias,
    proj_in,
    bias_in,
    grn_gamma,
    grn_beta,
    proj_out,
    bias_out,
):
    fresh = extended(inputs[:, 0], (("row", 1),), 3)
    proj_in, proj_out = gathered_weights(proj_in[0], proj_out[0])
    sections = lax.axis_size("section")
    section_index = lax.axis_index("section")
    num_micro = inputs.shape[0]
    own_params = (
        depth_kernel[0],
        depth_bias[0],
        norm_gain[0],
        norm_bias[0],
        proj_in,
        bias_in[0],
        grn_gamma[0],
        grn_beta[0],
        proj_out,
        bias_out[0],
    )
    num_ticks = num_micro + sections - 1
    current = fresh[:1]
    outputs = []
    for tick_index in range(num_ticks):
        hand_on = tick_index + 1 < num_ticks
        produced, current = conv_block(
            current, fresh, min(tick_index + 1, num_micro - 1), own_params, hand_on
        )
        outputs.append(produced)
    stacked = jnp.stack(outputs)
    saved = lax.dynamic_slice_in_dim(stacked, section_index, num_micro, axis=0)
    return saved[None]


def solution(mesh):
    return jax.shard_map(
        on_device,
        mesh=mesh,
        in_specs=(
            P(None, "dp", "row", None, None),
            P("section", None, None, None),
            P("section", None),
            P("section", None),
            P("section", None),
            P("section", None, "dp"),
            P("section", None),
            P("section", None),
            P("section", None),
            P("section", "dp", None),
            P("section", None),
        ),
        out_specs=P("section", None, "dp", "row", None, None),
        check_vma=False,
    )
```

```python
import functools
import math

import jax
import jax.numpy as jnp
from jax import lax
from jax.experimental import pallas as pl
from jax.experimental.pallas import tpu as pltpu
from jax.sharding import PartitionSpec as P

MESH = pl.DeviceIdType.MESH

EPS_NORM = 1e-06
EPS_GRN = 1e-06


def extended(cells, sides, width):
    for axis, dim in sides:
        count = lax.axis_size(axis)
        ends = count - 1
        head = lax.slice_in_dim(cells, 0, width, axis=dim)
        tail = lax.slice_in_dim(cells, cells.shape[dim] - width, cells.shape[dim], axis=dim)
        cells = jnp.concatenate(
            [
                lax.ppermute(tail, axis, [(i, (i + 1) % count) for i in range(ends)]),
                cells,
                lax.ppermute(head, axis, [((i + 1) % count, i) for i in range(ends)]),
            ],
            axis=dim,
        )
    return cells


def _pointwise_kernel(
    n,
    sections,
    hand_on,
    fresh_index,
    padded_ref,
    fresh_ref,
    held_ref,
    other_ref,
    bias_in_ref,
    gamma_ref,
    beta_ref,
    bias_out_ref,
    taps_ref,
    depth_bias_ref,
    gain_ref,
    shift_ref,
    out_ref,
    *rest,
):
    if hand_on:
        next_ref, wide_ref, conv_ref, normed_ref, act_ref, slots, send_sem, recv_sem = rest[:8]
        hand_send, hand_recv, fresh_sem = rest[8:]
    else:
        wide_ref, conv_ref, normed_ref, act_ref, slots, send_sem, recv_sem = rest
    me = lax.axis_index("row")
    section = lax.axis_index("section")
    barrier = pltpu.get_barrier_semaphore()
    for k in range(1, n):
        pl.semaphore_signal(
            barrier, inc=1, device_id={"row": lax.rem(me + k, n)}, device_id_type=MESH
        )
    waits = n - 1
    if hand_on:
        cells = out_ref.shape[0]
        edge = 3 * cells // 4
        has_above = me > 0
        has_below = me < n - 1
        has_prev = section > 0
        has_next = section < sections - 1
        @pl.when(has_prev)
        def _():
            pl.semaphore_signal(
                barrier, inc=1, device_id={"section": section - 1}, device_id_type=MESH
            )

        waits = waits + has_next.astype(jnp.int32)
    padded_rows, margin_cols, channels = wide_ref.shape
    cols = padded_ref.shape[0] // padded_rows
    out_rows = padded_rows - 6
    zeros = jnp.zeros((8, channels), jnp.float32)
    for r in range(padded_rows):
        wide_ref[r, pl.ds(0, 8), :] = zeros
        wide_ref[r, pl.ds(8, cols), :] = padded_ref[pl.ds(r * cols, cols), :].astype(jnp.float32)
        wide_ref[r, pl.ds(8 + cols, margin_cols - 8 - cols), :] = zeros[: margin_cols - 8 - cols]

    for start in range(0, channels, 128):
        lanes = pl.ds(start, min(128, channels - start))
        acc = [
            jnp.broadcast_to(
                depth_bias_ref[:, lanes].astype(jnp.float32), (cols, min(128, channels - start))
            )
            for h in range(out_rows)
        ]
        for r in range(padded_rows):
            for j in range(7):
                slab = wide_ref[r, pl.ds(j + 5, cols), lanes]
                for h in range(out_rows):
                    i = r - h
                    if 0 <= i < 7:
                        tap = taps_ref[pl.ds(i * 7 + j, 1), lanes].astype(jnp.float32)
                        acc[h] = acc[h] + slab * tap
        for h in range(out_rows):
            conv_ref[h, :, lanes] = acc[h]

    def norm_row(h, carry):
        acc = conv_ref[h]
        mean = jnp.mean(acc, axis=-1, keepdims=True)
        center = acc - mean
        spread = jnp.mean(center * center, axis=-1, keepdims=True)
        normed = (
            center * lax.rsqrt(spread + EPS_NORM) * gain_ref[...].astype(jnp.float32)
            + shift_ref[...].astype(jnp.float32)
        )
        normed_ref[pl.ds(pl.multiple_of(h * cols, 16), cols), :] = normed.astype(normed_ref.dtype)
        return carry

    lax.fori_loop(0, out_rows, norm_row, 0)
    first_core = lax.rem(me, 2) == 0

    def raise_with(proj_in_t_ref):
        raised = lax.dot_general(
            normed_ref[...],
            proj_in_t_ref[...],
            (((1,), (1,)), ((), ())),
            preferred_element_type=jnp.float32,
        ) + bias_in_ref[...].astype(jnp.float32)
        act_ref[...] = (0.5 * raised * (1.0 + lax.erf(raised * (1.0 / math.sqrt(2.0))))).astype(
            jnp.bfloat16
        )

    pl.when(first_core)(lambda: raise_with(held_ref))
    pl.when(jnp.logical_not(first_core))(lambda: raise_with(other_ref))
    grouped = act_ref[...].astype(jnp.float32)
    slots[me] = jnp.sum(grouped * grouped, axis=0, keepdims=True)
    pl.semaphore_wait(barrier, waits)
    sends = []
    for k in sorted(range(1, n), key=lambda k: -min(k, n - k)):
        copy = pltpu.make_async_remote_copy(
            src_ref=slots.at[me],
            dst_ref=slots.at[me],
            send_sem=send_sem.at[k],
            recv_sem=recv_sem.at[me],
            device_id={"row": lax.rem(me + k, n)},
            device_id_type=MESH,
        )
        copy.start()
        sends.append(copy)
    if hand_on:
        fresh_copy = pltpu.make_async_copy(
            fresh_ref.at[fresh_index], next_ref.at[pl.ds(edge, cells)], fresh_sem
        )
        pl.when(section == 0)(fresh_copy.start)

        @pl.when(jnp.logical_not(has_above))
        def _():
            next_ref[pl.ds(0, edge), :] = jnp.zeros((edge, next_ref.shape[1]), next_ref.dtype)

        @pl.when(jnp.logical_not(has_below))
        def _():
            next_ref[pl.ds(edge + cells, edge), :] = jnp.zeros(
                (edge, next_ref.shape[1]), next_ref.dtype
            )

    for k in range(1, n):
        src = lax.rem(me + k, n)
        pltpu.make_async_remote_copy(
            src_ref=slots.at[src],
            dst_ref=slots.at[src],
            send_sem=send_sem.at[k],
            recv_sem=recv_sem.at[src],
            device_id={"row": src},
            device_id_type=MESH,
        ).wait_recv()
    total_sq = slots[0]
    for j in range(1, n):
        total_sq = total_sq + slots[j]
    magnitude = jnp.sqrt(total_sq)
    grn_ratio = magnitude / (jnp.mean(magnitude, axis=-1, keepdims=True) + EPS_GRN)
    grouped = act_ref[...].astype(jnp.float32)
    hidden = (
        gamma_ref[...].astype(jnp.float32) * grouped * grn_ratio
        + beta_ref[...].astype(jnp.float32)
        + grouped
    ).astype(jnp.bfloat16)
    cells = out_ref.shape[0]
    edge = 3 * cells // 4

    def lower_with(proj_out_ref):
        update = jnp.dot(
            hidden, proj_out_ref[...], preferred_element_type=jnp.float32
        ) + bias_out_ref[...].astype(jnp.float32)
        current = padded_ref[pl.ds(edge, cells), :].astype(jnp.float32)
        out_ref[...] = (current + update).astype(out_ref.dtype)

    pl.when(first_core)(lambda: lower_with(other_ref))
    pl.when(jnp.logical_not(first_core))(lambda: lower_with(held_ref))
    if not hand_on:
        for copy in sends:
            copy.wait_send()
        return
    own_rows = pl.ds(edge, cells)
    handed = pltpu.make_async_remote_copy(
        src_ref=out_ref,
        dst_ref=next_ref.at[own_rows],
        send_sem=hand_send.at[1],
        recv_sem=hand_recv.at[1],
        device_id={"section": section + 1},
        device_id_type=MESH,
    )

    @pl.when(has_next)
    def _():
        handed.start()

    halos = (
        (2, pl.ds(edge, edge), pl.ds(edge + cells, edge), -1, has_above),
        (0, pl.ds(cells, edge), pl.ds(0, edge), 1, has_below),
    )

    def halo_copy(slot, src, dst, peer_row):
        return pltpu.make_async_remote_copy(
            src_ref=next_ref.at[src],
            dst_ref=next_ref.at[dst],
            send_sem=hand_send.at[slot],
            recv_sem=hand_recv.at[slot],
            device_id={"row": peer_row},
            device_id_type=MESH,
        )

    pl.when(has_prev)(handed.wait_recv)
    pl.when(section == 0)(fresh_copy.wait)
    for slot, src, dst, shift, cond in halos:
        @pl.when(cond)
        def _():
            halo_copy(slot, src, dst, me + shift).start()

    for slot, src, dst, shift, cond in halos:
        @pl.when(halos[slot // 2][4])
        def _():
            halo_copy(slot, src, dst, me).wait_recv()

    for slot, src, dst, shift, cond in halos:
        @pl.when(cond)
        def _():
            halo_copy(slot, src, dst, me + shift).wait_send()

    @pl.when(has_next)
    def _():
        handed.wait_send()

    for copy in sends:
        copy.wait_send()


def pointwise(
    padded,
    fresh,
    fresh_index,
    held,
    other,
    bias_in,
    grn_gamma,
    grn_beta,
    bias_out,
    depth_kernel,
    depth_bias,
    norm_gain,
    norm_bias,
    cols,
    hand_on,
):
    n = lax.axis_size("row")
    sections = lax.axis_size("section")
    channels = padded.shape[1]
    padded_rows = padded.shape[0] // cols
    cells = (padded_rows - 6) * cols
    hidden_units = held.shape[0]
    vmem = pl.BlockSpec(memory_space=pltpu.VMEM)
    out_shape = [jax.ShapeDtypeStruct((cells, channels), padded.dtype)]
    scratch = [
        pltpu.VMEM((padded_rows, -(-(cols + 11) // 8) * 8, channels), jnp.float32),
        pltpu.VMEM((padded_rows - 6, cols, channels), jnp.float32),
        pltpu.VMEM((cells, channels), jnp.bfloat16),
        pltpu.VMEM((cells, hidden_units), jnp.bfloat16),
        pltpu.VMEM((n, 1, hidden_units), jnp.float32),
        pltpu.SemaphoreType.DMA((n,)),
        pltpu.SemaphoreType.DMA((n,)),
    ]
    if hand_on:
        out_shape.append(jax.ShapeDtypeStruct(padded.shape, padded.dtype))
        scratch += [
            pltpu.SemaphoreType.DMA((3,)),
            pltpu.SemaphoreType.DMA((3,)),
            pltpu.SemaphoreType.DMA(()),
        ]
    return pl.pallas_call(
        functools.partial(_pointwise_kernel, n, sections, hand_on, fresh_index),
        out_shape=out_shape,
        in_specs=[vmem, pl.BlockSpec(memory_space=pl.ANY)] + [vmem] * 10,
        out_specs=[vmem] * len(out_shape),
        scratch_shapes=scratch,
        compiler_params=pltpu.CompilerParams(
            collective_id=1 + fresh_index if hand_on else 0, has_side_effects=True
        ),
        cost_estimate=pl.CostEstimate(
            flops=4 * cells * channels * hidden_units,
            transcendentals=cells * hidden_units,
            bytes_accessed=4 * channels * hidden_units + 8 * cells * channels,
        ),
    )(
        padded,
        fresh,
        held,
        other,
        bias_in.reshape(1, -1),
        grn_gamma.reshape(1, -1),
        grn_beta.reshape(1, -1),
        bias_out.reshape(1, -1),
        depth_kernel.reshape(-1, channels),
        depth_bias.reshape(1, -1),
        norm_gain.reshape(1, -1),
        norm_bias.reshape(1, -1),
    )


def passed_along(x, axis, by):
    count = lax.axis_size(axis)
    pairs = [(i, i + by) for i in range(count) if 0 <= i + by < count]
    return lax.ppermute(x, axis, pairs)


def depthwise(padded, kernel, bias_term):
    channels = padded.shape[-1]
    conv_out = lax.conv_general_dilated(
        padded.astype(jnp.float32),
        kernel.astype(jnp.float32)[:, :, None, :],
        (1, 1),
        "VALID",
        dimension_numbers=("NHWC", "HWIO", "NHWC"),
        feature_group_count=channels,
        precision=lax.Precision.HIGHEST,
    )
    return conv_out + bias_term.astype(jnp.float32)


def conv_block(padded, fresh, fresh_index, params, hand_on):
    (
        depth_kernel,
        depth_bias,
        norm_gain,
        norm_bias,
        proj_in,
        bias_in,
        grn_gamma,
        grn_beta,
        proj_out,
        bias_out,
    ) = params
    num_items, padded_rows, num_cols, channels = padded.shape
    results = pointwise(
        padded.reshape(-1, channels),
        fresh.reshape(fresh.shape[0], -1, channels),
        fresh_index,
        proj_in,
        proj_out,
        bias_in,
        grn_gamma,
        grn_beta,
        bias_out,
        depth_kernel,
        depth_bias,
        norm_gain,
        norm_bias,
        num_cols,
        hand_on,
    )
    produced = results[0].reshape(num_items, padded_rows - 6, num_cols, channels)
    arriving = results[1].reshape(padded.shape) if hand_on else None
    return produced, arriving


def _gather_kernel(n, chunks, mine_ref, held_ref, other_ref, send_sem, recv_sem, pass_send, pass_recv):
    me = lax.axis_index("dp")
    row = lax.axis_index("row")
    partner = {"row": row + 1 - 2 * lax.rem(row, 2)}
    right = {"dp": lax.rem(me + 1, n)}
    left = {"dp": lax.rem(me + n - 1, n)}
    barrier = pltpu.get_barrier_semaphore()
    for peer in (right, left, partner):
        pl.semaphore_signal(barrier, inc=1, device_id=peer, device_id_type=MESH)
    pl.semaphore_wait(barrier, 3)
    sends = []
    parts = len(chunks)

    def send(src, dst, send_sems, recv_sems, slot, c, peer):
        copy = pltpu.make_async_remote_copy(
            src_ref=src.at[chunks[c]],
            dst_ref=dst.at[slot, chunks[c]],
            send_sem=send_sems.at[len(sends)],
            recv_sem=recv_sems.at[slot * parts + c],
            device_id=peer,
            device_id_type=MESH,
        )
        copy.start()
        sends.append(copy)

    def arrived(dst, recv_sems, slot, c):
        pltpu.make_async_remote_copy(
            src_ref=mine_ref.at[chunks[c]],
            dst_ref=dst.at[slot, chunks[c]],
            send_sem=send_sem.at[0],
            recv_sem=recv_sems.at[slot * parts + c],
            device_id=right,
            device_id_type=MESH,
        ).wait_recv()

    to_right = n // 2
    to_left = n - 1 - to_right
    for c in range(parts):
        send(mine_ref, held_ref, send_sem, recv_sem, me, c, right)
        send(mine_ref, held_ref, send_sem, recv_sem, me, c, left)
    for c in range(parts):
        send(mine_ref, other_ref, pass_send, pass_recv, me, c, partner)
    held_ref[me] = mine_ref[...]
    for k in range(1, max(to_right, to_left) + 1):
        for c in range(parts):
            for steps, way, peer in ((to_right, -1, right), (to_left, 1, left)):
                if k > steps:
                    continue
                origin = lax.rem(me + n + way * k, n)
                arrived(held_ref, recv_sem, origin, c)
                if k < steps:
                    send(held_ref.at[origin], held_ref, send_sem, recv_sem, origin, c, peer)
                send(held_ref.at[origin], other_ref, pass_send, pass_recv, origin, c, partner)
    for slot in range(n):
        for c in range(parts):
            arrived(other_ref, pass_recv, slot, c)
    for copy in sends:
        copy.wait_send()


def gathered_weights(proj_in, proj_out):
    n = lax.axis_size("dp")
    first_core = lax.rem(lax.axis_index("row"), 2) == 0
    mine = jnp.where(first_core, proj_in.T, proj_out)
    part, channels = mine.shape
    vmem = pl.BlockSpec(memory_space=pltpu.VMEM)
    gathered = jax.ShapeDtypeStruct((n, part, channels), mine.dtype)
    held, other = pl.pallas_call(
        functools.partial(_gather_kernel, n, (pl.ds(0, 96), pl.ds(96, part - 96))),
        out_shape=[gathered, gathered],
        in_specs=[vmem],
        out_specs=[vmem, vmem],
        scratch_shapes=[
            pltpu.SemaphoreType.DMA((4 * n,)),
            pltpu.SemaphoreType.DMA((2 * n,)),
            pltpu.SemaphoreType.DMA((4 * n,)),
            pltpu.SemaphoreType.DMA((2 * n,)),
        ],
        compiler_params=pltpu.CompilerParams(collective_id=7, has_side_effects=True),
    )(mine)
    return held.reshape(n * part, channels), other.reshape(n * part, channels)


def on_device(
    inputs,
    depth_kernel,
    depth_bias,
    norm_gain,
    norm_bias,
    proj_in,
    bias_in,
    grn_gamma,
    grn_beta,
    proj_out,
    bias_out,
):
    fresh = inputs[:, 0]
    proj_in, proj_out = gathered_weights(proj_in[0], proj_out[0])
    sections = lax.axis_size("section")
    section_index = lax.axis_index("section")
    num_micro = inputs.shape[0]
    own_params = (
        depth_kernel[0],
        depth_bias[0],
        norm_gain[0],
        norm_bias[0],
        proj_in,
        bias_in[0],
        grn_gamma[0],
        grn_beta[0],
        proj_out,
        bias_out[0],
    )
    num_ticks = num_micro + sections - 1
    current = extended(fresh[:1], (("row", 1),), 3)
    outputs = []
    for tick_index in range(num_ticks):
        hand_on = tick_index + 1 < num_ticks
        produced, current = conv_block(
            current, fresh, min(tick_index + 1, num_micro - 1), own_params, hand_on
        )
        outputs.append(produced)
    stacked = jnp.stack(outputs)
    saved = lax.dynamic_slice_in_dim(stacked, section_index, num_micro, axis=0)
    return saved[None]


def solution(mesh):
    return jax.shard_map(
        on_device,
        mesh=mesh,
        in_specs=(
            P(None, "dp", "row", None, None),
            P("section", None, None, None),
            P("section", None),
            P("section", None),
            P("section", None),
            P("section", None, "dp"),
            P("section", None),
            P("section", None),
            P("section", None),
            P("section", "dp", None),
            P("section", None),
        ),
        out_specs=P("section", None, "dp", "row", None, None),
        check_vma=False,
    )
```

```python
import functools
import math

import jax
import jax.numpy as jnp
from jax import lax
from jax.experimental import pallas as pl
from jax.experimental.pallas import tpu as pltpu
from jax.sharding import PartitionSpec as P

MESH = pl.DeviceIdType.MESH

EPS_NORM = 1e-06
EPS_GRN = 1e-06


def extended(cells, sides, width):
    for axis, dim in sides:
        count = lax.axis_size(axis)
        ends = count - 1
        head = lax.slice_in_dim(cells, 0, width, axis=dim)
        tail = lax.slice_in_dim(cells, cells.shape[dim] - width, cells.shape[dim], axis=dim)
        cells = jnp.concatenate(
            [
                lax.ppermute(tail, axis, [(i, (i + 1) % count) for i in range(ends)]),
                cells,
                lax.ppermute(head, axis, [((i + 1) % count, i) for i in range(ends)]),
            ],
            axis=dim,
        )
    return cells


def _pointwise_kernel(
    n,
    sections,
    hand_on,
    fresh_index,
    padded_ref,
    fresh_ref,
    held_ref,
    other_ref,
    bias_in_ref,
    gamma_ref,
    beta_ref,
    bias_out_ref,
    taps_ref,
    depth_bias_ref,
    gain_ref,
    shift_ref,
    out_ref,
    *rest,
):
    if hand_on:
        next_ref, wide_ref, conv_ref, normed_ref, act_ref, slots, send_sem, recv_sem = rest[:8]
        hand_send, hand_recv, fresh_sem = rest[8:]
    else:
        wide_ref, conv_ref, normed_ref, act_ref, slots, send_sem, recv_sem = rest
    me = lax.axis_index("row")
    section = lax.axis_index("section")
    barrier = pltpu.get_barrier_semaphore()
    for k in range(1, n):
        pl.semaphore_signal(
            barrier, inc=1, device_id={"row": lax.rem(me + k, n)}, device_id_type=MESH
        )
    waits = n - 1
    if hand_on:
        cells = out_ref.shape[0]
        edge = 3 * cells // 4
        has_above = me > 0
        has_below = me < n - 1
        has_prev = section > 0
        has_next = section < sections - 1
        @pl.when(has_prev)
        def _():
            pl.semaphore_signal(
                barrier, inc=1, device_id={"section": section - 1}, device_id_type=MESH
            )

        waits = waits + has_next.astype(jnp.int32)
    padded_rows, margin_cols, channels = wide_ref.shape
    cols = padded_ref.shape[0] // padded_rows
    out_rows = padded_rows - 6
    zeros = jnp.zeros((8, channels), jnp.float32)
    for r in range(padded_rows):
        wide_ref[r, pl.ds(0, 8), :] = zeros
        wide_ref[r, pl.ds(8, cols), :] = padded_ref[pl.ds(r * cols, cols), :].astype(jnp.float32)
        wide_ref[r, pl.ds(8 + cols, margin_cols - 8 - cols), :] = zeros[: margin_cols - 8 - cols]

    for start in range(0, channels, 128):
        lanes = pl.ds(start, min(128, channels - start))
        acc = [
            jnp.broadcast_to(
                depth_bias_ref[:, lanes].astype(jnp.float32), (cols, min(128, channels - start))
            )
            for h in range(out_rows)
        ]
        for r in range(padded_rows):
            for j in range(7):
                slab = wide_ref[r, pl.ds(j + 5, cols), lanes]
                for h in range(out_rows):
                    i = r - h
                    if 0 <= i < 7:
                        tap = taps_ref[pl.ds(i * 7 + j, 1), lanes].astype(jnp.float32)
                        acc[h] = acc[h] + slab * tap
        for h in range(out_rows):
            conv_ref[h, :, lanes] = acc[h]

    def norm_row(h, carry):
        acc = conv_ref[h]
        mean = jnp.mean(acc, axis=-1, keepdims=True)
        center = acc - mean
        spread = jnp.mean(center * center, axis=-1, keepdims=True)
        normed = (
            center * lax.rsqrt(spread + EPS_NORM) * gain_ref[...].astype(jnp.float32)
            + shift_ref[...].astype(jnp.float32)
        )
        normed_ref[pl.ds(pl.multiple_of(h * cols, 16), cols), :] = normed.astype(normed_ref.dtype)
        return carry

    lax.fori_loop(0, out_rows, norm_row, 0)
    first_core = lax.rem(me, 2) == 0

    def raise_with(proj_in_t_ref):
        raised = lax.dot_general(
            normed_ref[...],
            proj_in_t_ref[...],
            (((1,), (1,)), ((), ())),
            preferred_element_type=jnp.float32,
        ) + bias_in_ref[...].astype(jnp.float32)
        act_ref[...] = (0.5 * raised * (1.0 + lax.erf(raised * (1.0 / math.sqrt(2.0))))).astype(
            jnp.bfloat16
        )

    pl.when(first_core)(lambda: raise_with(held_ref))
    pl.when(jnp.logical_not(first_core))(lambda: raise_with(other_ref))
    grouped = act_ref[...].astype(jnp.float32)
    slots[me] = jnp.sum(grouped * grouped, axis=0, keepdims=True)
    pl.semaphore_wait(barrier, waits)
    sends = []
    for k in sorted(range(1, n), key=lambda k: -min(k, n - k)):
        copy = pltpu.make_async_remote_copy(
            src_ref=slots.at[me],
            dst_ref=slots.at[me],
            send_sem=send_sem.at[k],
            recv_sem=recv_sem.at[me],
            device_id={"row": lax.rem(me + k, n)},
            device_id_type=MESH,
        )
        copy.start()
        sends.append(copy)
    if hand_on:
        @pl.when(section == 0)
        def _():
            fresh_copy = pltpu.make_async_copy(fresh_ref.at[fresh_index], next_ref, fresh_sem)
            fresh_copy.start()
            fresh_copy.wait()

        @pl.when(jnp.logical_and(has_prev, jnp.logical_not(has_above)))
        def _():
            next_ref[pl.ds(0, edge), :] = jnp.zeros((edge, next_ref.shape[1]), next_ref.dtype)

        @pl.when(jnp.logical_and(has_prev, jnp.logical_not(has_below)))
        def _():
            next_ref[pl.ds(edge + cells, edge), :] = jnp.zeros(
                (edge, next_ref.shape[1]), next_ref.dtype
            )

    for k in range(1, n):
        src = lax.rem(me + k, n)
        pltpu.make_async_remote_copy(
            src_ref=slots.at[src],
            dst_ref=slots.at[src],
            send_sem=send_sem.at[k],
            recv_sem=recv_sem.at[src],
            device_id={"row": src},
            device_id_type=MESH,
        ).wait_recv()
    total_sq = slots[0]
    for j in range(1, n):
        total_sq = total_sq + slots[j]
    magnitude = jnp.sqrt(total_sq)
    grn_ratio = magnitude / (jnp.mean(magnitude, axis=-1, keepdims=True) + EPS_GRN)
    grouped = act_ref[...].astype(jnp.float32)
    hidden = (
        gamma_ref[...].astype(jnp.float32) * grouped * grn_ratio
        + beta_ref[...].astype(jnp.float32)
        + grouped
    ).astype(jnp.bfloat16)
    cells = out_ref.shape[0]
    edge = 3 * cells // 4

    def lower_with(proj_out_ref):
        update = jnp.dot(
            hidden, proj_out_ref[...], preferred_element_type=jnp.float32
        ) + bias_out_ref[...].astype(jnp.float32)
        current = padded_ref[pl.ds(edge, cells), :].astype(jnp.float32)
        out_ref[...] = (current + update).astype(out_ref.dtype)

    pl.when(first_core)(lambda: lower_with(other_ref))
    pl.when(jnp.logical_not(first_core))(lambda: lower_with(held_ref))
    if not hand_on:
        for copy in sends:
            copy.wait_send()
        return
    own_rows = pl.ds(edge, cells)
    handed = pltpu.make_async_remote_copy(
        src_ref=out_ref,
        dst_ref=next_ref.at[own_rows],
        send_sem=hand_send.at[1],
        recv_sem=hand_recv.at[1],
        device_id={"section": section + 1},
        device_id_type=MESH,
    )

    @pl.when(has_next)
    def _():
        handed.start()

    halos = (
        (2, pl.ds(edge, edge), pl.ds(edge + cells, edge), -1, has_above),
        (0, pl.ds(cells, edge), pl.ds(0, edge), 1, has_below),
    )

    def halo_copy(slot, src, dst, peer_row):
        return pltpu.make_async_remote_copy(
            src_ref=next_ref.at[src],
            dst_ref=next_ref.at[dst],
            send_sem=hand_send.at[slot],
            recv_sem=hand_recv.at[slot],
            device_id={"row": peer_row},
            device_id_type=MESH,
        )

    @pl.when(has_prev)
    def _():
        handed.wait_recv()
        for slot, src, dst, shift, cond in halos:
            @pl.when(cond)
            def _():
                halo_copy(slot, src, dst, me + shift).start()

        for slot, src, dst, shift, cond in halos:
            @pl.when(halos[slot // 2][4])
            def _():
                halo_copy(slot, src, dst, me).wait_recv()

        for slot, src, dst, shift, cond in halos:
            @pl.when(cond)
            def _():
                halo_copy(slot, src, dst, me + shift).wait_send()

    @pl.when(has_next)
    def _():
        handed.wait_send()

    for copy in sends:
        copy.wait_send()


def pointwise(
    padded,
    fresh,
    fresh_index,
    held,
    other,
    bias_in,
    grn_gamma,
    grn_beta,
    bias_out,
    depth_kernel,
    depth_bias,
    norm_gain,
    norm_bias,
    cols,
    hand_on,
):
    n = lax.axis_size("row")
    sections = lax.axis_size("section")
    channels = padded.shape[1]
    padded_rows = padded.shape[0] // cols
    cells = (padded_rows - 6) * cols
    hidden_units = held.shape[0]
    vmem = pl.BlockSpec(memory_space=pltpu.VMEM)
    out_shape = [jax.ShapeDtypeStruct((cells, channels), padded.dtype)]
    scratch = [
        pltpu.VMEM((padded_rows, -(-(cols + 11) // 8) * 8, channels), jnp.float32),
        pltpu.VMEM((padded_rows - 6, cols, channels), jnp.float32),
        pltpu.VMEM((cells, channels), jnp.bfloat16),
        pltpu.VMEM((cells, hidden_units), jnp.bfloat16),
        pltpu.VMEM((n, 1, hidden_units), jnp.float32),
        pltpu.SemaphoreType.DMA((n,)),
        pltpu.SemaphoreType.DMA((n,)),
    ]
    if hand_on:
        out_shape.append(jax.ShapeDtypeStruct(fresh.shape[1:], fresh.dtype))
        scratch += [
            pltpu.SemaphoreType.DMA((3,)),
            pltpu.SemaphoreType.DMA((3,)),
            pltpu.SemaphoreType.DMA(()),
        ]
    return pl.pallas_call(
        functools.partial(_pointwise_kernel, n, sections, hand_on, fresh_index),
        out_shape=out_shape,
        in_specs=[vmem, pl.BlockSpec(memory_space=pl.ANY)] + [vmem] * 10,
        out_specs=[vmem] * len(out_shape),
        scratch_shapes=scratch,
        compiler_params=pltpu.CompilerParams(
            collective_id=1 + fresh_index if hand_on else 0, has_side_effects=True
        ),
        cost_estimate=pl.CostEstimate(
            flops=4 * cells * channels * hidden_units,
            transcendentals=cells * hidden_units,
            bytes_accessed=4 * channels * hidden_units + 8 * cells * channels,
        ),
    )(
        padded,
        fresh,
        held,
        other,
        bias_in.reshape(1, -1),
        grn_gamma.reshape(1, -1),
        grn_beta.reshape(1, -1),
        bias_out.reshape(1, -1),
        depth_kernel.reshape(-1, channels),
        depth_bias.reshape(1, -1),
        norm_gain.reshape(1, -1),
        norm_bias.reshape(1, -1),
    )


def passed_along(x, axis, by):
    count = lax.axis_size(axis)
    pairs = [(i, i + by) for i in range(count) if 0 <= i + by < count]
    return lax.ppermute(x, axis, pairs)


def depthwise(padded, kernel, bias_term):
    channels = padded.shape[-1]
    conv_out = lax.conv_general_dilated(
        padded.astype(jnp.float32),
        kernel.astype(jnp.float32)[:, :, None, :],
        (1, 1),
        "VALID",
        dimension_numbers=("NHWC", "HWIO", "NHWC"),
        feature_group_count=channels,
        precision=lax.Precision.HIGHEST,
    )
    return conv_out + bias_term.astype(jnp.float32)


def conv_block(padded, fresh, fresh_index, params, hand_on):
    (
        depth_kernel,
        depth_bias,
        norm_gain,
        norm_bias,
        proj_in,
        bias_in,
        grn_gamma,
        grn_beta,
        proj_out,
        bias_out,
    ) = params
    num_items, padded_rows, num_cols, channels = padded.shape
    results = pointwise(
        padded.reshape(-1, channels),
        fresh.reshape(fresh.shape[0], -1, channels),
        fresh_index,
        proj_in,
        proj_out,
        bias_in,
        grn_gamma,
        grn_beta,
        bias_out,
        depth_kernel,
        depth_bias,
        norm_gain,
        norm_bias,
        num_cols,
        hand_on,
    )
    produced = results[0].reshape(num_items, padded_rows - 6, num_cols, channels)
    arriving = results[1].reshape(padded.shape) if hand_on else None
    return produced, arriving


def _gather_kernel(
    n,
    chunks,
    rows,
    mine_ref,
    images_ref,
    held_ref,
    other_ref,
    fresh_ref,
    send_sem,
    recv_sem,
    pass_send,
    pass_recv,
    halo_send,
    halo_recv,
    own_sem,
):
    me = lax.axis_index("dp")
    row = lax.axis_index("row")
    odd = lax.rem(row, 2) == 1
    partner = {"row": row + 1 - 2 * lax.rem(row, 2)}
    outer = jnp.where(odd, row + 1, row - 1)
    has_outer = jnp.logical_and(outer >= 0, outer < rows)
    right = {"dp": lax.rem(me + 1, n)}
    left = {"dp": lax.rem(me + n - 1, n)}
    barrier = pltpu.get_barrier_semaphore()
    for peer in (right, left, partner):
        pl.semaphore_signal(barrier, inc=1, device_id=peer, device_id_type=MESH)

    @pl.when(has_outer)
    def _():
        pl.semaphore_signal(barrier, inc=1, device_id={"row": outer}, device_id_type=MESH)

    pl.semaphore_wait(barrier, 3 + has_outer.astype(jnp.int32))
    cells = images_ref.shape[1]
    edge = 3 * cells // 4
    own = pltpu.make_async_copy(images_ref, fresh_ref.at[:, pl.ds(edge, cells)], own_sem)
    own.start()
    has_above = row > 0
    has_below = row < rows - 1
    halos = (
        (0, pl.ds(0, edge), pl.ds(edge + cells, edge), -1, has_above),
        (1, pl.ds(cells - edge, edge), pl.ds(0, edge), 1, has_below),
    )

    def halo_copy(slot, src, dst, peer_row):
        return pltpu.make_async_remote_copy(
            src_ref=images_ref.at[:, src],
            dst_ref=fresh_ref.at[:, dst],
            send_sem=halo_send.at[slot],
            recv_sem=halo_recv.at[slot],
            device_id={"row": peer_row},
            device_id_type=MESH,
        )

    for slot, src, dst, shift, cond in halos:
        pl.when(cond)(halo_copy(slot, src, dst, row + shift).start)

    @pl.when(jnp.logical_not(has_above))
    def _():
        fresh_ref[:, pl.ds(0, edge), :] = jnp.zeros(
            (fresh_ref.shape[0], edge, fresh_ref.shape[2]), fresh_ref.dtype
        )

    @pl.when(jnp.logical_not(has_below))
    def _():
        fresh_ref[:, pl.ds(edge + cells, edge), :] = jnp.zeros(
            (fresh_ref.shape[0], edge, fresh_ref.shape[2]), fresh_ref.dtype
        )

    sends = []
    parts = len(chunks)

    def send(src, dst, send_sems, recv_sems, slot, c, peer):
        copy = pltpu.make_async_remote_copy(
            src_ref=src.at[chunks[c]],
            dst_ref=dst.at[slot, chunks[c]],
            send_sem=send_sems.at[len(sends)],
            recv_sem=recv_sems.at[slot * parts + c],
            device_id=peer,
            device_id_type=MESH,
        )
        copy.start()
        sends.append(copy)

    def arrived(dst, recv_sems, slot, c):
        pltpu.make_async_remote_copy(
            src_ref=mine_ref.at[chunks[c]],
            dst_ref=dst.at[slot, chunks[c]],
            send_sem=send_sem.at[0],
            recv_sem=recv_sems.at[slot * parts + c],
            device_id=right,
            device_id_type=MESH,
        ).wait_recv()

    to_right = n // 2
    to_left = n - 1 - to_right
    for c in range(parts):
        send(mine_ref, held_ref, send_sem, recv_sem, me, c, right)
        send(mine_ref, held_ref, send_sem, recv_sem, me, c, left)
    for c in range(parts):
        send(mine_ref, other_ref, pass_send, pass_recv, me, c, partner)
    held_ref[me] = mine_ref[...]
    for k in range(1, max(to_right, to_left) + 1):
        for c in range(parts):
            for steps, way, peer in ((to_right, -1, right), (to_left, 1, left)):
                if k > steps:
                    continue
                origin = lax.rem(me + n + way * k, n)
                arrived(held_ref, recv_sem, origin, c)
                if k < steps:
                    send(held_ref.at[origin], held_ref, send_sem, recv_sem, origin, c, peer)
                send(held_ref.at[origin], other_ref, pass_send, pass_recv, origin, c, partner)
    for slot in range(n):
        for c in range(parts):
            arrived(other_ref, pass_recv, slot, c)
    for slot, src, dst, shift, cond in halos:
        pl.when(halos[1 - slot][4])(halo_copy(slot, src, dst, row).wait_recv)
    for slot, src, dst, shift, cond in halos:
        pl.when(cond)(halo_copy(slot, src, dst, row + shift).wait_send)
    own.wait()
    for copy in sends:
        copy.wait_send()


def gathered_weights(proj_in, proj_out, images):
    n = lax.axis_size("dp")
    first_core = lax.rem(lax.axis_index("row"), 2) == 0
    mine = jnp.where(first_core, proj_in.T, proj_out)
    part, channels = mine.shape
    vmem = pl.BlockSpec(memory_space=pltpu.VMEM)
    gathered = jax.ShapeDtypeStruct((n, part, channels), mine.dtype)
    micro, cells, _ = images.shape
    fresh = jax.ShapeDtypeStruct((micro, cells * 5 // 2, channels), images.dtype)
    held, other, fresh = pl.pallas_call(
        functools.partial(
            _gather_kernel, n, (pl.ds(0, 96), pl.ds(96, part - 96)), lax.axis_size("row")
        ),
        out_shape=[gathered, gathered, fresh],
        in_specs=[vmem, vmem],
        out_specs=[vmem, vmem, vmem],
        scratch_shapes=[
            pltpu.SemaphoreType.DMA((4 * n,)),
            pltpu.SemaphoreType.DMA((2 * n,)),
            pltpu.SemaphoreType.DMA((4 * n,)),
            pltpu.SemaphoreType.DMA((2 * n,)),
            pltpu.SemaphoreType.DMA((2,)),
            pltpu.SemaphoreType.DMA((2,)),
            pltpu.SemaphoreType.DMA(()),
        ],
        compiler_params=pltpu.CompilerParams(collective_id=7, has_side_effects=True),
    )(mine, images)
    return held.reshape(n * part, channels), other.reshape(n * part, channels), fresh


def on_device(
    inputs,
    depth_kernel,
    depth_bias,
    norm_gain,
    norm_bias,
    proj_in,
    bias_in,
    grn_gamma,
    grn_beta,
    proj_out,
    bias_out,
):
    num_micro, _, num_rows, num_cols, channels = inputs.shape
    proj_in, proj_out, fresh = gathered_weights(
        proj_in[0], proj_out[0], inputs.reshape(num_micro, num_rows * num_cols, channels)
    )
    fresh = fresh.reshape(num_micro, -1, num_cols, channels)
    sections = lax.axis_size("section")
    section_index = lax.axis_index("section")
    num_micro = inputs.shape[0]
    own_params = (
        depth_kernel[0],
        depth_bias[0],
        norm_gain[0],
        norm_bias[0],
        proj_in,
        bias_in[0],
        grn_gamma[0],
        grn_beta[0],
        proj_out,
        bias_out[0],
    )
    num_ticks = num_micro + sections - 1
    current = fresh[:1]
    outputs = []
    for tick_index in range(num_ticks):
        hand_on = tick_index + 1 < num_ticks
        produced, current = conv_block(
            current, fresh, min(tick_index + 1, num_micro - 1), own_params, hand_on
        )
        outputs.append(produced)
    stacked = jnp.stack(outputs)
    saved = lax.dynamic_slice_in_dim(stacked, section_index, num_micro, axis=0)
    return saved[None]


def solution(mesh):
    return jax.shard_map(
        on_device,
        mesh=mesh,
        in_specs=(
            P(None, "dp", "row", None, None),
            P("section", None, None, None),
            P("section", None),
            P("section", None),
            P("section", None),
            P("section", None, "dp"),
            P("section", None),
            P("section", None),
            P("section", None),
            P("section", "dp", None),
            P("section", None),
        ),
        out_specs=P("section", None, "dp", "row", None, None),
        check_vma=False,
    )
```

```python
import functools
import math

import jax
import jax.numpy as jnp
from jax import lax
from jax.experimental import pallas as pl
from jax.experimental.pallas import tpu as pltpu
from jax.sharding import PartitionSpec as P

MESH = pl.DeviceIdType.MESH

EPS_NORM = 1e-06
EPS_GRN = 1e-06


def extended(cells, sides, width):
    for axis, dim in sides:
        count = lax.axis_size(axis)
        ends = count - 1
        head = lax.slice_in_dim(cells, 0, width, axis=dim)
        tail = lax.slice_in_dim(cells, cells.shape[dim] - width, cells.shape[dim], axis=dim)
        cells = jnp.concatenate(
            [
                lax.ppermute(tail, axis, [(i, (i + 1) % count) for i in range(ends)]),
                cells,
                lax.ppermute(head, axis, [((i + 1) % count, i) for i in range(ends)]),
            ],
            axis=dim,
        )
    return cells


def _pointwise_kernel(
    n,
    sections,
    hand_on,
    fresh_index,
    padded_ref,
    fresh_ref,
    held_ref,
    other_ref,
    bias_in_ref,
    gamma_ref,
    beta_ref,
    bias_out_ref,
    taps_ref,
    depth_bias_ref,
    gain_ref,
    shift_ref,
    out_ref,
    *rest,
):
    if hand_on:
        next_ref, wide_ref, conv_ref, normed_ref, act_ref, slots, send_sem, recv_sem = rest[:8]
        hand_send, hand_recv, fresh_sem = rest[8:]
    else:
        wide_ref, conv_ref, normed_ref, act_ref, slots, send_sem, recv_sem = rest
    me = lax.axis_index("row")
    section = lax.axis_index("section")
    barrier = pltpu.get_barrier_semaphore()
    for k in range(1, n):
        pl.semaphore_signal(
            barrier, inc=1, device_id={"row": lax.rem(me + k, n)}, device_id_type=MESH
        )
    waits = n - 1
    if hand_on:
        cells = out_ref.shape[0]
        edge = 3 * cells // 4
        has_above = me > 0
        has_below = me < n - 1
        has_prev = section > 0
        has_next = section < sections - 1
        @pl.when(has_prev)
        def _():
            pl.semaphore_signal(
                barrier, inc=1, device_id={"section": section - 1}, device_id_type=MESH
            )

        waits = waits + has_next.astype(jnp.int32)
    padded_rows, margin_cols, channels = wide_ref.shape
    cols = padded_ref.shape[0] // padded_rows
    out_rows = padded_rows - 6
    zeros = jnp.zeros((8, channels), jnp.float32)
    for r in range(padded_rows):
        wide_ref[r, pl.ds(0, 8), :] = zeros
        wide_ref[r, pl.ds(8, cols), :] = padded_ref[pl.ds(r * cols, cols), :].astype(jnp.float32)
        wide_ref[r, pl.ds(8 + cols, margin_cols - 8 - cols), :] = zeros[: margin_cols - 8 - cols]

    for start in range(0, channels, 128):
        lanes = pl.ds(start, min(128, channels - start))
        acc = [
            jnp.broadcast_to(
                depth_bias_ref[:, lanes].astype(jnp.float32), (cols, min(128, channels - start))
            )
            for h in range(out_rows)
        ]
        for r in range(padded_rows):
            for j in range(7):
                slab = wide_ref[r, pl.ds(j + 5, cols), lanes]
                for h in range(out_rows):
                    i = r - h
                    if 0 <= i < 7:
                        tap = taps_ref[pl.ds(i * 7 + j, 1), lanes].astype(jnp.float32)
                        acc[h] = acc[h] + slab * tap
        for h in range(out_rows):
            conv_ref[h, :, lanes] = acc[h]

    def norm_row(h, carry):
        acc = conv_ref[h]
        mean = jnp.mean(acc, axis=-1, keepdims=True)
        center = acc - mean
        spread = jnp.mean(center * center, axis=-1, keepdims=True)
        normed = (
            center * lax.rsqrt(spread + EPS_NORM) * gain_ref[...].astype(jnp.float32)
            + shift_ref[...].astype(jnp.float32)
        )
        normed_ref[pl.ds(pl.multiple_of(h * cols, 16), cols), :] = normed.astype(normed_ref.dtype)
        return carry

    lax.fori_loop(0, out_rows, norm_row, 0)
    first_core = lax.rem(me, 2) == 0

    def raise_with(proj_in_t_ref):
        raised = lax.dot_general(
            normed_ref[...],
            proj_in_t_ref[...],
            (((1,), (1,)), ((), ())),
            preferred_element_type=jnp.float32,
        ) + bias_in_ref[...].astype(jnp.float32)
        act_ref[...] = (0.5 * raised * (1.0 + lax.erf(raised * (1.0 / math.sqrt(2.0))))).astype(
            jnp.bfloat16
        )

    pl.when(first_core)(lambda: raise_with(held_ref))
    pl.when(jnp.logical_not(first_core))(lambda: raise_with(other_ref))
    grouped = act_ref[...].astype(jnp.float32)
    slots[me] = jnp.sum(grouped * grouped, axis=0, keepdims=True)
    pl.semaphore_wait(barrier, waits)
    sends = []
    for k in sorted(range(1, n), key=lambda k: -min(k, n - k)):
        copy = pltpu.make_async_remote_copy(
            src_ref=slots.at[me],
            dst_ref=slots.at[me],
            send_sem=send_sem.at[k],
            recv_sem=recv_sem.at[me],
            device_id={"row": lax.rem(me + k, n)},
            device_id_type=MESH,
        )
        copy.start()
        sends.append(copy)
    if hand_on:
        fresh_copy = pltpu.make_async_copy(fresh_ref.at[fresh_index], next_ref, fresh_sem)
        pl.when(section == 0)(fresh_copy.start)

        @pl.when(jnp.logical_and(has_prev, jnp.logical_not(has_above)))
        def _():
            next_ref[pl.ds(0, edge), :] = jnp.zeros((edge, next_ref.shape[1]), next_ref.dtype)

        @pl.when(jnp.logical_and(has_prev, jnp.logical_not(has_below)))
        def _():
            next_ref[pl.ds(edge + cells, edge), :] = jnp.zeros(
                (edge, next_ref.shape[1]), next_ref.dtype
            )

    for k in range(1, n):
        src = lax.rem(me + k, n)
        pltpu.make_async_remote_copy(
            src_ref=slots.at[src],
            dst_ref=slots.at[src],
            send_sem=send_sem.at[k],
            recv_sem=recv_sem.at[src],
            device_id={"row": src},
            device_id_type=MESH,
        ).wait_recv()
    total_sq = slots[0]
    for j in range(1, n):
        total_sq = total_sq + slots[j]
    magnitude = jnp.sqrt(total_sq)
    grn_ratio = magnitude / (jnp.mean(magnitude, axis=-1, keepdims=True) + EPS_GRN)
    grouped = act_ref[...].astype(jnp.float32)
    hidden = (
        gamma_ref[...].astype(jnp.float32) * grouped * grn_ratio
        + beta_ref[...].astype(jnp.float32)
        + grouped
    ).astype(jnp.bfloat16)
    cells = out_ref.shape[0]
    edge = 3 * cells // 4

    def lower_with(proj_out_ref):
        update = jnp.dot(
            hidden, proj_out_ref[...], preferred_element_type=jnp.float32
        ) + bias_out_ref[...].astype(jnp.float32)
        current = padded_ref[pl.ds(edge, cells), :].astype(jnp.float32)
        out_ref[...] = (current + update).astype(out_ref.dtype)

    pl.when(first_core)(lambda: lower_with(other_ref))
    pl.when(jnp.logical_not(first_core))(lambda: lower_with(held_ref))
    if not hand_on:
        for copy in sends:
            copy.wait_send()
        return
    own_rows = pl.ds(edge, cells)
    handed = pltpu.make_async_remote_copy(
        src_ref=out_ref,
        dst_ref=next_ref.at[own_rows],
        send_sem=hand_send.at[1],
        recv_sem=hand_recv.at[1],
        device_id={"section": section + 1},
        device_id_type=MESH,
    )

    @pl.when(has_next)
    def _():
        handed.start()

    halos = (
        (2, pl.ds(edge, edge), pl.ds(edge + cells, edge), -1, has_above),
        (0, pl.ds(cells, edge), pl.ds(0, edge), 1, has_below),
    )

    def halo_copy(slot, src, dst, peer_row):
        return pltpu.make_async_remote_copy(
            src_ref=next_ref.at[src],
            dst_ref=next_ref.at[dst],
            send_sem=hand_send.at[slot],
            recv_sem=hand_recv.at[slot],
            device_id={"row": peer_row},
            device_id_type=MESH,
        )

    @pl.when(has_prev)
    def _():
        handed.wait_recv()
        for slot, src, dst, shift, cond in halos:
            @pl.when(cond)
            def _():
                halo_copy(slot, src, dst, me + shift).start()

        for slot, src, dst, shift, cond in halos:
            @pl.when(halos[slot // 2][4])
            def _():
                halo_copy(slot, src, dst, me).wait_recv()

        for slot, src, dst, shift, cond in halos:
            @pl.when(cond)
            def _():
                halo_copy(slot, src, dst, me + shift).wait_send()

    @pl.when(has_next)
    def _():
        handed.wait_send()

    pl.when(section == 0)(fresh_copy.wait)
    for copy in sends:
        copy.wait_send()


def pointwise(
    padded,
    fresh,
    fresh_index,
    held,
    other,
    bias_in,
    grn_gamma,
    grn_beta,
    bias_out,
    depth_kernel,
    depth_bias,
    norm_gain,
    norm_bias,
    cols,
    hand_on,
):
    n = lax.axis_size("row")
    sections = lax.axis_size("section")
    channels = padded.shape[1]
    padded_rows = padded.shape[0] // cols
    cells = (padded_rows - 6) * cols
    hidden_units = held.shape[0]
    vmem = pl.BlockSpec(memory_space=pltpu.VMEM)
    out_shape = [jax.ShapeDtypeStruct((cells, channels), padded.dtype)]
    scratch = [
        pltpu.VMEM((padded_rows, -(-(cols + 11) // 8) * 8, channels), jnp.float32),
        pltpu.VMEM((padded_rows - 6, cols, channels), jnp.float32),
        pltpu.VMEM((cells, channels), jnp.bfloat16),
        pltpu.VMEM((cells, hidden_units), jnp.bfloat16),
        pltpu.VMEM((n, 1, hidden_units), jnp.float32),
        pltpu.SemaphoreType.DMA((n,)),
        pltpu.SemaphoreType.DMA((n,)),
    ]
    if hand_on:
        out_shape.append(jax.ShapeDtypeStruct(fresh.shape[1:], fresh.dtype))
        scratch += [
            pltpu.SemaphoreType.DMA((3,)),
            pltpu.SemaphoreType.DMA((3,)),
            pltpu.SemaphoreType.DMA(()),
        ]
    return pl.pallas_call(
        functools.partial(_pointwise_kernel, n, sections, hand_on, fresh_index),
        out_shape=out_shape,
        in_specs=[vmem, pl.BlockSpec(memory_space=pl.ANY)] + [vmem] * 10,
        out_specs=[vmem] * len(out_shape),
        scratch_shapes=scratch,
        compiler_params=pltpu.CompilerParams(
            collective_id=1 + fresh_index if hand_on else 0, has_side_effects=True
        ),
        cost_estimate=pl.CostEstimate(
            flops=4 * cells * channels * hidden_units,
            transcendentals=cells * hidden_units,
            bytes_accessed=4 * channels * hidden_units + 8 * cells * channels,
        ),
    )(
        padded,
        fresh,
        held,
        other,
        bias_in.reshape(1, -1),
        grn_gamma.reshape(1, -1),
        grn_beta.reshape(1, -1),
        bias_out.reshape(1, -1),
        depth_kernel.reshape(-1, channels),
        depth_bias.reshape(1, -1),
        norm_gain.reshape(1, -1),
        norm_bias.reshape(1, -1),
    )


def passed_along(x, axis, by):
    count = lax.axis_size(axis)
    pairs = [(i, i + by) for i in range(count) if 0 <= i + by < count]
    return lax.ppermute(x, axis, pairs)


def depthwise(padded, kernel, bias_term):
    channels = padded.shape[-1]
    conv_out = lax.conv_general_dilated(
        padded.astype(jnp.float32),
        kernel.astype(jnp.float32)[:, :, None, :],
        (1, 1),
        "VALID",
        dimension_numbers=("NHWC", "HWIO", "NHWC"),
        feature_group_count=channels,
        precision=lax.Precision.HIGHEST,
    )
    return conv_out + bias_term.astype(jnp.float32)


def conv_block(padded, fresh, fresh_index, params, hand_on):
    (
        depth_kernel,
        depth_bias,
        norm_gain,
        norm_bias,
        proj_in,
        bias_in,
        grn_gamma,
        grn_beta,
        proj_out,
        bias_out,
    ) = params
    num_items, padded_rows, num_cols, channels = padded.shape
    results = pointwise(
        padded.reshape(-1, channels),
        fresh.reshape(fresh.shape[0], -1, channels),
        fresh_index,
        proj_in,
        proj_out,
        bias_in,
        grn_gamma,
        grn_beta,
        bias_out,
        depth_kernel,
        depth_bias,
        norm_gain,
        norm_bias,
        num_cols,
        hand_on,
    )
    produced = results[0].reshape(num_items, padded_rows - 6, num_cols, channels)
    arriving = results[1].reshape(padded.shape) if hand_on else None
    return produced, arriving


def _gather_kernel(
    n,
    chunks,
    rows,
    mine_ref,
    images_ref,
    held_ref,
    other_ref,
    fresh_ref,
    send_sem,
    recv_sem,
    pass_send,
    pass_recv,
    halo_send,
    halo_recv,
    own_sem,
):
    me = lax.axis_index("dp")
    row = lax.axis_index("row")
    odd = lax.rem(row, 2) == 1
    partner = {"row": row + 1 - 2 * lax.rem(row, 2)}
    outer = jnp.where(odd, row + 1, row - 1)
    has_outer = jnp.logical_and(outer >= 0, outer < rows)
    right = {"dp": lax.rem(me + 1, n)}
    left = {"dp": lax.rem(me + n - 1, n)}
    barrier = pltpu.get_barrier_semaphore()
    for peer in (right, left, partner):
        pl.semaphore_signal(barrier, inc=1, device_id=peer, device_id_type=MESH)

    @pl.when(has_outer)
    def _():
        pl.semaphore_signal(barrier, inc=1, device_id={"row": outer}, device_id_type=MESH)

    pl.semaphore_wait(barrier, 3 + has_outer.astype(jnp.int32))
    cells = images_ref.shape[1]
    edge = 3 * cells // 4
    own = pltpu.make_async_copy(images_ref, fresh_ref.at[:, pl.ds(edge, cells)], own_sem)
    own.start()
    has_above = row > 0
    has_below = row < rows - 1
    halos = (
        (0, pl.ds(0, edge), pl.ds(edge + cells, edge), -1, has_above),
        (1, pl.ds(cells - edge, edge), pl.ds(0, edge), 1, has_below),
    )

    def halo_copy(slot, src, dst, peer_row):
        return pltpu.make_async_remote_copy(
            src_ref=images_ref.at[:, src],
            dst_ref=fresh_ref.at[:, dst],
            send_sem=halo_send.at[slot],
            recv_sem=halo_recv.at[slot],
            device_id={"row": peer_row},
            device_id_type=MESH,
        )

    for slot, src, dst, shift, cond in halos:
        pl.when(cond)(halo_copy(slot, src, dst, row + shift).start)

    @pl.when(jnp.logical_not(has_above))
    def _():
        fresh_ref[:, pl.ds(0, edge), :] = jnp.zeros(
            (fresh_ref.shape[0], edge, fresh_ref.shape[2]), fresh_ref.dtype
        )

    @pl.when(jnp.logical_not(has_below))
    def _():
        fresh_ref[:, pl.ds(edge + cells, edge), :] = jnp.zeros(
            (fresh_ref.shape[0], edge, fresh_ref.shape[2]), fresh_ref.dtype
        )

    sends = []
    parts = len(chunks)

    def send(src, dst, send_sems, recv_sems, slot, c, peer):
        copy = pltpu.make_async_remote_copy(
            src_ref=src.at[chunks[c]],
            dst_ref=dst.at[slot, chunks[c]],
            send_sem=send_sems.at[len(sends)],
            recv_sem=recv_sems.at[slot * parts + c],
            device_id=peer,
            device_id_type=MESH,
        )
        copy.start()
        sends.append(copy)

    def arrived(dst, recv_sems, slot, c):
        pltpu.make_async_remote_copy(
            src_ref=mine_ref.at[chunks[c]],
            dst_ref=dst.at[slot, chunks[c]],
            send_sem=send_sem.at[0],
            recv_sem=recv_sems.at[slot * parts + c],
            device_id=right,
            device_id_type=MESH,
        ).wait_recv()

    to_right = n // 2
    to_left = n - 1 - to_right
    for c in range(parts):
        send(mine_ref, held_ref, send_sem, recv_sem, me, c, right)
        send(mine_ref, held_ref, send_sem, recv_sem, me, c, left)
    for c in range(parts):
        send(mine_ref, other_ref, pass_send, pass_recv, me, c, partner)
    held_ref[me] = mine_ref[...]
    for k in range(1, max(to_right, to_left) + 1):
        for c in range(parts):
            for steps, way, peer in ((to_right, -1, right), (to_left, 1, left)):
                if k > steps:
                    continue
                origin = lax.rem(me + n + way * k, n)
                arrived(held_ref, recv_sem, origin, c)
                if k < steps:
                    send(held_ref.at[origin], held_ref, send_sem, recv_sem, origin, c, peer)
                send(held_ref.at[origin], other_ref, pass_send, pass_recv, origin, c, partner)
    for slot in range(n):
        for c in range(parts):
            arrived(other_ref, pass_recv, slot, c)
    for slot, src, dst, shift, cond in halos:
        pl.when(halos[1 - slot][4])(halo_copy(slot, src, dst, row).wait_recv)
    for slot, src, dst, shift, cond in halos:
        pl.when(cond)(halo_copy(slot, src, dst, row + shift).wait_send)
    own.wait()
    for copy in sends:
        copy.wait_send()


def gathered_weights(proj_in, proj_out, images):
    n = lax.axis_size("dp")
    first_core = lax.rem(lax.axis_index("row"), 2) == 0
    mine = jnp.where(first_core, proj_in.T, proj_out)
    part, channels = mine.shape
    vmem = pl.BlockSpec(memory_space=pltpu.VMEM)
    gathered = jax.ShapeDtypeStruct((n, part, channels), mine.dtype)
    micro, cells, _ = images.shape
    fresh = jax.ShapeDtypeStruct((micro, cells * 5 // 2, channels), images.dtype)
    held, other, fresh = pl.pallas_call(
        functools.partial(
            _gather_kernel, n, (pl.ds(0, 96), pl.ds(96, part - 96)), lax.axis_size("row")
        ),
        out_shape=[gathered, gathered, fresh],
        in_specs=[vmem, vmem],
        out_specs=[vmem, vmem, vmem],
        scratch_shapes=[
            pltpu.SemaphoreType.DMA((4 * n,)),
            pltpu.SemaphoreType.DMA((2 * n,)),
            pltpu.SemaphoreType.DMA((4 * n,)),
            pltpu.SemaphoreType.DMA((2 * n,)),
            pltpu.SemaphoreType.DMA((2,)),
            pltpu.SemaphoreType.DMA((2,)),
            pltpu.SemaphoreType.DMA(()),
        ],
        compiler_params=pltpu.CompilerParams(collective_id=7, has_side_effects=True),
    )(mine, images)
    return held.reshape(n * part, channels), other.reshape(n * part, channels), fresh


def on_device(
    inputs,
    depth_kernel,
    depth_bias,
    norm_gain,
    norm_bias,
    proj_in,
    bias_in,
    grn_gamma,
    grn_beta,
    proj_out,
    bias_out,
):
    num_micro, _, num_rows, num_cols, channels = inputs.shape
    proj_in, proj_out, fresh = gathered_weights(
        proj_in[0], proj_out[0], inputs.reshape(num_micro, num_rows * num_cols, channels)
    )
    fresh = fresh.reshape(num_micro, -1, num_cols, channels)
    sections = lax.axis_size("section")
    section_index = lax.axis_index("section")
    num_micro = inputs.shape[0]
    own_params = (
        depth_kernel[0],
        depth_bias[0],
        norm_gain[0],
        norm_bias[0],
        proj_in,
        bias_in[0],
        grn_gamma[0],
        grn_beta[0],
        proj_out,
        bias_out[0],
    )
    num_ticks = num_micro + sections - 1
    current = fresh[:1]
    outputs = []
    for tick_index in range(num_ticks):
        hand_on = tick_index + 1 < num_ticks
        produced, current = conv_block(
            current, fresh, min(tick_index + 1, num_micro - 1), own_params, hand_on
        )
        outputs.append(produced)
    stacked = jnp.stack(outputs)
    saved = lax.dynamic_slice_in_dim(stacked, section_index, num_micro, axis=0)
    return saved[None]


def solution(mesh):
    return jax.shard_map(
        on_device,
        mesh=mesh,
        in_specs=(
            P(None, "dp", "row", None, None),
            P("section", None, None, None),
            P("section", None),
            P("section", None),
            P("section", None),
            P("section", None, "dp"),
            P("section", None),
            P("section", None),
            P("section", None),
            P("section", "dp", None),
            P("section", None),
        ),
        out_specs=P("section", None, "dp", "row", None, None),
        check_vma=False,
    )
```

```python
import functools
import math

import jax
import jax.numpy as jnp
from jax import lax
from jax.experimental import pallas as pl
from jax.experimental.pallas import tpu as pltpu
from jax.sharding import PartitionSpec as P

MESH = pl.DeviceIdType.MESH

EPS_NORM = 1e-06
EPS_GRN = 1e-06


def extended(cells, sides, width):
    for axis, dim in sides:
        count = lax.axis_size(axis)
        ends = count - 1
        head = lax.slice_in_dim(cells, 0, width, axis=dim)
        tail = lax.slice_in_dim(cells, cells.shape[dim] - width, cells.shape[dim], axis=dim)
        cells = jnp.concatenate(
            [
                lax.ppermute(tail, axis, [(i, (i + 1) % count) for i in range(ends)]),
                cells,
                lax.ppermute(head, axis, [((i + 1) % count, i) for i in range(ends)]),
            ],
            axis=dim,
        )
    return cells


def _pointwise_kernel(
    n,
    sections,
    hand_on,
    fresh_index,
    padded_ref,
    fresh_ref,
    held_ref,
    other_ref,
    bias_in_ref,
    gamma_ref,
    beta_ref,
    bias_out_ref,
    taps_ref,
    depth_bias_ref,
    gain_ref,
    shift_ref,
    out_ref,
    *rest,
):
    if hand_on:
        next_ref, wide_ref, conv_ref, normed_ref, act_ref, slots, send_sem, recv_sem = rest[:8]
        hand_send, hand_recv, fresh_sem = rest[8:]
    else:
        wide_ref, conv_ref, normed_ref, act_ref, slots, send_sem, recv_sem = rest
    me = lax.axis_index("row")
    section = lax.axis_index("section")
    barrier = pltpu.get_barrier_semaphore()
    for k in range(1, n):
        pl.semaphore_signal(
            barrier, inc=1, device_id={"row": lax.rem(me + k, n)}, device_id_type=MESH
        )
    waits = n - 1
    if hand_on:
        cells = out_ref.shape[0]
        edge = 3 * cells // 4
        has_above = me > 0
        has_below = me < n - 1
        has_prev = section > 0
        has_next = section < sections - 1
        @pl.when(has_prev)
        def _():
            pl.semaphore_signal(
                barrier, inc=1, device_id={"section": section - 1}, device_id_type=MESH
            )

        waits = waits + has_next.astype(jnp.int32)
    padded_rows, margin_cols, channels = wide_ref.shape
    cols = out_ref.shape[0] // (padded_rows - 6)
    out_rows = padded_rows - 6
    zeros = jnp.zeros((8, channels), jnp.float32)
    for r in range(padded_rows):
        wide_ref[r, pl.ds(0, 8), :] = zeros
        wide_ref[r, pl.ds(8, cols), :] = padded_ref[pl.ds(r * cols, cols), :].astype(jnp.float32)
        wide_ref[r, pl.ds(8 + cols, margin_cols - 8 - cols), :] = zeros[: margin_cols - 8 - cols]

    for start in range(0, channels, 128):
        lanes = pl.ds(start, min(128, channels - start))
        acc = [
            jnp.broadcast_to(
                depth_bias_ref[:, lanes].astype(jnp.float32), (cols, min(128, channels - start))
            )
            for h in range(out_rows)
        ]
        for r in range(padded_rows):
            for j in range(7):
                slab = wide_ref[r, pl.ds(j + 5, cols), lanes]
                for h in range(out_rows):
                    i = r - h
                    if 0 <= i < 7:
                        tap = taps_ref[i, pl.ds(j, 1), lanes].astype(jnp.float32)
                        acc[h] = acc[h] + slab * tap
        for h in range(out_rows):
            conv_ref[h, :, lanes] = acc[h]

    def norm_row(h, carry):
        acc = conv_ref[h]
        mean = jnp.mean(acc, axis=-1, keepdims=True)
        center = acc - mean
        spread = jnp.mean(center * center, axis=-1, keepdims=True)
        normed = (
            center * lax.rsqrt(spread + EPS_NORM) * gain_ref[...].astype(jnp.float32)
            + shift_ref[...].astype(jnp.float32)
        )
        normed_ref[pl.ds(pl.multiple_of(h * cols, 16), cols), :] = normed.astype(normed_ref.dtype)
        return carry

    lax.fori_loop(0, out_rows, norm_row, 0)
    first_core = lax.rem(me, 2) == 0

    def raise_with(proj_in_t_ref):
        raised = lax.dot_general(
            normed_ref[...],
            proj_in_t_ref[...],
            (((1,), (1,)), ((), ())),
            preferred_element_type=jnp.float32,
        ) + bias_in_ref[...].astype(jnp.float32)
        act_ref[...] = (0.5 * raised * (1.0 + lax.erf(raised * (1.0 / math.sqrt(2.0))))).astype(
            jnp.bfloat16
        )

    pl.when(first_core)(lambda: raise_with(held_ref))
    pl.when(jnp.logical_not(first_core))(lambda: raise_with(other_ref))
    grouped = act_ref[...].astype(jnp.float32)
    slots[me] = jnp.sum(grouped * grouped, axis=0, keepdims=True)
    pl.semaphore_wait(barrier, waits)
    sends = []
    for k in sorted(range(1, n), key=lambda k: -min(k, n - k)):
        copy = pltpu.make_async_remote_copy(
            src_ref=slots.at[me],
            dst_ref=slots.at[me],
            send_sem=send_sem.at[k],
            recv_sem=recv_sem.at[me],
            device_id={"row": lax.rem(me + k, n)},
            device_id_type=MESH,
        )
        copy.start()
        sends.append(copy)
    if hand_on:
        fresh_copy = pltpu.make_async_copy(fresh_ref.at[fresh_index], next_ref, fresh_sem)
        pl.when(section == 0)(fresh_copy.start)

        @pl.when(jnp.logical_and(has_prev, jnp.logical_not(has_above)))
        def _():
            next_ref[pl.ds(0, edge), :] = jnp.zeros((edge, next_ref.shape[1]), next_ref.dtype)

        @pl.when(jnp.logical_and(has_prev, jnp.logical_not(has_below)))
        def _():
            next_ref[pl.ds(edge + cells, edge), :] = jnp.zeros(
                (edge, next_ref.shape[1]), next_ref.dtype
            )

    for k in range(1, n):
        src = lax.rem(me + k, n)
        pltpu.make_async_remote_copy(
            src_ref=slots.at[src],
            dst_ref=slots.at[src],
            send_sem=send_sem.at[k],
            recv_sem=recv_sem.at[src],
            device_id={"row": src},
            device_id_type=MESH,
        ).wait_recv()
    total_sq = slots[0]
    for j in range(1, n):
        total_sq = total_sq + slots[j]
    magnitude = jnp.sqrt(total_sq)
    grn_ratio = magnitude / (jnp.mean(magnitude, axis=-1, keepdims=True) + EPS_GRN)
    grouped = act_ref[...].astype(jnp.float32)
    hidden = (
        gamma_ref[...].astype(jnp.float32) * grouped * grn_ratio
        + beta_ref[...].astype(jnp.float32)
        + grouped
    ).astype(jnp.bfloat16)
    cells = out_ref.shape[0]
    edge = 3 * cells // 4

    def lower_with(proj_out_ref):
        update = jnp.dot(
            hidden, proj_out_ref[...], preferred_element_type=jnp.float32
        ) + bias_out_ref[...].astype(jnp.float32)
        current = padded_ref[pl.ds(edge, cells), :].astype(jnp.float32)
        out_ref[...] = (current + update).astype(out_ref.dtype)

    pl.when(first_core)(lambda: lower_with(other_ref))
    pl.when(jnp.logical_not(first_core))(lambda: lower_with(held_ref))
    if not hand_on:
        for copy in sends:
            copy.wait_send()
        return
    own_rows = pl.ds(edge, cells)
    handed = pltpu.make_async_remote_copy(
        src_ref=out_ref,
        dst_ref=next_ref.at[own_rows],
        send_sem=hand_send.at[1],
        recv_sem=hand_recv.at[1],
        device_id={"section": section + 1},
        device_id_type=MESH,
    )

    @pl.when(has_next)
    def _():
        handed.start()

    halos = (
        (2, pl.ds(edge, edge), pl.ds(edge + cells, edge), -1, has_above),
        (0, pl.ds(cells, edge), pl.ds(0, edge), 1, has_below),
    )

    def halo_copy(slot, src, dst, peer_row):
        return pltpu.make_async_remote_copy(
            src_ref=next_ref.at[src],
            dst_ref=next_ref.at[dst],
            send_sem=hand_send.at[slot],
            recv_sem=hand_recv.at[slot],
            device_id={"row": peer_row},
            device_id_type=MESH,
        )

    @pl.when(has_prev)
    def _():
        handed.wait_recv()
        for slot, src, dst, shift, cond in halos:
            @pl.when(cond)
            def _():
                halo_copy(slot, src, dst, me + shift).start()

        for slot, src, dst, shift, cond in halos:
            @pl.when(halos[slot // 2][4])
            def _():
                halo_copy(slot, src, dst, me).wait_recv()

        for slot, src, dst, shift, cond in halos:
            @pl.when(cond)
            def _():
                halo_copy(slot, src, dst, me + shift).wait_send()

    @pl.when(has_next)
    def _():
        handed.wait_send()

    pl.when(section == 0)(fresh_copy.wait)
    for copy in sends:
        copy.wait_send()


def pointwise(
    padded,
    fresh,
    fresh_index,
    held,
    other,
    bias_in,
    grn_gamma,
    grn_beta,
    bias_out,
    depth_kernel,
    depth_bias,
    norm_gain,
    norm_bias,
    cols,
    hand_on,
):
    n = lax.axis_size("row")
    sections = lax.axis_size("section")
    channels = padded.shape[1]
    padded_rows = fresh.shape[1] // cols
    cells = (padded_rows - 6) * cols
    hidden_units = held.shape[0]
    vmem = pl.BlockSpec(memory_space=pltpu.VMEM)
    out_shape = [jax.ShapeDtypeStruct((cells, channels), padded.dtype)]
    scratch = [
        pltpu.VMEM((padded_rows, -(-(cols + 11) // 8) * 8, channels), jnp.float32),
        pltpu.VMEM((padded_rows - 6, cols, channels), jnp.float32),
        pltpu.VMEM((cells, channels), jnp.bfloat16),
        pltpu.VMEM((cells, hidden_units), jnp.bfloat16),
        pltpu.VMEM((n, 1, hidden_units), jnp.float32),
        pltpu.SemaphoreType.DMA((n,)),
        pltpu.SemaphoreType.DMA((n,)),
    ]
    if hand_on:
        out_shape.append(jax.ShapeDtypeStruct(fresh.shape[1:], fresh.dtype))
        scratch += [
            pltpu.SemaphoreType.DMA((3,)),
            pltpu.SemaphoreType.DMA((3,)),
            pltpu.SemaphoreType.DMA(()),
        ]
    return pl.pallas_call(
        functools.partial(_pointwise_kernel, n, sections, hand_on, fresh_index),
        out_shape=out_shape,
        in_specs=[vmem, pl.BlockSpec(memory_space=pl.ANY)] + [vmem] * 10,
        out_specs=[vmem] * len(out_shape),
        scratch_shapes=scratch,
        compiler_params=pltpu.CompilerParams(
            collective_id=1 + fresh_index if hand_on else 0, has_side_effects=True
        ),
        cost_estimate=pl.CostEstimate(
            flops=4 * cells * channels * hidden_units,
            transcendentals=cells * hidden_units,
            bytes_accessed=4 * channels * hidden_units + 8 * cells * channels,
        ),
    )(
        padded,
        fresh,
        held,
        other,
        bias_in.reshape(1, -1),
        grn_gamma.reshape(1, -1),
        grn_beta.reshape(1, -1),
        bias_out.reshape(1, -1),
        depth_kernel,
        depth_bias.reshape(1, -1),
        norm_gain.reshape(1, -1),
        norm_bias.reshape(1, -1),
    )


def passed_along(x, axis, by):
    count = lax.axis_size(axis)
    pairs = [(i, i + by) for i in range(count) if 0 <= i + by < count]
    return lax.ppermute(x, axis, pairs)


def depthwise(padded, kernel, bias_term):
    channels = padded.shape[-1]
    conv_out = lax.conv_general_dilated(
        padded.astype(jnp.float32),
        kernel.astype(jnp.float32)[:, :, None, :],
        (1, 1),
        "VALID",
        dimension_numbers=("NHWC", "HWIO", "NHWC"),
        feature_group_count=channels,
        precision=lax.Precision.HIGHEST,
    )
    return conv_out + bias_term.astype(jnp.float32)


def conv_block(padded, fresh, fresh_index, params, hand_on):
    (
        depth_kernel,
        depth_bias,
        norm_gain,
        norm_bias,
        proj_in,
        bias_in,
        grn_gamma,
        grn_beta,
        proj_out,
        bias_out,
    ) = params
    num_items, padded_rows, num_cols, channels = padded.shape
    results = pointwise(
        padded.reshape(-1, channels),
        fresh.reshape(fresh.shape[0], -1, channels),
        fresh_index,
        proj_in,
        proj_out,
        bias_in,
        grn_gamma,
        grn_beta,
        bias_out,
        depth_kernel,
        depth_bias,
        norm_gain,
        norm_bias,
        num_cols,
        hand_on,
    )
    produced = results[0].reshape(1, -1, num_cols, channels)
    arriving = results[1].reshape(1, -1, num_cols, channels) if hand_on else None
    return produced, arriving


def _gather_kernel(
    n,
    chunks,
    rows,
    mine_ref,
    images_ref,
    held_ref,
    other_ref,
    fresh_ref,
    send_sem,
    recv_sem,
    pass_send,
    pass_recv,
    halo_send,
    halo_recv,
    own_sem,
):
    me = lax.axis_index("dp")
    row = lax.axis_index("row")
    odd = lax.rem(row, 2) == 1
    partner = {"row": row + 1 - 2 * lax.rem(row, 2)}
    outer = jnp.where(odd, row + 1, row - 1)
    has_outer = jnp.logical_and(outer >= 0, outer < rows)
    right = {"dp": lax.rem(me + 1, n)}
    left = {"dp": lax.rem(me + n - 1, n)}
    barrier = pltpu.get_barrier_semaphore()
    for peer in (right, left, partner):
        pl.semaphore_signal(barrier, inc=1, device_id=peer, device_id_type=MESH)

    @pl.when(has_outer)
    def _():
        pl.semaphore_signal(barrier, inc=1, device_id={"row": outer}, device_id_type=MESH)

    pl.semaphore_wait(barrier, 3 + has_outer.astype(jnp.int32))
    cells = images_ref.shape[1]
    edge = 3 * cells // 4
    own = pltpu.make_async_copy(images_ref, fresh_ref.at[:, pl.ds(edge, cells)], own_sem)
    own.start()
    has_above = row > 0
    has_below = row < rows - 1
    halos = (
        (0, pl.ds(0, edge), pl.ds(edge + cells, edge), -1, has_above),
        (1, pl.ds(cells - edge, edge), pl.ds(0, edge), 1, has_below),
    )

    def halo_copy(slot, src, dst, peer_row):
        return pltpu.make_async_remote_copy(
            src_ref=images_ref.at[:, src],
            dst_ref=fresh_ref.at[:, dst],
            send_sem=halo_send.at[slot],
            recv_sem=halo_recv.at[slot],
            device_id={"row": peer_row},
            device_id_type=MESH,
        )

    for slot, src, dst, shift, cond in halos:
        pl.when(cond)(halo_copy(slot, src, dst, row + shift).start)

    @pl.when(jnp.logical_not(has_above))
    def _():
        fresh_ref[:, pl.ds(0, edge), :] = jnp.zeros(
            (fresh_ref.shape[0], edge, fresh_ref.shape[2]), fresh_ref.dtype
        )

    @pl.when(jnp.logical_not(has_below))
    def _():
        fresh_ref[:, pl.ds(edge + cells, edge), :] = jnp.zeros(
            (fresh_ref.shape[0], edge, fresh_ref.shape[2]), fresh_ref.dtype
        )

    sends = []
    parts = len(chunks)

    def send(src, dst, send_sems, recv_sems, slot, c, peer):
        copy = pltpu.make_async_remote_copy(
            src_ref=src.at[chunks[c]],
            dst_ref=dst.at[slot, chunks[c]],
            send_sem=send_sems.at[len(sends)],
            recv_sem=recv_sems.at[slot * parts + c],
            device_id=peer,
            device_id_type=MESH,
        )
        copy.start()
        sends.append(copy)

    def arrived(dst, recv_sems, slot, c):
        pltpu.make_async_remote_copy(
            src_ref=mine_ref.at[chunks[c]],
            dst_ref=dst.at[slot, chunks[c]],
            send_sem=send_sem.at[0],
            recv_sem=recv_sems.at[slot * parts + c],
            device_id=right,
            device_id_type=MESH,
        ).wait_recv()

    to_right = n // 2
    to_left = n - 1 - to_right
    for c in range(parts):
        send(mine_ref, held_ref, send_sem, recv_sem, me, c, right)
        send(mine_ref, held_ref, send_sem, recv_sem, me, c, left)
    for c in range(parts):
        send(mine_ref, other_ref, pass_send, pass_recv, me, c, partner)
    held_ref[me] = mine_ref[...]
    for k in range(1, max(to_right, to_left) + 1):
        for c in range(parts):
            for steps, way, peer in ((to_right, -1, right), (to_left, 1, left)):
                if k > steps:
                    continue
                origin = lax.rem(me + n + way * k, n)
                arrived(held_ref, recv_sem, origin, c)
                if k < steps:
                    send(held_ref.at[origin], held_ref, send_sem, recv_sem, origin, c, peer)
                send(held_ref.at[origin], other_ref, pass_send, pass_recv, origin, c, partner)
    for slot in range(n):
        for c in range(parts):
            arrived(other_ref, pass_recv, slot, c)
    for slot, src, dst, shift, cond in halos:
        pl.when(halos[1 - slot][4])(halo_copy(slot, src, dst, row).wait_recv)
    for slot, src, dst, shift, cond in halos:
        pl.when(cond)(halo_copy(slot, src, dst, row + shift).wait_send)
    own.wait()
    for copy in sends:
        copy.wait_send()


def gathered_weights(proj_in, proj_out, images):
    n = lax.axis_size("dp")
    first_core = lax.rem(lax.axis_index("row"), 2) == 0
    mine = jnp.where(first_core, proj_in.T, proj_out)
    part, channels = mine.shape
    vmem = pl.BlockSpec(memory_space=pltpu.VMEM)
    gathered = jax.ShapeDtypeStruct((n, part, channels), mine.dtype)
    micro, cells, _ = images.shape
    fresh = jax.ShapeDtypeStruct((micro, cells * 5 // 2, channels), images.dtype)
    held, other, fresh = pl.pallas_call(
        functools.partial(
            _gather_kernel, n, (pl.ds(0, 96), pl.ds(96, part - 96)), lax.axis_size("row")
        ),
        out_shape=[gathered, gathered, fresh],
        in_specs=[vmem, vmem],
        out_specs=[vmem, vmem, vmem],
        scratch_shapes=[
            pltpu.SemaphoreType.DMA((4 * n,)),
            pltpu.SemaphoreType.DMA((2 * n,)),
            pltpu.SemaphoreType.DMA((4 * n,)),
            pltpu.SemaphoreType.DMA((2 * n,)),
            pltpu.SemaphoreType.DMA((2,)),
            pltpu.SemaphoreType.DMA((2,)),
            pltpu.SemaphoreType.DMA(()),
        ],
        compiler_params=pltpu.CompilerParams(collective_id=7, has_side_effects=True),
    )(mine, images)
    return held.reshape(n * part, channels), other.reshape(n * part, channels), fresh


def on_device(
    inputs,
    depth_kernel,
    depth_bias,
    norm_gain,
    norm_bias,
    proj_in,
    bias_in,
    grn_gamma,
    grn_beta,
    proj_out,
    bias_out,
):
    num_micro, _, num_rows, num_cols, channels = inputs.shape
    proj_in, proj_out, fresh = gathered_weights(
        proj_in[0], proj_out[0], inputs.reshape(num_micro, num_rows * num_cols, channels)
    )
    fresh = fresh.reshape(num_micro, -1, num_cols, channels)
    sections = lax.axis_size("section")
    section_index = lax.axis_index("section")
    num_micro = inputs.shape[0]
    own_params = (
        depth_kernel[0],
        depth_bias[0],
        norm_gain[0],
        norm_bias[0],
        proj_in,
        bias_in[0],
        grn_gamma[0],
        grn_beta[0],
        proj_out,
        bias_out[0],
    )
    num_ticks = num_micro + sections - 1
    current = fresh
    outputs = []
    for tick_index in range(num_ticks):
        hand_on = tick_index + 1 < num_ticks
        produced, current = conv_block(
            current, fresh, min(tick_index + 1, num_micro - 1), own_params, hand_on
        )
        outputs.append(produced)
    stacked = jnp.stack(outputs)
    saved = lax.dynamic_slice_in_dim(stacked, section_index, num_micro, axis=0)
    return saved[None]


def solution(mesh):
    return jax.shard_map(
        on_device,
        mesh=mesh,
        in_specs=(
            P(None, "dp", "row", None, None),
            P("section", None, None, None),
            P("section", None),
            P("section", None),
            P("section", None),
            P("section", None, "dp"),
            P("section", None),
            P("section", None),
            P("section", None),
            P("section", "dp", None),
            P("section", None),
        ),
        out_specs=P("section", None, "dp", "row", None, None),
        check_vma=False,
    )
```

```python
import functools
import math

import jax
import jax.numpy as jnp
from jax import lax
from jax.experimental import pallas as pl
from jax.experimental.pallas import tpu as pltpu
from jax.sharding import PartitionSpec as P

MESH = pl.DeviceIdType.MESH

EPS_NORM = 1e-06
EPS_GRN = 1e-06


def extended(cells, sides, width):
    for axis, dim in sides:
        count = lax.axis_size(axis)
        ends = count - 1
        head = lax.slice_in_dim(cells, 0, width, axis=dim)
        tail = lax.slice_in_dim(cells, cells.shape[dim] - width, cells.shape[dim], axis=dim)
        cells = jnp.concatenate(
            [
                lax.ppermute(tail, axis, [(i, (i + 1) % count) for i in range(ends)]),
                cells,
                lax.ppermute(head, axis, [((i + 1) % count, i) for i in range(ends)]),
            ],
            axis=dim,
        )
    return cells


def _pointwise_kernel(
    n,
    sections,
    hand_on,
    fresh_index,
    padded_ref,
    fresh_ref,
    held_ref,
    other_ref,
    bias_in_ref,
    gamma_ref,
    beta_ref,
    bias_out_ref,
    taps_ref,
    depth_bias_ref,
    gain_ref,
    shift_ref,
    out_ref,
    *rest,
):
    if hand_on:
        next_ref, wide_ref, conv_ref, normed_ref, act_ref, slots, send_sem, recv_sem = rest[:8]
        hand_send, hand_recv, fresh_sem = rest[8:]
    else:
        wide_ref, conv_ref, normed_ref, act_ref, slots, send_sem, recv_sem = rest
    me = lax.axis_index("row")
    section = lax.axis_index("section")
    barrier = pltpu.get_barrier_semaphore()
    for k in range(1, n):
        pl.semaphore_signal(
            barrier, inc=1, device_id={"row": lax.rem(me + k, n)}, device_id_type=MESH
        )
    waits = n - 1
    if hand_on:
        cells = out_ref.shape[0]
        edge = 3 * cells // 4
        has_above = me > 0
        has_below = me < n - 1
        has_prev = section > 0
        has_next = section < sections - 1
        @pl.when(has_prev)
        def _():
            pl.semaphore_signal(
                barrier, inc=1, device_id={"section": section - 1}, device_id_type=MESH
            )

        waits = waits + has_next.astype(jnp.int32)
    padded_rows, margin_cols, channels = wide_ref.shape
    cols = out_ref.shape[0] // (padded_rows - 6)
    out_rows = padded_rows - 6
    zeros = jnp.zeros((8, channels), jnp.float32)
    for r in range(padded_rows):
        wide_ref[r, pl.ds(0, 8), :] = zeros
        wide_ref[r, pl.ds(8, cols), :] = padded_ref[pl.ds(r * cols, cols), :].astype(jnp.float32)
        wide_ref[r, pl.ds(8 + cols, margin_cols - 8 - cols), :] = zeros[: margin_cols - 8 - cols]

    for start in range(0, channels, 128):
        lanes = pl.ds(start, min(128, channels - start))
        acc = [
            jnp.broadcast_to(
                depth_bias_ref[:, lanes].astype(jnp.float32), (cols, min(128, channels - start))
            )
            for h in range(out_rows)
        ]
        for r in range(padded_rows):
            for j in range(7):
                slab = wide_ref[r, pl.ds(j + 5, cols), lanes]
                for h in range(out_rows):
                    i = r - h
                    if 0 <= i < 7:
                        tap = taps_ref[i, pl.ds(j, 1), lanes].astype(jnp.float32)
                        acc[h] = acc[h] + slab * tap
        for h in range(out_rows):
            conv_ref[h, :, lanes] = acc[h]

    def norm_row(h, carry):
        acc = conv_ref[h]
        mean = jnp.mean(acc, axis=-1, keepdims=True)
        center = acc - mean
        spread = jnp.mean(center * center, axis=-1, keepdims=True)
        normed = (
            center * lax.rsqrt(spread + EPS_NORM) * gain_ref[...].astype(jnp.float32)
            + shift_ref[...].astype(jnp.float32)
        )
        normed_ref[pl.ds(pl.multiple_of(h * cols, 16), cols), :] = normed.astype(normed_ref.dtype)
        return carry

    lax.fori_loop(0, out_rows, norm_row, 0)
    first_core = lax.rem(me, 2) == 0

    def raise_with(proj_in_t_ref):
        raised = lax.dot_general(
            normed_ref[...],
            proj_in_t_ref[...],
            (((1,), (1,)), ((), ())),
            preferred_element_type=jnp.float32,
        ) + bias_in_ref[...].astype(jnp.float32)
        act_ref[...] = (0.5 * raised * (1.0 + lax.erf(raised * (1.0 / math.sqrt(2.0))))).astype(
            jnp.bfloat16
        )

    pl.when(first_core)(lambda: raise_with(held_ref))
    pl.when(jnp.logical_not(first_core))(lambda: raise_with(other_ref))
    grouped = act_ref[...].astype(jnp.float32)
    slots[me] = jnp.sum(grouped * grouped, axis=0, keepdims=True)
    pl.semaphore_wait(barrier, waits)
    sends = []
    for k in sorted(range(1, n), key=lambda k: -min(k, n - k)):
        copy = pltpu.make_async_remote_copy(
            src_ref=slots.at[me],
            dst_ref=slots.at[me],
            send_sem=send_sem.at[k],
            recv_sem=recv_sem.at[me],
            device_id={"row": lax.rem(me + k, n)},
            device_id_type=MESH,
        )
        copy.start()
        sends.append(copy)
    if hand_on:
        fresh_copy = pltpu.make_async_copy(fresh_ref.at[fresh_index], next_ref, fresh_sem)
        pl.when(section == 0)(fresh_copy.start)

        @pl.when(jnp.logical_and(has_prev, jnp.logical_not(has_above)))
        def _():
            next_ref[pl.ds(0, edge), :] = jnp.zeros((edge, next_ref.shape[1]), next_ref.dtype)

        @pl.when(jnp.logical_and(has_prev, jnp.logical_not(has_below)))
        def _():
            next_ref[pl.ds(edge + cells, edge), :] = jnp.zeros(
                (edge, next_ref.shape[1]), next_ref.dtype
            )

    for k in range(1, n):
        src = lax.rem(me + k, n)
        pltpu.make_async_remote_copy(
            src_ref=slots.at[src],
            dst_ref=slots.at[src],
            send_sem=send_sem.at[k],
            recv_sem=recv_sem.at[src],
            device_id={"row": src},
            device_id_type=MESH,
        ).wait_recv()
    total_sq = slots[0]
    for j in range(1, n):
        total_sq = total_sq + slots[j]
    magnitude = jnp.sqrt(total_sq)
    grn_ratio = magnitude / (jnp.mean(magnitude, axis=-1, keepdims=True) + EPS_GRN)
    grouped = act_ref[...].astype(jnp.float32)
    hidden = (
        gamma_ref[...].astype(jnp.float32) * grouped * grn_ratio
        + beta_ref[...].astype(jnp.float32)
        + grouped
    ).astype(jnp.bfloat16)
    cells = out_ref.shape[0]
    edge = 3 * cells // 4

    def lower_with(proj_out_ref):
        update = jnp.dot(
            hidden, proj_out_ref[...], preferred_element_type=jnp.float32
        ) + bias_out_ref[...].astype(jnp.float32)
        current = padded_ref[pl.ds(edge, cells), :].astype(jnp.float32)
        out_ref[...] = (current + update).astype(out_ref.dtype)

    pl.when(first_core)(lambda: lower_with(other_ref))
    pl.when(jnp.logical_not(first_core))(lambda: lower_with(held_ref))
    if not hand_on:
        for copy in sends:
            copy.wait_send()
        return
    own_rows = pl.ds(edge, cells)
    handed = pltpu.make_async_remote_copy(
        src_ref=out_ref,
        dst_ref=next_ref.at[own_rows],
        send_sem=hand_send.at[1],
        recv_sem=hand_recv.at[1],
        device_id={"section": section + 1},
        device_id_type=MESH,
    )

    @pl.when(has_next)
    def _():
        handed.start()

    halos = (
        (2, pl.ds(edge, edge), pl.ds(edge + cells, edge), -1, has_above),
        (0, pl.ds(cells, edge), pl.ds(0, edge), 1, has_below),
    )

    def halo_copy(slot, src, dst, peer_row):
        return pltpu.make_async_remote_copy(
            src_ref=next_ref.at[src],
            dst_ref=next_ref.at[dst],
            send_sem=hand_send.at[slot],
            recv_sem=hand_recv.at[slot],
            device_id={"row": peer_row},
            device_id_type=MESH,
        )

    @pl.when(has_prev)
    def _():
        handed.wait_recv()
        for slot, src, dst, shift, cond in halos:
            @pl.when(cond)
            def _():
                halo_copy(slot, src, dst, me + shift).start()

        for slot, src, dst, shift, cond in halos:
            @pl.when(halos[slot // 2][4])
            def _():
                halo_copy(slot, src, dst, me).wait_recv()

        for slot, src, dst, shift, cond in halos:
            @pl.when(cond)
            def _():
                halo_copy(slot, src, dst, me + shift).wait_send()

    @pl.when(has_next)
    def _():
        handed.wait_send()

    pl.when(section == 0)(fresh_copy.wait)
    for copy in sends:
        copy.wait_send()


def pointwise(
    padded,
    fresh,
    fresh_index,
    held,
    other,
    bias_in,
    grn_gamma,
    grn_beta,
    bias_out,
    depth_kernel,
    depth_bias,
    norm_gain,
    norm_bias,
    cols,
    hand_on,
):
    n = lax.axis_size("row")
    sections = lax.axis_size("section")
    channels = padded.shape[1]
    padded_rows = fresh.shape[1] // cols
    cells = (padded_rows - 6) * cols
    hidden_units = held.shape[0]
    vmem = pl.BlockSpec(memory_space=pltpu.VMEM)
    out_shape = [jax.ShapeDtypeStruct((cells, channels), padded.dtype)]
    scratch = [
        pltpu.VMEM((padded_rows, -(-(cols + 11) // 8) * 8, channels), jnp.float32),
        pltpu.VMEM((padded_rows - 6, cols, channels), jnp.float32),
        pltpu.VMEM((cells, channels), jnp.bfloat16),
        pltpu.VMEM((cells, hidden_units), jnp.bfloat16),
        pltpu.VMEM((n, 1, hidden_units), jnp.float32),
        pltpu.SemaphoreType.DMA((n,)),
        pltpu.SemaphoreType.DMA((n,)),
    ]
    if hand_on:
        out_shape.append(jax.ShapeDtypeStruct(fresh.shape[1:], fresh.dtype))
        scratch += [
            pltpu.SemaphoreType.DMA((3,)),
            pltpu.SemaphoreType.DMA((3,)),
            pltpu.SemaphoreType.DMA(()),
        ]
    return pl.pallas_call(
        functools.partial(_pointwise_kernel, n, sections, hand_on, fresh_index),
        out_shape=out_shape,
        in_specs=[vmem, pl.BlockSpec(memory_space=pl.ANY)] + [vmem] * 10,
        out_specs=[vmem] * len(out_shape),
        scratch_shapes=scratch,
        compiler_params=pltpu.CompilerParams(
            collective_id=1 + fresh_index if hand_on else 0, has_side_effects=True
        ),
        cost_estimate=pl.CostEstimate(
            flops=4 * cells * channels * hidden_units,
            transcendentals=cells * hidden_units,
            bytes_accessed=4 * channels * hidden_units + 8 * cells * channels,
        ),
    )(
        padded,
        fresh,
        held,
        other,
        bias_in.reshape(1, -1),
        grn_gamma.reshape(1, -1),
        grn_beta.reshape(1, -1),
        bias_out.reshape(1, -1),
        depth_kernel,
        depth_bias.reshape(1, -1),
        norm_gain.reshape(1, -1),
        norm_bias.reshape(1, -1),
    )


def passed_along(x, axis, by):
    count = lax.axis_size(axis)
    pairs = [(i, i + by) for i in range(count) if 0 <= i + by < count]
    return lax.ppermute(x, axis, pairs)


def depthwise(padded, kernel, bias_term):
    channels = padded.shape[-1]
    conv_out = lax.conv_general_dilated(
        padded.astype(jnp.float32),
        kernel.astype(jnp.float32)[:, :, None, :],
        (1, 1),
        "VALID",
        dimension_numbers=("NHWC", "HWIO", "NHWC"),
        feature_group_count=channels,
        precision=lax.Precision.HIGHEST,
    )
    return conv_out + bias_term.astype(jnp.float32)


def conv_block(padded, fresh, fresh_index, params, hand_on):
    (
        depth_kernel,
        depth_bias,
        norm_gain,
        norm_bias,
        proj_in,
        bias_in,
        grn_gamma,
        grn_beta,
        proj_out,
        bias_out,
    ) = params
    num_items, padded_rows, num_cols, channels = padded.shape
    results = pointwise(
        padded.reshape(-1, channels),
        fresh.reshape(fresh.shape[0], -1, channels),
        fresh_index,
        proj_in,
        proj_out,
        bias_in,
        grn_gamma,
        grn_beta,
        bias_out,
        depth_kernel,
        depth_bias,
        norm_gain,
        norm_bias,
        num_cols,
        hand_on,
    )
    produced = results[0].reshape(1, -1, num_cols, channels)
    arriving = results[1].reshape(1, -1, num_cols, channels) if hand_on else None
    return produced, arriving


def _gather_kernel(
    n,
    chunks,
    rows,
    proj_in_ref,
    proj_out_ref,
    images_ref,
    held_ref,
    other_ref,
    fresh_ref,
    send_sem,
    recv_sem,
    pass_send,
    pass_recv,
    halo_send,
    halo_recv,
    own_sem,
    mine_ref,
):
    me = lax.axis_index("dp")
    row = lax.axis_index("row")
    odd = lax.rem(row, 2) == 1
    partner = {"row": row + 1 - 2 * lax.rem(row, 2)}
    outer = jnp.where(odd, row + 1, row - 1)
    has_outer = jnp.logical_and(outer >= 0, outer < rows)
    right = {"dp": lax.rem(me + 1, n)}
    left = {"dp": lax.rem(me + n - 1, n)}
    barrier = pltpu.get_barrier_semaphore()
    for peer in (right, left, partner):
        pl.semaphore_signal(barrier, inc=1, device_id=peer, device_id_type=MESH)
    first_core = jnp.logical_not(odd)

    @pl.when(first_core)
    def _():
        mine_ref[...] = proj_in_ref[...].astype(jnp.float32).T.astype(mine_ref.dtype)

    @pl.when(odd)
    def _():
        mine_ref[...] = proj_out_ref[...]

    @pl.when(has_outer)
    def _():
        pl.semaphore_signal(barrier, inc=1, device_id={"row": outer}, device_id_type=MESH)

    pl.semaphore_wait(barrier, 3 + has_outer.astype(jnp.int32))
    cells = images_ref.shape[1]
    edge = 3 * cells // 4
    own = pltpu.make_async_copy(images_ref, fresh_ref.at[:, pl.ds(edge, cells)], own_sem)
    own.start()
    has_above = row > 0
    has_below = row < rows - 1
    halos = (
        (0, pl.ds(0, edge), pl.ds(edge + cells, edge), -1, has_above),
        (1, pl.ds(cells - edge, edge), pl.ds(0, edge), 1, has_below),
    )

    def halo_copy(slot, src, dst, peer_row):
        return pltpu.make_async_remote_copy(
            src_ref=images_ref.at[:, src],
            dst_ref=fresh_ref.at[:, dst],
            send_sem=halo_send.at[slot],
            recv_sem=halo_recv.at[slot],
            device_id={"row": peer_row},
            device_id_type=MESH,
        )

    for slot, src, dst, shift, cond in halos:
        pl.when(cond)(halo_copy(slot, src, dst, row + shift).start)

    @pl.when(jnp.logical_not(has_above))
    def _():
        fresh_ref[:, pl.ds(0, edge), :] = jnp.zeros(
            (fresh_ref.shape[0], edge, fresh_ref.shape[2]), fresh_ref.dtype
        )

    @pl.when(jnp.logical_not(has_below))
    def _():
        fresh_ref[:, pl.ds(edge + cells, edge), :] = jnp.zeros(
            (fresh_ref.shape[0], edge, fresh_ref.shape[2]), fresh_ref.dtype
        )

    sends = []
    parts = len(chunks)

    def send(src, dst, send_sems, recv_sems, slot, c, peer):
        copy = pltpu.make_async_remote_copy(
            src_ref=src.at[chunks[c]],
            dst_ref=dst.at[slot, chunks[c]],
            send_sem=send_sems.at[len(sends)],
            recv_sem=recv_sems.at[slot * parts + c],
            device_id=peer,
            device_id_type=MESH,
        )
        copy.start()
        sends.append(copy)

    def arrived(dst, recv_sems, slot, c):
        pltpu.make_async_remote_copy(
            src_ref=mine_ref.at[chunks[c]],
            dst_ref=dst.at[slot, chunks[c]],
            send_sem=send_sem.at[0],
            recv_sem=recv_sems.at[slot * parts + c],
            device_id=right,
            device_id_type=MESH,
        ).wait_recv()

    to_right = n // 2
    to_left = n - 1 - to_right
    for c in range(parts):
        send(mine_ref, held_ref, send_sem, recv_sem, me, c, right)
        send(mine_ref, held_ref, send_sem, recv_sem, me, c, left)
    for c in range(parts):
        send(mine_ref, other_ref, pass_send, pass_recv, me, c, partner)
    held_ref[me] = mine_ref[...]
    for k in range(1, max(to_right, to_left) + 1):
        for c in range(parts):
            for steps, way, peer in ((to_right, -1, right), (to_left, 1, left)):
                if k > steps:
                    continue
                origin = lax.rem(me + n + way * k, n)
                arrived(held_ref, recv_sem, origin, c)
                if k < steps:
                    send(held_ref.at[origin], held_ref, send_sem, recv_sem, origin, c, peer)
                send(held_ref.at[origin], other_ref, pass_send, pass_recv, origin, c, partner)
    for slot in range(n):
        for c in range(parts):
            arrived(other_ref, pass_recv, slot, c)
    for slot, src, dst, shift, cond in halos:
        pl.when(halos[1 - slot][4])(halo_copy(slot, src, dst, row).wait_recv)
    for slot, src, dst, shift, cond in halos:
        pl.when(cond)(halo_copy(slot, src, dst, row + shift).wait_send)
    own.wait()
    for copy in sends:
        copy.wait_send()


def gathered_weights(proj_in, proj_out, images):
    n = lax.axis_size("dp")
    part, channels = proj_out.shape
    vmem = pl.BlockSpec(memory_space=pltpu.VMEM)
    gathered = jax.ShapeDtypeStruct((n, part, channels), proj_out.dtype)
    micro, cells, _ = images.shape
    fresh = jax.ShapeDtypeStruct((micro, cells * 5 // 2, channels), images.dtype)
    held, other, fresh = pl.pallas_call(
        functools.partial(
            _gather_kernel, n, (pl.ds(0, 96), pl.ds(96, part - 96)), lax.axis_size("row")
        ),
        out_shape=[gathered, gathered, fresh],
        in_specs=[vmem, vmem, vmem],
        out_specs=[vmem, vmem, vmem],
        scratch_shapes=[
            pltpu.SemaphoreType.DMA((4 * n,)),
            pltpu.SemaphoreType.DMA((2 * n,)),
            pltpu.SemaphoreType.DMA((4 * n,)),
            pltpu.SemaphoreType.DMA((2 * n,)),
            pltpu.SemaphoreType.DMA((2,)),
            pltpu.SemaphoreType.DMA((2,)),
            pltpu.SemaphoreType.DMA(()),
            pltpu.VMEM((part, channels), proj_out.dtype),
        ],
        compiler_params=pltpu.CompilerParams(collective_id=7, has_side_effects=True),
    )(proj_in, proj_out, images)
    return held.reshape(n * part, channels), other.reshape(n * part, channels), fresh


def on_device(
    inputs,
    depth_kernel,
    depth_bias,
    norm_gain,
    norm_bias,
    proj_in,
    bias_in,
    grn_gamma,
    grn_beta,
    proj_out,
    bias_out,
):
    num_micro, _, num_rows, num_cols, channels = inputs.shape
    proj_in, proj_out, fresh = gathered_weights(
        proj_in[0], proj_out[0], inputs.reshape(num_micro, num_rows * num_cols, channels)
    )
    fresh = fresh.reshape(num_micro, -1, num_cols, channels)
    sections = lax.axis_size("section")
    section_index = lax.axis_index("section")
    num_micro = inputs.shape[0]
    own_params = (
        depth_kernel[0],
        depth_bias[0],
        norm_gain[0],
        norm_bias[0],
        proj_in,
        bias_in[0],
        grn_gamma[0],
        grn_beta[0],
        proj_out,
        bias_out[0],
    )
    num_ticks = num_micro + sections - 1
    current = fresh
    outputs = []
    for tick_index in range(num_ticks):
        hand_on = tick_index + 1 < num_ticks
        produced, current = conv_block(
            current, fresh, min(tick_index + 1, num_micro - 1), own_params, hand_on
        )
        outputs.append(produced)
    stacked = jnp.stack(outputs)
    saved = lax.dynamic_slice_in_dim(stacked, section_index, num_micro, axis=0)
    return saved[None]


def solution(mesh):
    return jax.shard_map(
        on_device,
        mesh=mesh,
        in_specs=(
            P(None, "dp", "row", None, None),
            P("section", None, None, None),
            P("section", None),
            P("section", None),
            P("section", None),
            P("section", None, "dp"),
            P("section", None),
            P("section", None),
            P("section", None),
            P("section", "dp", None),
            P("section", None),
        ),
        out_specs=P("section", None, "dp", "row", None, None),
        check_vma=False,
    )
```

```python
import functools
import math

import jax
import jax.numpy as jnp
from jax import lax
from jax.experimental import pallas as pl
from jax.experimental.pallas import tpu as pltpu
from jax.sharding import PartitionSpec as P

MESH = pl.DeviceIdType.MESH

EPS_NORM = 1e-06
EPS_GRN = 1e-06


def extended(cells, sides, width):
    for axis, dim in sides:
        count = lax.axis_size(axis)
        ends = count - 1
        head = lax.slice_in_dim(cells, 0, width, axis=dim)
        tail = lax.slice_in_dim(cells, cells.shape[dim] - width, cells.shape[dim], axis=dim)
        cells = jnp.concatenate(
            [
                lax.ppermute(tail, axis, [(i, (i + 1) % count) for i in range(ends)]),
                cells,
                lax.ppermute(head, axis, [((i + 1) % count, i) for i in range(ends)]),
            ],
            axis=dim,
        )
    return cells


def _pointwise_kernel(
    n,
    sections,
    hand_on,
    fresh_index,
    padded_ref,
    fresh_ref,
    held_ref,
    other_ref,
    bias_in_ref,
    gamma_ref,
    beta_ref,
    bias_out_ref,
    taps_ref,
    depth_bias_ref,
    gain_ref,
    shift_ref,
    out_ref,
    *rest,
):
    if hand_on:
        next_ref, wide_ref, conv_ref, normed_ref, act_ref, slots, send_sem, recv_sem = rest[:8]
        hand_send, hand_recv, fresh_sem = rest[8:]
    else:
        wide_ref, conv_ref, normed_ref, act_ref, slots, send_sem, recv_sem = rest
    me = lax.axis_index("row")
    section = lax.axis_index("section")
    barrier = pltpu.get_barrier_semaphore()
    for k in range(1, n):
        pl.semaphore_signal(
            barrier, inc=1, device_id={"row": lax.rem(me + k, n)}, device_id_type=MESH
        )
    waits = n - 1
    if hand_on:
        cells = out_ref.shape[0]
        edge = 3 * cells // 4
        has_above = me > 0
        has_below = me < n - 1
        has_prev = section > 0
        has_next = section < sections - 1
        @pl.when(has_prev)
        def _():
            pl.semaphore_signal(
                barrier, inc=1, device_id={"section": section - 1}, device_id_type=MESH
            )

        waits = waits + has_next.astype(jnp.int32)
    padded_rows, margin_cols, channels = wide_ref.shape
    cols = out_ref.shape[0] // (padded_rows - 6)
    out_rows = padded_rows - 6
    zeros = jnp.zeros((8, channels), jnp.float32)
    for r in range(padded_rows):
        wide_ref[r, pl.ds(0, 8), :] = zeros
        wide_ref[r, pl.ds(8, cols), :] = padded_ref[pl.ds(r * cols, cols), :].astype(jnp.float32)
        wide_ref[r, pl.ds(8 + cols, margin_cols - 8 - cols), :] = zeros[: margin_cols - 8 - cols]

    for start in range(0, channels, 128):
        lanes = pl.ds(start, min(128, channels - start))
        acc = [
            jnp.broadcast_to(
                depth_bias_ref[:, lanes].astype(jnp.float32), (cols, min(128, channels - start))
            )
            for h in range(out_rows)
        ]
        for r in range(padded_rows):
            for j in range(7):
                slab = wide_ref[r, pl.ds(j + 5, cols), lanes]
                for h in range(out_rows):
                    i = r - h
                    if 0 <= i < 7:
                        tap = taps_ref[i, pl.ds(j, 1), lanes].astype(jnp.float32)
                        acc[h] = acc[h] + slab * tap
        for h in range(out_rows):
            conv_ref[h, :, lanes] = acc[h]

    def norm_row(h, carry):
        acc = conv_ref[h]
        mean = jnp.mean(acc, axis=-1, keepdims=True)
        center = acc - mean
        spread = jnp.mean(center * center, axis=-1, keepdims=True)
        normed = (
            center * lax.rsqrt(spread + EPS_NORM) * gain_ref[...].astype(jnp.float32)
            + shift_ref[...].astype(jnp.float32)
        )
        normed_ref[pl.ds(pl.multiple_of(h * cols, 16), cols), :] = normed.astype(normed_ref.dtype)
        return carry

    lax.fori_loop(0, out_rows, norm_row, 0)
    first_core = lax.rem(me, 2) == 0

    def raise_with(proj_in_t_ref):
        raised = lax.dot_general(
            normed_ref[...],
            proj_in_t_ref[...],
            (((1,), (1,)), ((), ())),
            preferred_element_type=jnp.float32,
        ) + bias_in_ref[...].astype(jnp.float32)
        act_ref[...] = (0.5 * raised * (1.0 + lax.erf(raised * (1.0 / math.sqrt(2.0))))).astype(
            jnp.bfloat16
        )

    pl.when(first_core)(lambda: raise_with(held_ref))
    pl.when(jnp.logical_not(first_core))(lambda: raise_with(other_ref))
    grouped = act_ref[...].astype(jnp.float32)
    slots[me] = jnp.sum(grouped * grouped, axis=0, keepdims=True)
    pl.semaphore_wait(barrier, waits)
    sends = []
    for k in sorted(range(1, n), key=lambda k: -min(k, n - k)):
        copy = pltpu.make_async_remote_copy(
            src_ref=slots.at[me],
            dst_ref=slots.at[me],
            send_sem=send_sem.at[k],
            recv_sem=recv_sem.at[me],
            device_id={"row": lax.rem(me + k, n)},
            device_id_type=MESH,
        )
        copy.start()
        sends.append(copy)
    if hand_on:
        fresh_copy = pltpu.make_async_copy(fresh_ref.at[fresh_index], next_ref, fresh_sem)
        pl.when(section == 0)(fresh_copy.start)

        @pl.when(jnp.logical_and(has_prev, jnp.logical_not(has_above)))
        def _():
            next_ref[pl.ds(0, edge), :] = jnp.zeros((edge, next_ref.shape[1]), next_ref.dtype)

        @pl.when(jnp.logical_and(has_prev, jnp.logical_not(has_below)))
        def _():
            next_ref[pl.ds(edge + cells, edge), :] = jnp.zeros(
                (edge, next_ref.shape[1]), next_ref.dtype
            )

    for k in range(1, n):
        src = lax.rem(me + k, n)
        pltpu.make_async_remote_copy(
            src_ref=slots.at[src],
            dst_ref=slots.at[src],
            send_sem=send_sem.at[k],
            recv_sem=recv_sem.at[src],
            device_id={"row": src},
            device_id_type=MESH,
        ).wait_recv()
    total_sq = slots[0]
    for j in range(1, n):
        total_sq = total_sq + slots[j]
    magnitude = jnp.sqrt(total_sq)
    grn_ratio = magnitude / (jnp.mean(magnitude, axis=-1, keepdims=True) + EPS_GRN)
    grouped = act_ref[...].astype(jnp.float32)
    hidden = (
        gamma_ref[...].astype(jnp.float32) * grouped * grn_ratio
        + beta_ref[...].astype(jnp.float32)
        + grouped
    ).astype(jnp.bfloat16)
    cells = out_ref.shape[0]
    edge = 3 * cells // 4

    def lower_with(proj_out_ref):
        update = jnp.dot(
            hidden, proj_out_ref[...], preferred_element_type=jnp.float32
        ) + bias_out_ref[...].astype(jnp.float32)
        current = padded_ref[pl.ds(edge, cells), :].astype(jnp.float32)
        out_ref[...] = (current + update).astype(out_ref.dtype)

    pl.when(first_core)(lambda: lower_with(other_ref))
    pl.when(jnp.logical_not(first_core))(lambda: lower_with(held_ref))
    if not hand_on:
        for copy in sends:
            copy.wait_send()
        return
    own_rows = pl.ds(edge, cells)
    handed = pltpu.make_async_remote_copy(
        src_ref=out_ref,
        dst_ref=next_ref.at[own_rows],
        send_sem=hand_send.at[1],
        recv_sem=hand_recv.at[1],
        device_id={"section": section + 1},
        device_id_type=MESH,
    )

    @pl.when(has_next)
    def _():
        handed.start()

    halos = (
        (2, pl.ds(edge, edge), pl.ds(edge + cells, edge), -1, has_above),
        (0, pl.ds(cells, edge), pl.ds(0, edge), 1, has_below),
    )

    def halo_copy(slot, src, dst, peer_row):
        return pltpu.make_async_remote_copy(
            src_ref=next_ref.at[src],
            dst_ref=next_ref.at[dst],
            send_sem=hand_send.at[slot],
            recv_sem=hand_recv.at[slot],
            device_id={"row": peer_row},
            device_id_type=MESH,
        )

    @pl.when(has_prev)
    def _():
        handed.wait_recv()
        for slot, src, dst, shift, cond in halos:
            @pl.when(cond)
            def _():
                halo_copy(slot, src, dst, me + shift).start()

        for slot, src, dst, shift, cond in halos:
            @pl.when(halos[slot // 2][4])
            def _():
                halo_copy(slot, src, dst, me).wait_recv()

        for slot, src, dst, shift, cond in halos:
            @pl.when(cond)
            def _():
                halo_copy(slot, src, dst, me + shift).wait_send()

    @pl.when(has_next)
    def _():
        handed.wait_send()

    pl.when(section == 0)(fresh_copy.wait)
    for copy in sends:
        copy.wait_send()


def pointwise(
    padded,
    fresh,
    fresh_index,
    held,
    other,
    bias_in,
    grn_gamma,
    grn_beta,
    bias_out,
    depth_kernel,
    depth_bias,
    norm_gain,
    norm_bias,
    cols,
    hand_on,
):
    n = lax.axis_size("row")
    sections = lax.axis_size("section")
    channels = padded.shape[1]
    padded_rows = fresh.shape[1] // cols
    cells = (padded_rows - 6) * cols
    hidden_units = held.shape[0]
    vmem = pl.BlockSpec(memory_space=pltpu.VMEM)
    out_shape = [jax.ShapeDtypeStruct((cells, channels), padded.dtype)]
    scratch = [
        pltpu.VMEM((padded_rows, -(-(cols + 11) // 8) * 8, channels), jnp.float32),
        pltpu.VMEM((padded_rows - 6, cols, channels), jnp.float32),
        pltpu.VMEM((cells, channels), jnp.bfloat16),
        pltpu.VMEM((cells, hidden_units), jnp.bfloat16),
        pltpu.VMEM((n, 1, hidden_units), jnp.float32),
        pltpu.SemaphoreType.DMA((n,)),
        pltpu.SemaphoreType.DMA((n,)),
    ]
    if hand_on:
        out_shape.append(jax.ShapeDtypeStruct(fresh.shape[1:], fresh.dtype))
        scratch += [
            pltpu.SemaphoreType.DMA((3,)),
            pltpu.SemaphoreType.DMA((3,)),
            pltpu.SemaphoreType.DMA(()),
        ]
    return pl.pallas_call(
        functools.partial(_pointwise_kernel, n, sections, hand_on, fresh_index),
        out_shape=out_shape,
        in_specs=[vmem, pl.BlockSpec(memory_space=pl.ANY)] + [vmem] * 10,
        out_specs=[vmem] * len(out_shape),
        scratch_shapes=scratch,
        compiler_params=pltpu.CompilerParams(
            collective_id=1 + fresh_index if hand_on else 0, has_side_effects=True
        ),
        cost_estimate=pl.CostEstimate(
            flops=4 * cells * channels * hidden_units,
            transcendentals=cells * hidden_units,
            bytes_accessed=4 * channels * hidden_units + 8 * cells * channels,
        ),
    )(
        padded,
        fresh,
        held,
        other,
        bias_in.reshape(1, -1),
        grn_gamma.reshape(1, -1),
        grn_beta.reshape(1, -1),
        bias_out.reshape(1, -1),
        depth_kernel,
        depth_bias.reshape(1, -1),
        norm_gain.reshape(1, -1),
        norm_bias.reshape(1, -1),
    )


def passed_along(x, axis, by):
    count = lax.axis_size(axis)
    pairs = [(i, i + by) for i in range(count) if 0 <= i + by < count]
    return lax.ppermute(x, axis, pairs)


def depthwise(padded, kernel, bias_term):
    channels = padded.shape[-1]
    conv_out = lax.conv_general_dilated(
        padded.astype(jnp.float32),
        kernel.astype(jnp.float32)[:, :, None, :],
        (1, 1),
        "VALID",
        dimension_numbers=("NHWC", "HWIO", "NHWC"),
        feature_group_count=channels,
        precision=lax.Precision.HIGHEST,
    )
    return conv_out + bias_term.astype(jnp.float32)


def conv_block(padded, fresh, fresh_index, params, hand_on):
    (
        depth_kernel,
        depth_bias,
        norm_gain,
        norm_bias,
        proj_in,
        bias_in,
        grn_gamma,
        grn_beta,
        proj_out,
        bias_out,
    ) = params
    num_items, padded_rows, num_cols, channels = padded.shape
    results = pointwise(
        padded.reshape(-1, channels),
        fresh.reshape(fresh.shape[0], -1, channels),
        fresh_index,
        proj_in,
        proj_out,
        bias_in,
        grn_gamma,
        grn_beta,
        bias_out,
        depth_kernel,
        depth_bias,
        norm_gain,
        norm_bias,
        num_cols,
        hand_on,
    )
    produced = results[0].reshape(1, -1, num_cols, channels)
    arriving = results[1].reshape(1, -1, num_cols, channels) if hand_on else None
    return produced, arriving


def _gather_kernel(
    n,
    chunks,
    rows,
    proj_in_ref,
    proj_out_ref,
    images_ref,
    held_ref,
    other_ref,
    fresh_ref,
    send_sem,
    recv_sem,
    pass_send,
    pass_recv,
    halo_send,
    halo_recv,
    own_sem,
    mine_ref,
):
    me = lax.axis_index("dp")
    row = lax.axis_index("row")
    odd = lax.rem(row, 2) == 1
    partner = {"row": row + 1 - 2 * lax.rem(row, 2)}
    outer = jnp.where(odd, row + 1, row - 1)
    has_outer = jnp.logical_and(outer >= 0, outer < rows)
    right = {"dp": lax.rem(me + 1, n)}
    left = {"dp": lax.rem(me + n - 1, n)}
    barrier = pltpu.get_barrier_semaphore()
    for peer in (right, left, partner):
        pl.semaphore_signal(barrier, inc=1, device_id=peer, device_id_type=MESH)
    first_core = jnp.logical_not(odd)

    @pl.when(first_core)
    def _():
        mine_ref[...] = proj_in_ref[...].astype(jnp.float32).T.astype(mine_ref.dtype)

    @pl.when(odd)
    def _():
        mine_ref[...] = proj_out_ref[...]

    @pl.when(has_outer)
    def _():
        pl.semaphore_signal(barrier, inc=1, device_id={"row": outer}, device_id_type=MESH)

    pl.semaphore_wait(barrier, 3 + has_outer.astype(jnp.int32))
    cells = images_ref.shape[1]
    edge = 3 * cells // 4
    own = pltpu.make_async_copy(images_ref, fresh_ref.at[:, pl.ds(edge, cells)], own_sem)
    own.start()
    has_above = row > 0
    has_below = row < rows - 1
    halos = (
        (0, pl.ds(0, edge), pl.ds(edge + cells, edge), -1, has_above),
        (1, pl.ds(cells - edge, edge), pl.ds(0, edge), 1, has_below),
    )

    def halo_copy(slot, src, dst, peer_row):
        return pltpu.make_async_remote_copy(
            src_ref=images_ref.at[:, src],
            dst_ref=fresh_ref.at[:, dst],
            send_sem=halo_send.at[slot],
            recv_sem=halo_recv.at[slot],
            device_id={"row": peer_row},
            device_id_type=MESH,
        )

    for slot, src, dst, shift, cond in halos:
        pl.when(cond)(halo_copy(slot, src, dst, row + shift).start)

    @pl.when(jnp.logical_not(has_above))
    def _():
        fresh_ref[:, pl.ds(0, edge), :] = jnp.zeros(
            (fresh_ref.shape[0], edge, fresh_ref.shape[2]), fresh_ref.dtype
        )

    @pl.when(jnp.logical_not(has_below))
    def _():
        fresh_ref[:, pl.ds(edge + cells, edge), :] = jnp.zeros(
            (fresh_ref.shape[0], edge, fresh_ref.shape[2]), fresh_ref.dtype
        )

    sends = []
    parts = len(chunks)

    def send(src, dst, send_sems, recv_sems, slot, c, peer):
        copy = pltpu.make_async_remote_copy(
            src_ref=src.at[chunks[c]],
            dst_ref=dst.at[slot, chunks[c]],
            send_sem=send_sems.at[len(sends)],
            recv_sem=recv_sems.at[slot * parts + c],
            device_id=peer,
            device_id_type=MESH,
        )
        copy.start()
        sends.append(copy)

    def arrived(dst, recv_sems, slot, c):
        pltpu.make_async_remote_copy(
            src_ref=mine_ref.at[chunks[c]],
            dst_ref=dst.at[slot, chunks[c]],
            send_sem=send_sem.at[0],
            recv_sem=recv_sems.at[slot * parts + c],
            device_id=right,
            device_id_type=MESH,
        ).wait_recv()

    to_right = n // 2
    to_left = n - 1 - to_right
    for c in range(parts):
        send(mine_ref, held_ref, send_sem, recv_sem, me, c, right)
        send(mine_ref, held_ref, send_sem, recv_sem, me, c, left)
    for c in range(parts):
        send(mine_ref, other_ref, pass_send, pass_recv, me, c, partner)
    held_ref[me] = mine_ref[...]
    for k in range(1, max(to_right, to_left) + 1):
        for c in range(parts):
            for steps, way, peer in ((to_right, -1, right), (to_left, 1, left)):
                if k > steps:
                    continue
                origin = lax.rem(me + n + way * k, n)
                arrived(held_ref, recv_sem, origin, c)
                if k < steps:
                    send(held_ref.at[origin], held_ref, send_sem, recv_sem, origin, c, peer)
                send(held_ref.at[origin], other_ref, pass_send, pass_recv, origin, c, partner)
    for slot in range(n):
        for c in range(parts):
            arrived(other_ref, pass_recv, slot, c)
    for slot, src, dst, shift, cond in halos:
        pl.when(halos[1 - slot][4])(halo_copy(slot, src, dst, row).wait_recv)
    for slot, src, dst, shift, cond in halos:
        pl.when(cond)(halo_copy(slot, src, dst, row + shift).wait_send)
    own.wait()
    for copy in sends:
        copy.wait_send()


def gathered_weights(proj_in, proj_out, images):
    n = lax.axis_size("dp")
    part, channels = proj_out.shape
    vmem = pl.BlockSpec(memory_space=pltpu.VMEM)
    gathered = jax.ShapeDtypeStruct((n, part, channels), proj_out.dtype)
    micro, cells, _ = images.shape
    fresh = jax.ShapeDtypeStruct((micro, cells * 5 // 2, channels), images.dtype)
    held, other, fresh = pl.pallas_call(
        functools.partial(
            _gather_kernel, n, (pl.ds(0, 64), pl.ds(64, 64), pl.ds(128, part - 128)), lax.axis_size("row")
        ),
        out_shape=[gathered, gathered, fresh],
        in_specs=[vmem, vmem, vmem],
        out_specs=[vmem, vmem, vmem],
        scratch_shapes=[
            pltpu.SemaphoreType.DMA((6 * n,)),
            pltpu.SemaphoreType.DMA((3 * n,)),
            pltpu.SemaphoreType.DMA((6 * n,)),
            pltpu.SemaphoreType.DMA((3 * n,)),
            pltpu.SemaphoreType.DMA((2,)),
            pltpu.SemaphoreType.DMA((2,)),
            pltpu.SemaphoreType.DMA(()),
            pltpu.VMEM((part, channels), proj_out.dtype),
        ],
        compiler_params=pltpu.CompilerParams(collective_id=7, has_side_effects=True),
    )(proj_in, proj_out, images)
    return held.reshape(n * part, channels), other.reshape(n * part, channels), fresh


def on_device(
    inputs,
    depth_kernel,
    depth_bias,
    norm_gain,
    norm_bias,
    proj_in,
    bias_in,
    grn_gamma,
    grn_beta,
    proj_out,
    bias_out,
):
    num_micro, _, num_rows, num_cols, channels = inputs.shape
    proj_in, proj_out, fresh = gathered_weights(
        proj_in[0], proj_out[0], inputs.reshape(num_micro, num_rows * num_cols, channels)
    )
    fresh = fresh.reshape(num_micro, -1, num_cols, channels)
    sections = lax.axis_size("section")
    section_index = lax.axis_index("section")
    num_micro = inputs.shape[0]
    own_params = (
        depth_kernel[0],
        depth_bias[0],
        norm_gain[0],
        norm_bias[0],
        proj_in,
        bias_in[0],
        grn_gamma[0],
        grn_beta[0],
        proj_out,
        bias_out[0],
    )
    num_ticks = num_micro + sections - 1
    current = fresh
    outputs = []
    for tick_index in range(num_ticks):
        hand_on = tick_index + 1 < num_ticks
        produced, current = conv_block(
            current, fresh, min(tick_index + 1, num_micro - 1), own_params, hand_on
        )
        outputs.append(produced)
    stacked = jnp.stack(outputs)
    saved = lax.dynamic_slice_in_dim(stacked, section_index, num_micro, axis=0)
    return saved[None]


def solution(mesh):
    return jax.shard_map(
        on_device,
        mesh=mesh,
        in_specs=(
            P(None, "dp", "row", None, None),
            P("section", None, None, None),
            P("section", None),
            P("section", None),
            P("section", None),
            P("section", None, "dp"),
            P("section", None),
            P("section", None),
            P("section", None),
            P("section", "dp", None),
            P("section", None),
        ),
        out_specs=P("section", None, "dp", "row", None, None),
        check_vma=False,
    )
```

```python
import functools
import math

import jax
import jax.numpy as jnp
from jax import lax
from jax.experimental import pallas as pl
from jax.experimental.pallas import tpu as pltpu
from jax.sharding import PartitionSpec as P

MESH = pl.DeviceIdType.MESH

EPS_NORM = 1e-06
EPS_GRN = 1e-06


def extended(cells, sides, width):
    for axis, dim in sides:
        count = lax.axis_size(axis)
        ends = count - 1
        head = lax.slice_in_dim(cells, 0, width, axis=dim)
        tail = lax.slice_in_dim(cells, cells.shape[dim] - width, cells.shape[dim], axis=dim)
        cells = jnp.concatenate(
            [
                lax.ppermute(tail, axis, [(i, (i + 1) % count) for i in range(ends)]),
                cells,
                lax.ppermute(head, axis, [((i + 1) % count, i) for i in range(ends)]),
            ],
            axis=dim,
        )
    return cells


def _pointwise_kernel(
    n,
    sections,
    hand_on,
    fresh_index,
    padded_ref,
    fresh_ref,
    held_ref,
    other_ref,
    bias_in_ref,
    gamma_ref,
    beta_ref,
    bias_out_ref,
    taps_ref,
    depth_bias_ref,
    gain_ref,
    shift_ref,
    out_ref,
    *rest,
):
    if hand_on:
        next_ref, wide_ref, conv_ref, normed_ref, act_ref, slots, send_sem, recv_sem = rest[:8]
        hand_send, hand_recv, fresh_sem = rest[8:]
    else:
        wide_ref, conv_ref, normed_ref, act_ref, slots, send_sem, recv_sem = rest
    me = lax.axis_index("row")
    section = lax.axis_index("section")
    barrier = pltpu.get_barrier_semaphore()
    for k in range(1, n):
        pl.semaphore_signal(
            barrier, inc=1, device_id={"row": lax.rem(me + k, n)}, device_id_type=MESH
        )
    waits = n - 1
    if hand_on:
        cells = out_ref.shape[0]
        edge = 3 * cells // 4
        has_above = me > 0
        has_below = me < n - 1
        has_prev = section > 0
        has_next = section < sections - 1
        @pl.when(has_prev)
        def _():
            pl.semaphore_signal(
                barrier, inc=1, device_id={"section": section - 1}, device_id_type=MESH
            )

        waits = waits + has_next.astype(jnp.int32)
    padded_rows, margin_cols, channels = wide_ref.shape
    cols = out_ref.shape[0] // (padded_rows - 6)
    out_rows = padded_rows - 6
    zeros = jnp.zeros((8, channels), jnp.float32)
    for r in range(padded_rows):
        wide_ref[r, pl.ds(0, 8), :] = zeros
        wide_ref[r, pl.ds(8, cols), :] = padded_ref[pl.ds(r * cols, cols), :].astype(jnp.float32)
        wide_ref[r, pl.ds(8 + cols, margin_cols - 8 - cols), :] = zeros[: margin_cols - 8 - cols]

    for start in range(0, channels, 128):
        lanes = pl.ds(start, min(128, channels - start))
        acc = [
            jnp.broadcast_to(
                depth_bias_ref[:, lanes].astype(jnp.float32), (cols, min(128, channels - start))
            )
            for h in range(out_rows)
        ]
        for r in range(padded_rows):
            for j in range(7):
                slab = wide_ref[r, pl.ds(j + 5, cols), lanes]
                for h in range(out_rows):
                    i = r - h
                    if 0 <= i < 7:
                        tap = taps_ref[i, pl.ds(j, 1), lanes].astype(jnp.float32)
                        acc[h] = acc[h] + slab * tap
        for h in range(out_rows):
            conv_ref[h, :, lanes] = acc[h]

    def norm_row(h, carry):
        acc = conv_ref[h]
        mean = jnp.mean(acc, axis=-1, keepdims=True)
        center = acc - mean
        spread = jnp.mean(center * center, axis=-1, keepdims=True)
        normed = (
            center * lax.rsqrt(spread + EPS_NORM) * gain_ref[...].astype(jnp.float32)
            + shift_ref[...].astype(jnp.float32)
        )
        normed_ref[pl.ds(pl.multiple_of(h * cols, 16), cols), :] = normed.astype(normed_ref.dtype)
        return carry

    lax.fori_loop(0, out_rows, norm_row, 0)
    first_core = lax.rem(me, 2) == 0

    def raise_with(proj_in_t_ref):
        raised = lax.dot_general(
            normed_ref[...],
            proj_in_t_ref[...],
            (((1,), (1,)), ((), ())),
            preferred_element_type=jnp.float32,
        ) + bias_in_ref[...].astype(jnp.float32)
        act_ref[...] = (0.5 * raised * (1.0 + lax.erf(raised * (1.0 / math.sqrt(2.0))))).astype(
            jnp.bfloat16
        )

    pl.when(first_core)(lambda: raise_with(held_ref))
    pl.when(jnp.logical_not(first_core))(lambda: raise_with(other_ref))
    grouped = act_ref[...].astype(jnp.float32)
    slots[me] = jnp.sum(grouped * grouped, axis=0, keepdims=True)
    pl.semaphore_wait(barrier, waits)
    sends = []
    for k in sorted(range(1, n), key=lambda k: -min(k, n - k)):
        copy = pltpu.make_async_remote_copy(
            src_ref=slots.at[me],
            dst_ref=slots.at[me],
            send_sem=send_sem.at[k],
            recv_sem=recv_sem.at[me],
            device_id={"row": lax.rem(me + k, n)},
            device_id_type=MESH,
        )
        copy.start()
        sends.append(copy)
    if hand_on:
        fresh_copy = pltpu.make_async_copy(fresh_ref.at[fresh_index], next_ref, fresh_sem)
        pl.when(section == 0)(fresh_copy.start)

        @pl.when(jnp.logical_and(has_prev, jnp.logical_not(has_above)))
        def _():
            next_ref[pl.ds(0, edge), :] = jnp.zeros((edge, next_ref.shape[1]), next_ref.dtype)

        @pl.when(jnp.logical_and(has_prev, jnp.logical_not(has_below)))
        def _():
            next_ref[pl.ds(edge + cells, edge), :] = jnp.zeros(
                (edge, next_ref.shape[1]), next_ref.dtype
            )

    for k in range(1, n):
        src = lax.rem(me + k, n)
        pltpu.make_async_remote_copy(
            src_ref=slots.at[src],
            dst_ref=slots.at[src],
            send_sem=send_sem.at[k],
            recv_sem=recv_sem.at[src],
            device_id={"row": src},
            device_id_type=MESH,
        ).wait_recv()
    total_sq = slots[0]
    for j in range(1, n):
        total_sq = total_sq + slots[j]
    magnitude = jnp.sqrt(total_sq)
    grn_ratio = magnitude / (jnp.mean(magnitude, axis=-1, keepdims=True) + EPS_GRN)
    grouped = act_ref[...].astype(jnp.float32)
    hidden = (
        gamma_ref[...].astype(jnp.float32) * grouped * grn_ratio
        + beta_ref[...].astype(jnp.float32)
        + grouped
    ).astype(jnp.bfloat16)
    cells = out_ref.shape[0]
    edge = 3 * cells // 4

    def lower_with(proj_out_ref):
        update = jnp.dot(
            hidden, proj_out_ref[...], preferred_element_type=jnp.float32
        ) + bias_out_ref[...].astype(jnp.float32)
        current = padded_ref[pl.ds(edge, cells), :].astype(jnp.float32)
        out_ref[...] = (current + update).astype(out_ref.dtype)

    pl.when(first_core)(lambda: lower_with(other_ref))
    pl.when(jnp.logical_not(first_core))(lambda: lower_with(held_ref))
    if not hand_on:
        for copy in sends:
            copy.wait_send()
        return
    own_rows = pl.ds(edge, cells)
    handed = pltpu.make_async_remote_copy(
        src_ref=out_ref,
        dst_ref=next_ref.at[own_rows],
        send_sem=hand_send.at[1],
        recv_sem=hand_recv.at[1],
        device_id={"section": section + 1},
        device_id_type=MESH,
    )

    @pl.when(has_next)
    def _():
        handed.start()

    halos = (
        (2, pl.ds(edge, edge), pl.ds(edge + cells, edge), -1, has_above),
        (0, pl.ds(cells, edge), pl.ds(0, edge), 1, has_below),
    )

    def halo_copy(slot, src, dst, peer_row):
        return pltpu.make_async_remote_copy(
            src_ref=next_ref.at[src],
            dst_ref=next_ref.at[dst],
            send_sem=hand_send.at[slot],
            recv_sem=hand_recv.at[slot],
            device_id={"row": peer_row},
            device_id_type=MESH,
        )

    @pl.when(has_prev)
    def _():
        handed.wait_recv()
        for slot, src, dst, shift, cond in halos:
            @pl.when(cond)
            def _():
                halo_copy(slot, src, dst, me + shift).start()

        for slot, src, dst, shift, cond in halos:
            @pl.when(halos[slot // 2][4])
            def _():
                halo_copy(slot, src, dst, me).wait_recv()

        for slot, src, dst, shift, cond in halos:
            @pl.when(cond)
            def _():
                halo_copy(slot, src, dst, me + shift).wait_send()

    @pl.when(has_next)
    def _():
        handed.wait_send()

    pl.when(section == 0)(fresh_copy.wait)
    for copy in sends:
        copy.wait_send()


def pointwise(
    padded,
    fresh,
    fresh_index,
    held,
    other,
    bias_in,
    grn_gamma,
    grn_beta,
    bias_out,
    depth_kernel,
    depth_bias,
    norm_gain,
    norm_bias,
    cols,
    hand_on,
):
    n = lax.axis_size("row")
    sections = lax.axis_size("section")
    channels = padded.shape[1]
    padded_rows = fresh.shape[1] // cols
    cells = (padded_rows - 6) * cols
    hidden_units = held.shape[0]
    vmem = pl.BlockSpec(memory_space=pltpu.VMEM)
    out_shape = [jax.ShapeDtypeStruct((cells, channels), padded.dtype)]
    scratch = [
        pltpu.VMEM((padded_rows, -(-(cols + 11) // 8) * 8, channels), jnp.float32),
        pltpu.VMEM((padded_rows - 6, cols, channels), jnp.float32),
        pltpu.VMEM((cells, channels), jnp.bfloat16),
        pltpu.VMEM((cells, hidden_units), jnp.bfloat16),
        pltpu.VMEM((n, 1, hidden_units), jnp.float32),
        pltpu.SemaphoreType.DMA((n,)),
        pltpu.SemaphoreType.DMA((n,)),
    ]
    if hand_on:
        out_shape.append(jax.ShapeDtypeStruct(fresh.shape[1:], fresh.dtype))
        scratch += [
            pltpu.SemaphoreType.DMA((3,)),
            pltpu.SemaphoreType.DMA((3,)),
            pltpu.SemaphoreType.DMA(()),
        ]
    return pl.pallas_call(
        functools.partial(_pointwise_kernel, n, sections, hand_on, fresh_index),
        out_shape=out_shape,
        in_specs=[vmem, pl.BlockSpec(memory_space=pl.ANY)] + [vmem] * 10,
        out_specs=[vmem] * len(out_shape),
        scratch_shapes=scratch,
        compiler_params=pltpu.CompilerParams(
            collective_id=1 + fresh_index if hand_on else 0, has_side_effects=True
        ),
        cost_estimate=pl.CostEstimate(
            flops=4 * cells * channels * hidden_units,
            transcendentals=cells * hidden_units,
            bytes_accessed=4 * channels * hidden_units + 8 * cells * channels,
        ),
    )(
        padded,
        fresh,
        held,
        other,
        bias_in.reshape(1, -1),
        grn_gamma.reshape(1, -1),
        grn_beta.reshape(1, -1),
        bias_out.reshape(1, -1),
        depth_kernel,
        depth_bias.reshape(1, -1),
        norm_gain.reshape(1, -1),
        norm_bias.reshape(1, -1),
    )


def passed_along(x, axis, by):
    count = lax.axis_size(axis)
    pairs = [(i, i + by) for i in range(count) if 0 <= i + by < count]
    return lax.ppermute(x, axis, pairs)


def depthwise(padded, kernel, bias_term):
    channels = padded.shape[-1]
    conv_out = lax.conv_general_dilated(
        padded.astype(jnp.float32),
        kernel.astype(jnp.float32)[:, :, None, :],
        (1, 1),
        "VALID",
        dimension_numbers=("NHWC", "HWIO", "NHWC"),
        feature_group_count=channels,
        precision=lax.Precision.HIGHEST,
    )
    return conv_out + bias_term.astype(jnp.float32)


def conv_block(padded, fresh, fresh_index, params, hand_on):
    (
        depth_kernel,
        depth_bias,
        norm_gain,
        norm_bias,
        proj_in,
        bias_in,
        grn_gamma,
        grn_beta,
        proj_out,
        bias_out,
    ) = params
    num_items, padded_rows, num_cols, channels = padded.shape
    results = pointwise(
        padded.reshape(-1, channels),
        fresh.reshape(fresh.shape[0], -1, channels),
        fresh_index,
        proj_in,
        proj_out,
        bias_in,
        grn_gamma,
        grn_beta,
        bias_out,
        depth_kernel,
        depth_bias,
        norm_gain,
        norm_bias,
        num_cols,
        hand_on,
    )
    produced = results[0].reshape(1, -1, num_cols, channels)
    arriving = results[1].reshape(1, -1, num_cols, channels) if hand_on else None
    return produced, arriving


def _gather_kernel(
    n,
    chunks,
    rows,
    proj_in_ref,
    proj_out_ref,
    images_ref,
    held_ref,
    other_ref,
    fresh_ref,
    send_sem,
    recv_sem,
    pass_send,
    pass_recv,
    halo_send,
    halo_recv,
    own_sem,
    mine_ref,
):
    me = lax.axis_index("dp")
    row = lax.axis_index("row")
    odd = lax.rem(row, 2) == 1
    partner = {"row": row + 1 - 2 * lax.rem(row, 2)}
    outer = jnp.where(odd, row + 1, row - 1)
    has_outer = jnp.logical_and(outer >= 0, outer < rows)
    right = {"dp": lax.rem(me + 1, n)}
    left = {"dp": lax.rem(me + n - 1, n)}
    barrier = pltpu.get_barrier_semaphore()
    for peer in (right, left, partner):
        pl.semaphore_signal(barrier, inc=1, device_id=peer, device_id_type=MESH)
    first_core = jnp.logical_not(odd)

    @pl.when(first_core)
    def _():
        mine_ref[...] = proj_in_ref[...].astype(jnp.float32).T.astype(mine_ref.dtype)

    @pl.when(odd)
    def _():
        mine_ref[...] = proj_out_ref[...]

    @pl.when(has_outer)
    def _():
        pl.semaphore_signal(barrier, inc=1, device_id={"row": outer}, device_id_type=MESH)

    pl.semaphore_wait(barrier, 3 + has_outer.astype(jnp.int32))
    cells = images_ref.shape[1]
    edge = 3 * cells // 4
    own = pltpu.make_async_copy(images_ref, fresh_ref.at[:, pl.ds(edge, cells)], own_sem)
    own.start()
    has_above = row > 0
    has_below = row < rows - 1
    halos = (
        (0, pl.ds(0, edge), pl.ds(edge + cells, edge), -1, has_above),
        (1, pl.ds(cells - edge, edge), pl.ds(0, edge), 1, has_below),
    )

    def halo_copy(slot, src, dst, peer_row):
        return pltpu.make_async_remote_copy(
            src_ref=images_ref.at[:, src],
            dst_ref=fresh_ref.at[:, dst],
            send_sem=halo_send.at[slot],
            recv_sem=halo_recv.at[slot],
            device_id={"row": peer_row},
            device_id_type=MESH,
        )

    for slot, src, dst, shift, cond in halos:
        pl.when(cond)(halo_copy(slot, src, dst, row + shift).start)

    @pl.when(jnp.logical_not(has_above))
    def _():
        fresh_ref[:, pl.ds(0, edge), :] = jnp.zeros(
            (fresh_ref.shape[0], edge, fresh_ref.shape[2]), fresh_ref.dtype
        )

    @pl.when(jnp.logical_not(has_below))
    def _():
        fresh_ref[:, pl.ds(edge + cells, edge), :] = jnp.zeros(
            (fresh_ref.shape[0], edge, fresh_ref.shape[2]), fresh_ref.dtype
        )

    sends = []
    parts = len(chunks)

    def send(src, dst, send_sems, recv_sems, slot, c, peer):
        copy = pltpu.make_async_remote_copy(
            src_ref=src.at[chunks[c]],
            dst_ref=dst.at[slot, chunks[c]],
            send_sem=send_sems.at[len(sends)],
            recv_sem=recv_sems.at[slot * parts + c],
            device_id=peer,
            device_id_type=MESH,
        )
        copy.start()
        sends.append(copy)

    def arrived(dst, recv_sems, slot, c):
        pltpu.make_async_remote_copy(
            src_ref=mine_ref.at[chunks[c]],
            dst_ref=dst.at[slot, chunks[c]],
            send_sem=send_sem.at[0],
            recv_sem=recv_sems.at[slot * parts + c],
            device_id=right,
            device_id_type=MESH,
        ).wait_recv()

    to_right = n // 2
    to_left = n - 1 - to_right
    for c in range(parts):
        send(mine_ref, held_ref, send_sem, recv_sem, me, c, right)
        send(mine_ref, held_ref, send_sem, recv_sem, me, c, left)
    for c in range(parts):
        send(mine_ref, other_ref, pass_send, pass_recv, me, c, partner)
    held_ref[me] = mine_ref[...]
    for k in range(1, max(to_right, to_left) + 1):
        for c in range(parts):
            for steps, way, peer in ((to_right, -1, right), (to_left, 1, left)):
                if k > steps:
                    continue
                origin = lax.rem(me + n + way * k, n)
                arrived(held_ref, recv_sem, origin, c)
                if k < steps:
                    send(held_ref.at[origin], held_ref, send_sem, recv_sem, origin, c, peer)
                send(held_ref.at[origin], other_ref, pass_send, pass_recv, origin, c, partner)
    for slot in range(n):
        for c in range(parts):
            arrived(other_ref, pass_recv, slot, c)
    for slot, src, dst, shift, cond in halos:
        pl.when(halos[1 - slot][4])(halo_copy(slot, src, dst, row).wait_recv)
    for slot, src, dst, shift, cond in halos:
        pl.when(cond)(halo_copy(slot, src, dst, row + shift).wait_send)
    own.wait()
    for copy in sends:
        copy.wait_send()


def gathered_weights(proj_in, proj_out, images):
    n = lax.axis_size("dp")
    part, channels = proj_out.shape
    vmem = pl.BlockSpec(memory_space=pltpu.VMEM)
    gathered = jax.ShapeDtypeStruct((n, part, channels), proj_out.dtype)
    micro, cells, _ = images.shape
    fresh = jax.ShapeDtypeStruct((micro, cells * 5 // 2, channels), images.dtype)
    held, other, fresh = pl.pallas_call(
        functools.partial(
            _gather_kernel, n, (pl.ds(0, 48), pl.ds(48, 48), pl.ds(96, 48), pl.ds(144, part - 144)), lax.axis_size("row")
        ),
        out_shape=[gathered, gathered, fresh],
        in_specs=[vmem, vmem, vmem],
        out_specs=[vmem, vmem, vmem],
        scratch_shapes=[
            pltpu.SemaphoreType.DMA((8 * n,)),
            pltpu.SemaphoreType.DMA((4 * n,)),
            pltpu.SemaphoreType.DMA((8 * n,)),
            pltpu.SemaphoreType.DMA((4 * n,)),
            pltpu.SemaphoreType.DMA((2,)),
            pltpu.SemaphoreType.DMA((2,)),
            pltpu.SemaphoreType.DMA(()),
            pltpu.VMEM((part, channels), proj_out.dtype),
        ],
        compiler_params=pltpu.CompilerParams(collective_id=7, has_side_effects=True),
    )(proj_in, proj_out, images)
    return held.reshape(n * part, channels), other.reshape(n * part, channels), fresh


def on_device(
    inputs,
    depth_kernel,
    depth_bias,
    norm_gain,
    norm_bias,
    proj_in,
    bias_in,
    grn_gamma,
    grn_beta,
    proj_out,
    bias_out,
):
    num_micro, _, num_rows, num_cols, channels = inputs.shape
    proj_in, proj_out, fresh = gathered_weights(
        proj_in[0], proj_out[0], inputs.reshape(num_micro, num_rows * num_cols, channels)
    )
    fresh = fresh.reshape(num_micro, -1, num_cols, channels)
    sections = lax.axis_size("section")
    section_index = lax.axis_index("section")
    num_micro = inputs.shape[0]
    own_params = (
        depth_kernel[0],
        depth_bias[0],
        norm_gain[0],
        norm_bias[0],
        proj_in,
        bias_in[0],
        grn_gamma[0],
        grn_beta[0],
        proj_out,
        bias_out[0],
    )
    num_ticks = num_micro + sections - 1
    current = fresh
    outputs = []
    for tick_index in range(num_ticks):
        hand_on = tick_index + 1 < num_ticks
        produced, current = conv_block(
            current, fresh, min(tick_index + 1, num_micro - 1), own_params, hand_on
        )
        outputs.append(produced)
    stacked = jnp.stack(outputs)
    saved = lax.dynamic_slice_in_dim(stacked, section_index, num_micro, axis=0)
    return saved[None]


def solution(mesh):
    return jax.shard_map(
        on_device,
        mesh=mesh,
        in_specs=(
            P(None, "dp", "row", None, None),
            P("section", None, None, None),
            P("section", None),
            P("section", None),
            P("section", None),
            P("section", None, "dp"),
            P("section", None),
            P("section", None),
            P("section", None),
            P("section", "dp", None),
            P("section", None),
        ),
        out_specs=P("section", None, "dp", "row", None, None),
        check_vma=False,
    )
```
